32 devices in a mesh: rows: 8 (over z, y), group: 4 (over x, core).
Axes of the slice: x: 2, y: 2, z: 4, core: 2. Of those that a mesh axis runs over, the one named last changes fastest.
Arguments:
- inputs: bfloat16 [32, 2048, 768], P('rows', 'group'), may hold values from -6 to 6
- lengths: int32 [32, 4], P('rows'), may hold values from 1 to 1024, 2048 in all within a row
- params: float32 [6, 768], replicated
- first_moment: float32 [6, 768], replicated, may hold values from -0.0234375 to 0.0234375
- second_moment: float32 [6, 768], replicated, may hold values from 1.08506946e-07 to 8.6805557e-07
- cotangent: bfloat16 [32, 1024, 768], P('rows', 'group')
Outputs:
- output: bfloat16 [32, 1024, 768], P('rows', 'group')
- grad_inputs: bfloat16 [32, 2048, 768], P('rows', 'group')
- grad_norm: float32 [], replicated
- new_params: float32 [6, 768], replicated
- new_first: float32 [6, 768], replicated
- new_second: float32 [6, 768], replicated
The draws below stay inside these ranges and needn't reach their ends.
Inputs may be any that keep to these rules, and one draw needn't show every extreme that they name: Each row's 4 lengths sum to 2048.
All inputs are finite; a program needn't handle non-finite values.
Results may differ from the reference program's by a relative error of at most 0.0005.
Values may be sent and summed in bfloat16 or wider, within the bound.
No kernel may reach another device: no remote copies, remote signals or barrier semaphores. Data moves between devices by JAX's collectives and lax.ppermute only.
A program may use at most 256 MiB of HBM per device.

```python
import math
import jax
import jax.numpy as jnp
import numpy as np
from jax import lax

D = 768
ROW_LEN = 2048
NSEG = 4
STEP = 10
ROWS = 32
HALF = 1024


def draw_params(key, part):
    keys = jax.random.split(jax.random.fold_in(key, 11), 3)
    conv_taps = 0.5 * jax.random.normal(keys[0], (4, D), jnp.float32)
    conv_bias = 0.3 * jax.random.normal(keys[1], (1, D), jnp.float32)
    score_vector = 4.0 / math.sqrt(D) * jax.random.normal(keys[2], (1, D), jnp.float32)
    return jnp.concatenate([conv_taps, conv_bias, score_vector], axis=0)


def draw_cotangent(key, part):
    along_rows = lax.iota(jnp.float32, ROWS) / max(ROWS - 1, 1)
    along_place = lax.iota(jnp.float32, HALF) / max(HALF - 1, 1)
    inner = jax.random.fold_in(key, 23)
    base = jnp.clip(jax.random.normal(inner, (ROWS, HALF, D), jnp.float32), -5.0, 5.0)
    scales = jnp.exp(math.log(3.0) * along_rows)[:, None] * jnp.exp(math.log(3.0) * along_place)[None, :]
    return (base * scales[:, :, None] * 0.5).astype(jnp.bfloat16)


def shard_levels(key, extent, pieces, low, high):
    gain, own = 1.0, jax.random.fold_in(key, 6)
    for dim, blocks in pieces:
        steps = jnp.exp(jax.random.uniform(jax.random.fold_in(own, dim), (blocks,), jnp.float32, low / len(pieces), high / len(pieces)))
        gain = gain * jnp.repeat(steps, extent[dim] // blocks).reshape([-1 if axis == dim else 1 for axis in range(len(extent))])
    return gain


def length_profile(amount, total, most, slope):
    loads = [(1 << 20) // math.isqrt(grade ** slope) + 1 for grade in range(2, amount + 1)]
    rest, given = total - most - (amount - 1), [1] * (amount - 1)
    while rest > 0:
        free = [i for i in range(amount - 1) if given[i] < most]
        pool, budget = sum([loads[i] for i in free]), rest
        for i in free:
            addition = min(most - given[i], max(1, budget * loads[i] // pool), rest)
            given[i] = given[i] + addition
            rest = rest - addition
    return np.array([most] + given)


def uneven(key, number_of, total, most, skew):
    if number_of == 2:
        one = jax.random.randint(key, (), max(1, total - most), min(most, total - 1) + 1)
        return jnp.stack([one, total - one])
    sizes = jnp.asarray(length_profile(number_of, total, most, skew), jnp.int32)
    couples = (number_of - 1) // 2
    giver, taker = sizes[1:1 + 2 * couples:2], sizes[2:2 + 2 * couples:2]
    room = jnp.minimum(giver - 1, most - taker)
    moved = jax.random.randint(jax.random.fold_in(key, 1), (couples,), 0, 1 << 20) % (room + 1)
    sizes = sizes.at[1:1 + 2 * couples:2].set(giver - moved).at[2:2 + 2 * couples:2].set(taker + moved)
    return sizes[jax.random.permutation(jax.random.fold_in(key, 2), number_of)]


def scatter_about(stream_key, extent, spread, bound, shards=(), held_as=jnp.bfloat16):
    drawn = jax.random.normal(stream_key, extent, jnp.float32) * spread
    if len(shards) > 0:
        drawn = shard_levels(stream_key, extent, shards, -0.22, 0.18) * drawn
    return jnp.clip(drawn, min=-bound, max=bound).astype(held_as)


def setup_inputs(seed: int = 0) -> dict:
    streams_of = jax.random.split(jax.random.key(seed), 7)
    return {
        "inputs": scatter_about(streams_of[0], (ROWS, ROW_LEN, D), 1.0, 6.0, ((0, 8), (1, 4))),
        "lengths": jax.vmap(lambda own: uneven(own, NSEG, ROW_LEN, ROW_LEN // 2, 2))(jax.random.split(streams_of[1], ROWS)).reshape((ROWS, NSEG)).astype(jnp.int32),
        "params": draw_params(jax.random.fold_in(streams_of[6], 71), 0),
        "first_moment": scatter_about(streams_of[3], (6, D), (0.11 * (6 * D) ** -0.5), 0.0234375, (), jnp.float32),
        "second_moment": jnp.clip(jnp.exp(jax.random.uniform(streams_of[4], (6, D), jnp.float32, math.log(1.0850694565078811e-07), math.log(8.680555652063049e-07))), 1.0850694565078811e-07, 8.680555652063049e-07),
        "cotangent": draw_cotangent(jax.random.fold_in(streams_of[6], 71), 0),
    }


@jax.custom_vjp
def low(v):
    return lax.optimization_barrier(v.astype(jnp.bfloat16)).astype(jnp.float32)

@jax.custom_vjp
def low_back(v):
    return v

def low_keep(v):
    return (low(v), None)

def low_pass(kept, grad):
    return (grad,)

def back_keep(v):
    return (v, None)

def back_low(kept, grad):
    return (low(grad),)
low.defvjp(low_keep, low_pass)
low_back.defvjp(back_keep, back_low)
beta_one = 0.9
beta_two = 0.999
learn_rate = 0.2
decay_rate = 0.01
adam_eps = 1e-08
clip_limit = 1.0

def offsets(row_lengths, positions):
    seg_ends = jnp.cumsum(row_lengths).astype(jnp.int32)
    seg_starts = (seg_ends - row_lengths).astype(jnp.int32)
    inside = (positions[:, None] >= seg_starts[None, :]) & (positions[:, None] < seg_ends[None, :])
    chosen_start = lax.optimization_barrier(jnp.sum(jnp.where(inside, seg_starts[None, :], 0), axis=1)).astype(jnp.int32)
    chosen_end = lax.optimization_barrier(jnp.sum(jnp.where(inside, seg_ends[None, :], 0), axis=1)).astype(jnp.int32)
    return ((positions - chosen_start).astype(jnp.int32), (chosen_end - positions).astype(jnp.int32))

def mix_window(padded, off_ext, rem_ext, weights):
    span = padded.shape[0] - 9
    conv_rows = span + 6
    off_conv = off_ext[3:3 + conv_rows]
    conv_out = jnp.zeros((conv_rows, padded.shape[1]), padded.dtype) + weights[4]
    for k in range(4):
        keep_mask = (off_conv >= k).astype(padded.dtype)[:, None]
        conv_out = conv_out + keep_mask * weights[k] * padded[3 - k:3 - k + conv_rows]
    off_own = off_ext[6:6 + span]
    rem_own = rem_ext[6:6 + span]
    pooled = []
    for block_size in range(1, 5):
        within = off_own % block_size
        upper = jnp.minimum(block_size - within, rem_own)
        count = jnp.maximum(within + upper, 1)
        running = jnp.zeros((span, padded.shape[1]), padded.dtype)
        for j in range(1 - block_size, block_size):
            keep_mask = ((j >= -within) & (j < upper)).astype(padded.dtype)[:, None]
            running = running + keep_mask * conv_out[3 + j:3 + j + span]
        pooled.append(running / count.astype(padded.dtype)[:, None])
    stacked = jnp.stack(pooled)
    logits = lax.optimization_barrier(jnp.sum(stacked * weights[5], axis=2))
    largest = lax.optimization_barrier(jnp.max(logits, axis=0, keepdims=True))
    shares = jnp.exp(logits - largest)
    shares = shares / lax.optimization_barrier(jnp.sum(shares, axis=0, keepdims=True))
    mixed = lax.optimization_barrier(jnp.sum(shares[:, :, None] * stacked, axis=0))
    return lax.optimization_barrier(jnp.mean(mixed.reshape(span // 2, 2, padded.shape[1]), axis=1))

def adam_update(grads, weights, first_old, second_old):
    first_new = beta_one * first_old + (1.0 - beta_one) * grads
    second_new = beta_two * second_old + (1.0 - beta_two) * grads * grads
    first_hat = first_new / (1.0 - beta_one ** STEP)
    second_hat = second_new / (1.0 - beta_two ** STEP)
    updated = weights - learn_rate * (first_hat / (jnp.sqrt(second_hat) + adam_eps) + decay_rate * weights)
    return (updated, first_new, second_new)

def reference(inputs, lengths, params, first_moment, second_moment, cotangent):

    def forward(values, weights):

        def one_row(row_pair):
            row_values, row_lengths = row_pair
            padded = jnp.concatenate([jnp.zeros((6, row_values.shape[1]), row_values.dtype), row_values, jnp.zeros((3, row_values.shape[1]), row_values.dtype)], axis=0)
            positions = (lax.iota(jnp.int32, row_values.shape[0] + 9) - 6).astype(jnp.int32)
            off_ext, rem_ext = offsets(row_lengths, positions)
            return mix_window(padded, off_ext, rem_ext, weights)
        return lax.map(jax.checkpoint(one_row), (values, lengths))
    values = inputs.astype(jnp.float32)
    output, pullback = jax.vjp(forward, values, params)
    grad_values, grad_params = pullback(cotangent.astype(jnp.float32))
    grad_norm = jnp.sqrt(jnp.sum(grad_params * grad_params))
    clip_scale = jnp.minimum(1.0, clip_limit / (grad_norm + 1e-06))
    new_params, new_first, new_second = adam_update(grad_params * clip_scale, params, first_moment, second_moment)
    return (output.astype(jnp.bfloat16), grad_values.astype(jnp.bfloat16), grad_norm, new_params, new_first, new_second)
```

```python
import functools

import jax
import jax.numpy as jnp
from jax import lax
from jax.experimental import pallas as pl
from jax.experimental.pallas import tpu as pltpu
from jax.sharding import PartitionSpec as P

STEP = 10


beta_one = 0.9
beta_two = 0.999
learn_rate = 0.2
decay_rate = 0.01
adam_eps = 1e-08
clip_limit = 1.0

TAPS = 4
SLOTS = 64
OWN = 56
LEAD = 4
WINDOW = 128
PAD = 16
F32 = jnp.float32
BF16 = jnp.bfloat16


def passed_along(value, axis, steps):
    count = lax.axis_size(axis)
    initial, last = (max(0, -steps), min(count, count - steps))
    return lax.ppermute(value, axis, [(source, source + steps) for source in range(initial, last)])


def rotate_rows(x, amount):
    for bit in (1, 2, 4):
        x = jnp.where((amount & bit) != 0, pltpu.roll(x, 8 - bit, x.ndim - 2), x)
    return x


def split(x):
    high = x.astype(BF16)
    return high, (x - high.astype(F32)).astype(BF16)


def kernel(
    shapes,
    base_ref,
    len_ref,
    x_hbm,
    g_ref,
    up_ref,
    down_ref,
    par_ref,
    out_ref,
    gin_hbm,
    grad_ref,
    xbuf,
    g32,
    gws,
    comp,
    gcs,
    cs,
    es,
    out32,
    ginbuf,
    carry_p,
    carry_o,
    acc,
    sems,
):
    rows, length, half, features, tiles = shapes
    count = rows * tiles
    pairs = count // 2
    chunks = features // 128
    base = base_ref[0]

    def iota(shape, dim):
        return lax.broadcasted_iota(jnp.int32, shape, dim)

    sub8 = iota((8, 128), 0)
    lane8 = iota((8, 128), 1)
    slot8 = lane8 % SLOTS
    first = [2 * slot8 - 3 - (2 * p + lane8 // SLOTS) for p in range(2)]
    group_of = [(f + ((sub8 - f) & 7)) >> 3 for f in first]
    turn = [f & 7 for f in first]
    first_e = 2 * slot8 - 3
    group_of_e = (first_e + ((sub8 - first_e) & 7)) >> 3
    turn_e = first_e & 7

    copy_x = pltpu.make_async_copy(x_hbm, xbuf.at[:, pl.ds(PAD, length), :], sems.at[0])
    copy_x.start()
    subd = iota((8, features), 0)
    for r in range(rows):
        xbuf[r, 0:PAD, :] = up_ref[r]
        xbuf[r, PAD + length : 2 * PAD + length, :] = down_ref[r]
        rest = xbuf.shape[1] - 2 * PAD - length
        if rest > 0:
            xbuf[r, 2 * PAD + length :, :] = jnp.zeros((rest, features), BF16)
        g32[r, PAD : PAD + half, :] = g_ref[r].astype(F32)
        head = pltpu.roll(up_ref[r].astype(F32)[0:8], 6, 0)
        g32[r, 8:16, :] = jnp.where(subd >= 6, head, 0.0)
        tail = pltpu.roll(down_ref[r].astype(F32)[8:16], 3, 0)
        g32[r, PAD + half : PAD + half + 8, :] = jnp.where(subd < 3, tail, 0.0)
        g32[r, PAD + half + 8 :, :] = jnp.zeros((g32.shape[1] - PAD - half - 8, features), F32)
    acc[...] = jnp.zeros_like(acc)
    copy_x.wait()

    def window(r, m):
        return xbuf[r, pl.ds(pl.multiple_of(2 * OWN * m, 16), WINDOW), :]

    def place(tile):
        return tile // tiles, tile % tiles

    def products(pair, _):
        bias_sums = []
        for side in range(2):
            tile = 2 * pair + side
            r, m = place(tile)
            start = pl.multiple_of(OWN * m + 8, 8)
            bias_sum = jnp.zeros((SLOTS, 128), F32)
            for c in range(chunks):
                lanes = slice(128 * c, 128 * c + 128)
                g = g32[r, pl.ds(start, SLOTS), lanes]
                scorer = jnp.broadcast_to(par_ref[5:6, lanes], (8, 128))
                g = jnp.concatenate([jnp.where(sub8 < 2, scorer, g[0:8]), g[8:]], axis=0)
                bias_sum = bias_sum + g * par_ref[4:5, lanes]
                for k in range(TAPS):
                    high, low = split(g * par_ref[k : k + 1, lanes])
                    gws[tile, SLOTS * k : SLOTS * (k + 1), lanes] = high
                    gws[tile, SLOTS * k : SLOTS * (k + 1), features + 128 * c : features + 128 * c + 128] = low
            bias_sums.append(
                jnp.broadcast_to(jnp.sum(bias_sum, axis=1, keepdims=True), (SLOTS, 128))
            )
            x = window(r, m)
            product = lax.dot_general(
                jnp.concatenate([x, x], axis=1),
                gws[tile],
                (((1,), (1,)), ((), ())),
                preferred_element_type=F32,
            )
            for p in range(2):
                banded = jnp.zeros((8, 128), F32)
                scored = jnp.zeros((8, 128), F32)
                for v in range(WINDOW // 8):
                    part = product[8 * v : 8 * v + 8, 128 * p : 128 * p + 128]
                    score = jnp.where(
                        lane8 < SLOTS,
                        jnp.broadcast_to(part[:, 0:1], (8, 128)),
                        jnp.broadcast_to(part[:, SLOTS : SLOTS + 1], (8, 128)),
                    )
                    here = group_of[p] == v
                    banded = jnp.where(here, part, banded)
                    scored = jnp.where(here, score, scored)
                comp[p, tile] = banded
                comp[2 + p, tile] = scored
        gcs[pair] = jnp.concatenate(bias_sums, axis=0).T[0:8]
        return 0

    lax.fori_loop(0, pairs, products, 0)

    left = lane8 < SLOTS
    starts = []
    for r in range(rows):
        first_end = len_ref[r, 0]
        second_end = first_end + len_ref[r, 1]
        third_end = second_end + len_ref[r, 2]
        starts.append((first_end, second_end, third_end, third_end + len_ref[r, 3]))

    def segment(at, r):
        one, two, three, last = starts[r]
        begin = jnp.where(at >= one, one, 0)
        begin = jnp.where(at >= two, two, begin)
        begin = jnp.where(at >= three, three, begin)
        end = jnp.where(at >= one, two, one)
        end = jnp.where(at >= two, three, end)
        end = jnp.where(at >= three, last, end)
        return begin, end

    def tile_start(m):
        return base + 2 * OWN * m - PAD

    bias_score = jnp.sum(par_ref[4:5, :] * par_ref[5:6, :])
    products_of, scores_of, keeps_of = [], [], []
    for tile in range(count):
        r, m = place(tile)
        at = tile_start(m) + 2 * slot8 + sub8 - 3
        offset = at - segment(at, r)[0]
        keeps = [(offset >= 2 * p + lane8 // SLOTS) & (at >= 0) for p in range(2)]
        keeps_of.append(keeps)
        sums = []
        for which in (0, 2):
            total = jnp.zeros((8, 128), F32)
            for p in range(2):
                total = total + jnp.where(keeps[p], rotate_rows(comp[which + p, tile], turn[p]), 0.0)
            sums.append(total + pltpu.roll(total, SLOTS, 1))
        products_of.append(sums[0])
        scores_of.append(sums[1])

    for pair in range(pairs):
        one, two = 2 * pair, 2 * pair + 1
        delta = sub8 - 3
        dots = jnp.where(left, products_of[one], products_of[two]) + gcs[pair]
        scores = jnp.where(left, scores_of[one], scores_of[two]) + bias_score
        coef = jnp.zeros((8, 128), F32)
        coef_e = jnp.zeros((8, 128), F32)
        for p in range(2):
            at = [tile_start(place(t)[1]) + 2 * slot8 + p for t in (one, two)]
            found = [segment(a, place(t)[0]) for a, t in zip(at, (one, two))]
            at = jnp.where(left, at[0], at[1])
            begin = jnp.where(left, found[0][0], found[1][0])
            end = jnp.where(left, found[0][1], found[1][1])
            offset = jnp.maximum(at - begin, 0)
            remain = end - at
            masks, inverses, logits, grads = [], [], [], []
            for b in range(1, TAPS + 1):
                if b == 3:
                    thirds = ((offset.astype(F32) + 0.5) * (1.0 / 3.0)).astype(jnp.int32)
                    within = offset - 3 * thirds
                else:
                    within = offset & (b - 1)
                upper = jnp.minimum(b - within, remain)
                mask = (delta >= p - within) & (delta < p + upper)
                inverse = 1.0 / jnp.maximum(within + upper, 1).astype(F32)
                masks.append(mask)
                inverses.append(inverse)
                logits.append(jnp.sum(jnp.where(mask, scores, 0.0), axis=0, keepdims=True) * inverse)
                grads.append(
                    jnp.sum(jnp.where(mask, dots, 0.0), axis=0, keepdims=True) * (0.5 * inverse)
                )
            largest = functools.reduce(jnp.maximum, logits)
            powers = [jnp.exp(logit - largest) for logit in logits]
            scale = 1.0 / sum(powers)
            shares = [power * scale for power in powers]
            mean = sum(share * grad for share, grad in zip(shares, grads))
            for mask, inverse, share, grad in zip(masks, inverses, shares, grads):
                coef = coef + jnp.where(mask, (0.5 * share) * inverse, 0.0)
                coef_e = coef_e + jnp.where(mask, share * (grad - mean) * inverse, 0.0)
        owned = (slot8 >= LEAD) & (slot8 < LEAD + OWN)
        coef = jnp.where(owned, coef, 0.0)
        coef_e = jnp.where(owned, coef_e, 0.0)
        es[pair] = rotate_rows(coef_e, (8 - turn_e) & 7)
        swapped = pltpu.roll(coef, SLOTS, 1)
        for side, tile in enumerate((one, two)):
            both = jnp.where(left, coef, swapped) if side == 0 else jnp.where(left, swapped, coef)
            for p in range(2):
                kept = jnp.where(keeps_of[tile][p], both, 0.0)
                cs[p, tile] = rotate_rows(kept, (8 - turn[p]) & 7)

    for r in range(rows):
        g32[r, 8:16, :] = jnp.zeros((8, features), F32)
        g32[r, PAD + half : PAD + half + 8, :] = jnp.zeros((8, features), F32)

    rows_e = iota((SLOTS, 128), 0)

    def apply(pair, _):
        spread = jnp.concatenate(
            [jnp.where(group_of_e == v, es[pair], 0.0) for v in range(WINDOW // 8)], axis=0
        ).T
        for side in range(2):
            tile = 2 * pair + side
            r, m = place(tile)
            from_row = OWN * m - 8
            part = spread[SLOTS * side : SLOTS * side + SLOTS]
            here = (from_row + rows_e >= 0) & (from_row + rows_e < half)
            own_e = jnp.sum(jnp.where(here, part, 0.0), axis=0, keepdims=True)
            far_e = jnp.sum(jnp.where(here, 0.0, part), axis=0, keepdims=True)
            at = tile_start(m) + lane8
            one, two, three = [len_ref[r, i] for i in range(3)]
            two = one + two
            three = two + three
            begin = jnp.where(at >= one, one, 0)
            begin = jnp.where(at >= two, two, begin)
            begin = jnp.where(at >= three, three, begin)
            offset = at - begin
            bands = []
            for p in range(2):
                bands.append(
                    jnp.concatenate(
                        [jnp.where(group_of[p] == v, cs[p, tile], 0.0) for v in range(WINDOW // 8)],
                        axis=0,
                    ).T
                )
            band = []
            for k in range(TAPS):
                kept = (offset >= k) & (at >= 0)
                rows_k = jnp.where(
                    sub8 == 0,
                    jnp.broadcast_to(own_e, (8, 128)),
                    jnp.broadcast_to(far_e, (8, 128)),
                )
                rows_k = jnp.where(kept, rows_k, 0.0)
                if k > 0:
                    rows_k = pltpu.roll(rows_k, 128 - k, 1)
                matrix = bands[k // 2][SLOTS * (k % 2) : SLOTS * (k % 2) + SLOTS]
                band.append(jnp.where(sub8 < 2, rows_k, matrix[0:8]))
                band.append(matrix[8:])
            matrix = jnp.concatenate(band, axis=0)
            total = jnp.sum(matrix[0:SLOTS], axis=1, keepdims=True)
            high, low = split(matrix)
            x = window(r, m)
            mixed = lax.dot_general(
                jnp.concatenate([high, low], axis=1),
                jnp.concatenate([x, x], axis=0),
                (((1,), (0,)), ((), ())),
                preferred_element_type=F32,
            )
            start = pl.multiple_of(OWN * m + 8, 8)
            for c in range(chunks):
                lanes = slice(128 * c, 128 * c + 128)
                g = g32[r, pl.ds(start, SLOTS), lanes]
                scorer = jnp.broadcast_to(par_ref[5:6, lanes], (8, 128))
                g = jnp.concatenate(
                    [jnp.where(sub8 == 0, scorer, jnp.where(sub8 < LEAD, 0.0, g[0:8])), g[8:]], axis=0
                )
                value = total * par_ref[4:5, lanes]
                for k in range(TAPS):
                    taken = mixed[SLOTS * k : SLOTS * (k + 1), lanes]
                    value = value + taken * par_ref[k : k + 1, lanes]
                    acc[k, :, lanes] += jnp.sum((taken * g).reshape(SLOTS // 8, 8, 128), axis=0)
                acc[4, :, lanes] += jnp.sum((total * g).reshape(SLOTS // 8, 8, 128), axis=0)
                acc[5, :, lanes] += jnp.where(sub8 == 0, value[0:8], 0.0)
                before = jnp.where(m > 0, carry_o[:, lanes], 0.0)
                out32[r, pl.ds(start, 8), lanes] = before + jnp.where(sub8 < LEAD, 0.0, value[0:8])
                out32[r, pl.ds(start + 8, OWN - 8), lanes] = value[8:OWN]
                carry_o[:, lanes] = value[OWN:]
            back = lax.dot_general(
                jnp.concatenate([high, high, low], axis=0),
                jnp.concatenate(
                    [gws[tile, :, :features], gws[tile, :, features:], gws[tile, :, :features]], axis=0
                ),
                (((0,), (0,)), ((), ())),
                preferred_element_type=F32,
            )
            to_row = pl.multiple_of(2 * OWN * m, 16)
            before = jnp.where(m > 0, carry_p[...], 0.0)
            ginbuf[r, pl.ds(to_row, 16), :] = (before + back[0:16]).astype(BF16)
            ginbuf[r, pl.ds(to_row + 16, 2 * OWN - 16), :] = back[16 : 2 * OWN].astype(BF16)
            carry_p[...] = back[2 * OWN :]
        return 0

    lax.fori_loop(0, pairs, apply, 0)

    copy_out = pltpu.make_async_copy(ginbuf.at[:, pl.ds(PAD, length), :], gin_hbm, sems.at[0])
    copy_out.start()
    for r in range(rows):
        out_ref[r] = out32[r, PAD : PAD + half, :].astype(BF16)
    for k in range(TAPS + 2):
        grad_ref[k : k + 1, :] = jnp.sum(acc[k], axis=0, keepdims=True)
    copy_out.wait()


def fused(base, lengths, inputs, cotangent, up, down, params):
    rows, length, features = inputs.shape
    half = cotangent.shape[1]
    tiles = -(-(half + 3 + LEAD) // OWN)
    count = rows * tiles
    x_rows = 2 * OWN * (tiles - 1) + WINDOW
    g_rows = -(-(OWN * (tiles - 1) + 8 + SLOTS) // 16) * 16
    shapes = (rows, length, half, features, tiles)
    whole = pl.BlockSpec(memory_space=pltpu.VMEM)
    return pl.pallas_call(
        functools.partial(kernel, shapes),
        out_shape=(
            jax.ShapeDtypeStruct((rows, half, features), BF16),
            jax.ShapeDtypeStruct((rows, length, features), BF16),
            jax.ShapeDtypeStruct((TAPS + 2, features), F32),
        ),
        in_specs=[
            pl.BlockSpec(memory_space=pltpu.SMEM),
            pl.BlockSpec(memory_space=pltpu.SMEM),
            pl.BlockSpec(memory_space=pl.ANY),
            whole,
            whole,
            whole,
            whole,
        ],
        out_specs=(whole, pl.BlockSpec(memory_space=pl.ANY), whole),
        scratch_shapes=[
            pltpu.VMEM((rows, x_rows, features), BF16),
            pltpu.VMEM((rows, g_rows, features), F32),
            pltpu.VMEM((count, TAPS * SLOTS, 2 * features), BF16),
            pltpu.VMEM((4, count, 8, 128), F32),
            pltpu.VMEM((count // 2, 8, 128), F32),
            pltpu.VMEM((2, count, 8, 128), F32),
            pltpu.VMEM((count // 2, 8, 128), F32),
            pltpu.VMEM((rows, g_rows, features), F32),
            pltpu.VMEM((rows, x_rows, features), BF16),
            pltpu.VMEM((16, features), F32),
            pltpu.VMEM((8, features), F32),
            pltpu.VMEM((TAPS + 2, 8, features), F32),
            pltpu.SemaphoreType.DMA((2,)),
        ],
        compiler_params=pltpu.CompilerParams(vmem_limit_bytes=60 * 1024 * 1024),
    )(base, lengths, inputs, cotangent, up, down, params)


def adam_update(grads, weights, first_old, second_old):
    first_new = beta_one * first_old + (1.0 - beta_one) * grads
    second_new = beta_two * second_old + (1.0 - beta_two) * grads * grads
    first_hat = first_new / (1.0 - beta_one**STEP)
    second_hat = second_new / (1.0 - beta_two**STEP)
    updated = weights - learn_rate * (
        first_hat / (jnp.sqrt(second_hat) + adam_eps) + decay_rate * weights
    )
    return (updated, first_new, second_new)


def total_over(value, axis):
    count = lax.axis_size(axis)
    if count & (count - 1):
        return lax.psum(value, axis)
    step = 1
    while step < count:
        value = value + lax.ppermute(value, axis, [(i, i ^ step) for i in range(count)])
        step *= 2
    return value


def per_device(inputs, lengths, params, first_moment, second_moment, cotangent):
    length_here = inputs.shape[1]
    half_here = cotangent.shape[1]
    send_up = jnp.concatenate(
        [cotangent[:, half_here - 2 :], inputs[:, length_here - (PAD - 2) :]], axis=1
    )
    send_down = jnp.concatenate([inputs[:, : PAD - 3], cotangent[:, :3]], axis=1)
    up = passed_along(send_up, "group", 1)
    down = passed_along(send_down, "group", -1)
    base = (lax.axis_index("group") * length_here).astype(jnp.int32).reshape(1)
    output, grad_inputs, grad_local = fused(base, lengths, inputs, cotangent, up, down, params)
    grad_params = total_over(total_over(grad_local, "group"), "rows")
    grad_norm = jnp.sqrt(jnp.sum(grad_params * grad_params))
    clip_scale = jnp.minimum(1.0, clip_limit / (grad_norm + 1e-06))
    new_params, new_first, new_second = adam_update(
        grad_params * clip_scale, params, first_moment, second_moment
    )
    return (output, grad_inputs, grad_norm, new_params, new_first, new_second)


def solution(mesh):
    in_specs = (P("rows", "group", None), P("rows", None), P(), P(), P(), P("rows", "group", None))
    out_specs = (P("rows", "group", None), P("rows", "group", None), P(), P(), P(), P())
    return jax.shard_map(
        per_device, mesh=mesh, in_specs=in_specs, out_specs=out_specs, check_vma=False
    )
```

```python
import functools

import jax
import jax.numpy as jnp
from jax import lax
from jax.experimental import pallas as pl
from jax.experimental.pallas import tpu as pltpu
from jax.sharding import PartitionSpec as P

STEP = 10


beta_one = 0.9
beta_two = 0.999
learn_rate = 0.2
decay_rate = 0.01
adam_eps = 1e-08
clip_limit = 1.0

TAPS = 4
SLOTS = 64
OWN = 56
LEAD = 4
WINDOW = 128
PAD = 16
F32 = jnp.float32
BF16 = jnp.bfloat16


def passed_along(value, axis, steps):
    count = lax.axis_size(axis)
    initial, last = (max(0, -steps), min(count, count - steps))
    return lax.ppermute(value, axis, [(source, source + steps) for source in range(initial, last)])


def rotate_rows(x, amount):
    for bit in (1, 2, 4):
        x = jnp.where((amount & bit) != 0, pltpu.roll(x, 8 - bit, x.ndim - 2), x)
    return x


def split(x):
    high = x.astype(BF16)
    return high, (x - high.astype(F32)).astype(BF16)


def iota(shape, dim):
    return lax.broadcasted_iota(jnp.int32, shape, dim)


def ends_of(len_ref, r):
    one = len_ref[r, 0]
    two = one + len_ref[r, 1]
    three = two + len_ref[r, 2]
    return one, two, three, three + len_ref[r, 3]


def begin_of(at, ends):
    begin = jnp.where(at >= ends[0], ends[0], 0)
    begin = jnp.where(at >= ends[1], ends[1], begin)
    return jnp.where(at >= ends[2], ends[2], begin)


def end_of(at, ends):
    end = jnp.where(at >= ends[0], ends[1], ends[0])
    end = jnp.where(at >= ends[1], ends[2], end)
    return jnp.where(at >= ends[2], ends[3], end)


def lanes_of(c):
    return slice(128 * c, 128 * c + 128)


def gather_rows(g_rows, up, down, half):
    sub = iota((8, up.shape[1]), 0)
    head = jnp.where(sub >= 6, pltpu.roll(up[0:8], 6, 0), 0.0)
    tail = jnp.where(sub < 3, pltpu.roll(down[8:16], 3, 0), 0.0)
    return head, tail


def forward_kernel(
    shapes,
    base_ref,
    len_ref,
    x_hbm,
    g_hbm,
    up_ref,
    down_ref,
    par_ref,
    out_hbm,
    mat_hbm,
    grad_ref,
    xb,
    gb,
    xf,
    g32,
    conv_high,
    conv_low,
    comp,
    cs,
    es,
    out32,
    outb,
    mat,
    carry_o,
    acc,
    sems,
):
    rows, length, half, features, tiles = shapes
    count = rows * tiles
    pairs = count // 2
    chunks = features // 128
    base = base_ref[0]
    padded = xb.shape[1]

    copies_x = [
        pltpu.make_async_copy(x_hbm.at[r], xb.at[r, pl.ds(PAD, length), :], sems.at[0, r])
        for r in range(rows)
    ]
    copies_g = [pltpu.make_async_copy(g_hbm.at[r], gb.at[r], sems.at[1, r]) for r in range(rows)]
    for r in range(rows):
        copies_x[r].start()
    for r in range(rows):
        copies_g[r].start()

    sub8 = iota((8, 128), 0)
    lane8 = iota((8, 128), 1)
    slot8 = lane8 % SLOTS
    left = lane8 < SLOTS
    first = [2 * slot8 - 3 - (2 * p + lane8 // SLOTS) for p in range(2)]
    group_of = [(f + ((sub8 - f) & 7)) >> 3 for f in first]
    turn = [f & 7 for f in first]
    first_e = 2 * slot8 - 3
    group_of_e = (first_e + ((sub8 - first_e) & 7)) >> 3
    turn_e = first_e & 7

    def place(tile):
        return tile // tiles, tile % tiles

    def tile_start(m):
        return base + 2 * OWN * m - PAD

    acc[...] = jnp.zeros_like(acc)

    for r in range(rows):
        xb[r, 0:PAD, :] = up_ref[r]
        xb[r, PAD + length : 2 * PAD + length, :] = down_ref[r]
        rest = padded - 2 * PAD - length
        if rest > 0:
            xb[r, 2 * PAD + length :, :] = jnp.zeros((rest, features), BF16)
    for c in range(chunks):
        xf[c, 0:8, :] = jnp.zeros((8, 128), F32)

    def convolve(r, _):
        pltpu.make_async_copy(x_hbm.at[r], xb.at[r, pl.ds(PAD, length), :], sems.at[0, r]).wait()
        ends = ends_of(len_ref, r)

        def widen(i, _):
            at = pl.multiple_of(i * 32, 32)
            for c in range(chunks):
                xf[c, pl.ds(at + 8, 32), :] = xb[r, pl.ds(at, 32), lanes_of(c)].astype(F32)
            return 0

        lax.fori_loop(0, padded // 32, widen, 0)

        def taps(i, _):
            at = pl.multiple_of(i * 16, 16)
            keeps = []
            for j in range(2):
                position = base - PAD + at + 8 * j + sub8
                offset = position - begin_of(position, ends)
                keeps.append([offset >= k for k in range(TAPS)])
            for c in range(chunks):
                parts = []
                for j in range(2):
                    value = par_ref[4:5, lanes_of(c)] + par_ref[0:1, lanes_of(c)] * xf[
                        c, pl.ds(at + 8 * j + 8, 8), :
                    ]
                    for k in range(1, TAPS):
                        shifted = xf[c, pl.ds(at + 8 * j + 8 - k, 8), :]
                        value = value + par_ref[k : k + 1, lanes_of(c)] * jnp.where(
                            keeps[j][k], shifted, 0.0
                        )
                    parts.append(value)
                high, low = split(jnp.concatenate(parts, axis=0))
                conv_high[r, c, pl.ds(at, 16), :] = high
                conv_low[r, c, pl.ds(at, 16), :] = low
            return 0

        lax.fori_loop(0, padded // 16, taps, 0)
        return 0

    lax.fori_loop(0, rows, convolve, 0)

    for r in range(rows):
        copies_g[r].wait()
        up = up_ref[r].astype(F32)
        down = down_ref[r].astype(F32)
        head, tail = gather_rows(None, up, down, half)
        after = g32.shape[2] - PAD - half - 8
        for c in range(chunks):
            g32[r, c, 8:16, :] = head[:, lanes_of(c)]
            g32[r, c, PAD + half : PAD + half + 8, :] = tail[:, lanes_of(c)]
            g32[r, c, PAD + half + 8 :, :] = jnp.zeros((after, 128), F32)

    def widen_g(i, _):
        r = i // (half // 32)
        at = pl.multiple_of((i % (half // 32)) * 32, 32)
        for c in range(chunks):
            g32[r, c, pl.ds(at + PAD, 32), :] = gb[r, pl.ds(at, 32), lanes_of(c)].astype(F32)
        return 0

    lax.fori_loop(0, rows * (half // 32), widen_g, 0)

    scorer_high = [par_ref[5:6, lanes_of(c)].astype(BF16).astype(F32) for c in range(chunks)]
    scorer_low = [par_ref[5:6, lanes_of(c)] - scorer_high[c] for c in range(chunks)]

    def products(pair, _):
        dots, scores = [], []
        for side in range(2):
            r, m = place(2 * pair + side)
            start = pl.multiple_of(OWN * m + 8, 8)
            at = pl.multiple_of(2 * OWN * m, 16)
            streamed, held = [], []
            for c in range(chunks):
                g = g32[r, c, pl.ds(start, SLOTS), :]
                top = jnp.where(sub8 == 0, scorer_high[c], jnp.where(sub8 == 1, scorer_low[c], g[0:8]))
                streamed.append(jnp.concatenate([top, g[8:]], axis=0).astype(BF16))
                held.append(
                    jnp.concatenate(
                        [
                            conv_high[r, c, pl.ds(at, WINDOW), :],
                            conv_low[r, c, pl.ds(at, WINDOW), :],
                        ],
                        axis=0,
                    )
                )
            product = lax.dot_general(
                jnp.concatenate(streamed, axis=1),
                jnp.concatenate(held, axis=1),
                (((1,), (1,)), ((), ())),
                preferred_element_type=F32,
            )
            product = product[:, :WINDOW] + product[:, WINDOW:]
            dots.append(product)
            scores.append(jnp.broadcast_to(product[0:1] + product[1:2], (SLOTS, WINDOW)))
        dots = jnp.concatenate(dots, axis=0).T
        scores = jnp.concatenate(scores, axis=0).T
        banded = jnp.zeros((8, 128), F32)
        scored = jnp.zeros((8, 128), F32)
        for v in range(WINDOW // 8):
            here = group_of_e == v
            banded = jnp.where(here, dots[8 * v : 8 * v + 8], banded)
            scored = jnp.where(here, scores[8 * v : 8 * v + 8], scored)
        comp[0, pair] = banded
        comp[1, pair] = scored
        return 0

    lax.fori_loop(0, pairs, products, 0)

    ends = [ends_of(len_ref, r) for r in range(rows)]
    delta = sub8 - 3
    for pair in range(pairs):
        both = (2 * pair, 2 * pair + 1)
        dots = rotate_rows(comp[0, pair], turn_e)
        scores = rotate_rows(comp[1, pair], turn_e)
        coef = jnp.zeros((8, 128), F32)
        coef_e = jnp.zeros((8, 128), F32)
        for p in range(2):
            at = [tile_start(place(t)[1]) + 2 * slot8 + p for t in both]
            begin = [begin_of(a, ends[place(t)[0]]) for a, t in zip(at, both)]
            end = [end_of(a, ends[place(t)[0]]) for a, t in zip(at, both)]
            offset = jnp.maximum(jnp.where(left, at[0] - begin[0], at[1] - begin[1]), 0)
            remain = jnp.where(left, end[0] - at[0], end[1] - at[1])
            masks, inverses, logits, grads = [], [], [], []
            for b in range(1, TAPS + 1):
                if b == 3:
                    thirds = ((offset.astype(F32) + 0.5) * (1.0 / 3.0)).astype(jnp.int32)
                    within = offset - 3 * thirds
                else:
                    within = offset & (b - 1)
                upper = jnp.minimum(b - within, remain)
                mask = (delta >= p - within) & (delta < p + upper)
                inverse = 1.0 / jnp.maximum(within + upper, 1).astype(F32)
                masks.append(mask)
                inverses.append(inverse)
                logits.append(jnp.sum(jnp.where(mask, scores, 0.0), axis=0, keepdims=True) * inverse)
                grads.append(
                    jnp.sum(jnp.where(mask, dots, 0.0), axis=0, keepdims=True) * (0.5 * inverse)
                )
            largest = functools.reduce(jnp.maximum, logits)
            powers = [jnp.exp(logit - largest) for logit in logits]
            scale = 1.0 / sum(powers)
            shares = [power * scale for power in powers]
            mean = sum(share * grad for share, grad in zip(shares, grads))
            for mask, inverse, share, grad in zip(masks, inverses, shares, grads):
                coef = coef + jnp.where(mask, (0.5 * share) * inverse, 0.0)
                coef_e = coef_e + jnp.where(mask, share * (grad - mean) * inverse, 0.0)
        owned = (slot8 >= LEAD) & (slot8 < LEAD + OWN)
        coef = jnp.where(owned, coef, 0.0)
        coef_e = jnp.where(owned, coef_e, 0.0)
        es[pair] = rotate_rows(coef_e, (8 - turn_e) & 7)
        swapped = pltpu.roll(coef, SLOTS, 1)
        for side, tile in enumerate(both):
            r, m = place(tile)
            at = tile_start(m) + 2 * slot8 + delta
            offset = at - begin_of(at, ends[r])
            alone = jnp.where(left, coef, swapped) if side == 0 else jnp.where(left, swapped, coef)
            for p in range(2):
                kept = jnp.where((offset >= 2 * p + lane8 // SLOTS) & (at >= 0), alone, 0.0)
                cs[p, tile] = rotate_rows(kept, (8 - turn[p]) & 7)

    for r in range(rows):
        for c in range(chunks):
            g32[r, c, 8:16, :] = jnp.zeros((8, 128), F32)
            g32[r, c, PAD + half : PAD + half + 8, :] = jnp.zeros((8, 128), F32)

    rows_e = iota((SLOTS, 128), 0)
    wide = 2 if chunks % 2 == 0 else 1

    def apply(pair, _):
        spread = jnp.concatenate(
            [jnp.where(group_of_e == v, es[pair], 0.0) for v in range(WINDOW // 8)], axis=0
        ).T
        for side in range(2):
            tile = 2 * pair + side
            r, m = place(tile)
            from_row = OWN * m - 8
            part = spread[SLOTS * side : SLOTS * side + SLOTS]
            here = (from_row + rows_e >= 0) & (from_row + rows_e < half)
            own_e = jnp.sum(jnp.where(here, part, 0.0), axis=0, keepdims=True)
            all_e = jnp.sum(part, axis=0, keepdims=True)
            at = tile_start(m) + lane8
            offset = at - begin_of(at, ends_of(len_ref, r))
            bands = []
            for p in range(2):
                bands.append(
                    jnp.concatenate(
                        [jnp.where(group_of[p] == v, cs[p, tile], 0.0) for v in range(WINDOW // 8)],
                        axis=0,
                    ).T
                )
            band = []
            for k in range(TAPS):
                row_k = jnp.where((offset >= k) & (at >= 0), jnp.broadcast_to(own_e, (8, 128)), 0.0)
                if k > 0:
                    row_k = pltpu.roll(row_k, 128 - k, 1)
                matrix = bands[k // 2][SLOTS * (k % 2) : SLOTS * (k % 2) + SLOTS]
                band.append(jnp.where(sub8 == 0, row_k, matrix[0:8]))
                band.append(matrix[8:])
            matrix = jnp.concatenate(band, axis=0)
            total = jnp.sum(matrix[0:SLOTS], axis=1, keepdims=True)
            high, low = split(matrix)
            back = jnp.concatenate(
                [jnp.where(sub8 < 2, jnp.broadcast_to(all_e, (8, 128)), matrix[0:8]), matrix[8:SLOTS]],
                axis=0,
            )
            back_high, back_low = split(back)
            mat[tile, :, 0:WINDOW] = back_high
            mat[tile, :, WINDOW:] = back_low
            factor = jnp.concatenate([high, low], axis=1)
            start = pl.multiple_of(OWN * m + 8, 8)
            window = pl.multiple_of(2 * OWN * m, 16)
            for w in range(chunks // wide):
                x = xb[r, pl.ds(window, WINDOW), 128 * wide * w : 128 * wide * (w + 1)]
                mixed = lax.dot_general(
                    factor,
                    jnp.concatenate([x, x], axis=0),
                    (((1,), (0,)), ((), ())),
                    preferred_element_type=F32,
                )
                for i in range(wide):
                    c = wide * w + i
                    lanes = lanes_of(c)
                    g = g32[r, c, pl.ds(start, SLOTS), :]
                    top = jnp.where(
                        sub8 == 0, par_ref[5:6, lanes], jnp.where(sub8 < LEAD, 0.0, g[0:8])
                    )
                    g = jnp.concatenate([top, g[8:]], axis=0)
                    value = total * par_ref[4:5, lanes]
                    for k in range(TAPS):
                        taken = mixed[SLOTS * k : SLOTS * (k + 1), lanes_of(i)]
                        value = value + taken * par_ref[k : k + 1, lanes]
                        acc[k, :, lanes] += jnp.sum((taken * g).reshape(SLOTS // 8, 8, 128), axis=0)
                    acc[4, :, lanes] += jnp.sum((total * g).reshape(SLOTS // 8, 8, 128), axis=0)
                    acc[5, :, lanes] += jnp.where(sub8 == 0, value[0:8], 0.0)
                    before = jnp.where(m > 0, carry_o[:, lanes], 0.0)
                    out32[c, pl.ds(start, 8), :] = before + jnp.where(sub8 < LEAD, 0.0, value[0:8])
                    out32[c, pl.ds(start + 8, OWN - 8), :] = value[8:OWN]
                    carry_o[:, lanes] = value[OWN:]

            @pl.when(m == tiles - 1)
            def _():
                for c in range(chunks):
                    outb[r, :, lanes_of(c)] = out32[c, PAD : PAD + half, :].astype(BF16)
                pltpu.make_async_copy(outb.at[r], out_hbm.at[r], sems.at[2, r]).start()

        return 0

    lax.fori_loop(0, pairs, apply, 0)

    copy_mat = pltpu.make_async_copy(mat, mat_hbm, sems.at[3, 0])
    copy_mat.start()
    for k in range(TAPS + 2):
        grad_ref[k : k + 1, :] = jnp.sum(acc[k], axis=0, keepdims=True)
    for r in range(rows):
        pltpu.make_async_copy(outb.at[r], out_hbm.at[r], sems.at[2, r]).wait()
    copy_mat.wait()


def backward_kernel(
    shapes,
    r,
    base_ref,
    len_ref,
    g_hbm,
    mat_hbm,
    up_ref,
    down_ref,
    par_ref,
    *refs,
):
    gin_hbm, gb, mat, g32, dc, ginb, sems = refs[-7:]
    rows, length, half, features, tiles = shapes
    chunks = features // 128
    base = base_ref[0]
    copy_g = pltpu.make_async_copy(g_hbm.at[r], gb, sems.at[0])
    copy_g.start()
    copy_mat = pltpu.make_async_copy(mat_hbm.at[pl.ds(r * tiles, tiles)], mat, sems.at[1])
    copy_mat.start()
    sub8 = iota((8, 128), 0)
    ends = ends_of(len_ref, r)
    head, tail = gather_rows(None, up_ref[r].astype(F32), down_ref[r].astype(F32), half)
    after = g32.shape[1] - PAD - half - 8
    for c in range(chunks):
        g32[c, 8:16, :] = head[:, lanes_of(c)]
        g32[c, PAD + half : PAD + half + 8, :] = tail[:, lanes_of(c)]
        g32[c, PAD + half + 8 :, :] = jnp.zeros((after, 128), F32)
    copy_g.wait()

    def widen_g(i, _):
        at = pl.multiple_of(i * 32, 32)
        for c in range(chunks):
            g32[c, pl.ds(at + PAD, 32), :] = gb[pl.ds(at, 32), lanes_of(c)].astype(F32)
        return 0

    lax.fori_loop(0, half // 32, widen_g, 0)
    copy_mat.wait()

    for m in range(tiles):
        streamed = jnp.concatenate(
            [mat[m, :, 0:WINDOW].T, mat[m, :, WINDOW:].T], axis=1
        )
        for c in range(chunks):
            scorer = par_ref[5:6, lanes_of(c)]
            scorer_high = scorer.astype(BF16).astype(F32)
            g = g32[c, OWN * m + 8 : OWN * m + 8 + SLOTS, :]
            top = jnp.where(sub8 == 0, scorer_high, jnp.where(sub8 == 1, scorer - scorer_high, g[0:8]))
            g = jnp.concatenate([top, g[8:]], axis=0).astype(BF16)
            part = lax.dot_general(
                streamed,
                jnp.concatenate([g, g], axis=0),
                (((1,), (0,)), ((), ())),
                preferred_element_type=F32,
            )
            at = 2 * OWN * m
            before = dc[c, at : at + PAD, :] if m > 0 else 0.0
            dc[c, at : at + PAD, :] = before + part[0:PAD]
            dc[c, at + PAD : at + WINDOW, :] = part[PAD:]

    def taps(i, _):
        at = pl.multiple_of(i * 16, 16)
        keeps = []
        for j in range(2):
            position = base + at + 8 * j + sub8
            remain = end_of(position, ends) - position
            keeps.append([remain > k for k in range(TAPS)])
        for c in range(chunks):
            parts = []
            for j in range(2):
                value = par_ref[0:1, lanes_of(c)] * dc[c, pl.ds(at + PAD + 8 * j, 8), :]
                for k in range(1, TAPS):
                    shifted = dc[c, pl.ds(at + PAD + 8 * j + k, 8), :]
                    value = value + par_ref[k : k + 1, lanes_of(c)] * jnp.where(keeps[j][k], shifted, 0.0)
                parts.append(value)
            ginb[pl.ds(at, 16), lanes_of(c)] = jnp.concatenate(parts, axis=0).astype(BF16)
        return 0

    lax.fori_loop(0, length // 16, taps, 0)
    copy_out = pltpu.make_async_copy(ginb, gin_hbm.at[r], sems.at[2])
    copy_out.start()
    copy_out.wait()


SMEM = pl.BlockSpec(memory_space=pltpu.SMEM)
VMEM = pl.BlockSpec(memory_space=pltpu.VMEM)
HBM = pl.BlockSpec(memory_space=pl.ANY)


def sizes_of(length, half):
    tiles = -(-(half + 3 + LEAD) // OWN)
    x_rows = -(-(2 * OWN * (tiles - 1) + WINDOW) // 32) * 32
    g_rows = -(-(OWN * (tiles - 1) + 8 + SLOTS) // 16) * 16
    return tiles, x_rows, g_rows


def forward(base, lengths, inputs, cotangent, up, down, params):
    rows, length, features = inputs.shape
    half = cotangent.shape[1]
    chunks = features // 128
    tiles, x_rows, g_rows = sizes_of(length, half)
    count = rows * tiles
    shapes = (rows, length, half, features, tiles)
    return pl.pallas_call(
        functools.partial(forward_kernel, shapes),
        out_shape=(
            jax.ShapeDtypeStruct((rows, half, features), BF16),
            jax.ShapeDtypeStruct((count, SLOTS, 2 * WINDOW), BF16),
            jax.ShapeDtypeStruct((TAPS + 2, features), F32),
        ),
        in_specs=[SMEM, SMEM, HBM, HBM, VMEM, VMEM, VMEM],
        out_specs=(HBM, HBM, VMEM),
        scratch_shapes=[
            pltpu.VMEM((rows, x_rows, features), BF16),
            pltpu.VMEM((rows, half, features), BF16),
            pltpu.VMEM((chunks, x_rows + 8, 128), F32),
            pltpu.VMEM((rows, chunks, g_rows, 128), F32),
            pltpu.VMEM((rows, chunks, x_rows, 128), BF16),
            pltpu.VMEM((rows, chunks, x_rows, 128), BF16),
            pltpu.VMEM((2, count // 2, 8, 128), F32),
            pltpu.VMEM((2, count, 8, 128), F32),
            pltpu.VMEM((count // 2, 8, 128), F32),
            pltpu.VMEM((chunks, g_rows, 128), F32),
            pltpu.VMEM((rows, half, features), BF16),
            pltpu.VMEM((count, SLOTS, 2 * WINDOW), BF16),
            pltpu.VMEM((8, features), F32),
            pltpu.VMEM((TAPS + 2, 8, features), F32),
            pltpu.SemaphoreType.DMA((4, rows)),
        ],
        compiler_params=pltpu.CompilerParams(vmem_limit_bytes=40 * 1024 * 1024),
        cost_estimate=pl.CostEstimate(
            flops=2 * count * SLOTS * WINDOW * features * 12,
            bytes_accessed=8 * inputs.size,
            transcendentals=0,
        ),
    )(base, lengths, inputs, cotangent, up, down, params)


def backward(r, base, lengths, cotangent, matrices, up, down, params, grown):
    rows, half, features = cotangent.shape
    length = 2 * half
    chunks = features // 128
    tiles, x_rows, g_rows = sizes_of(length, half)
    shapes = (rows, length, half, features, tiles)
    operands = [base, lengths, cotangent, matrices, up, down, params]
    in_specs = [SMEM, SMEM, HBM, HBM, VMEM, VMEM, VMEM]
    if grown is not None:
        operands.append(grown)
        in_specs.append(HBM)
    return pl.pallas_call(
        functools.partial(backward_kernel, shapes, r),
        out_shape=jax.ShapeDtypeStruct((rows, length, features), BF16),
        in_specs=in_specs,
        out_specs=HBM,
        scratch_shapes=[
            pltpu.VMEM((half, features), BF16),
            pltpu.VMEM((tiles, SLOTS, 2 * WINDOW), BF16),
            pltpu.VMEM((chunks, g_rows, 128), F32),
            pltpu.VMEM((chunks, x_rows, 128), F32),
            pltpu.VMEM((length, features), BF16),
            pltpu.SemaphoreType.DMA((3,)),
        ],
        input_output_aliases={} if grown is None else {7: 0},
        compiler_params=pltpu.CompilerParams(vmem_limit_bytes=16 * 1024 * 1024),
        cost_estimate=pl.CostEstimate(
            flops=2 * tiles * SLOTS * WINDOW * features * 4,
            bytes_accessed=4 * length * features,
            transcendentals=0,
        ),
    )(*operands)


def adam_update(grads, weights, first_old, second_old):
    first_new = beta_one * first_old + (1.0 - beta_one) * grads
    second_new = beta_two * second_old + (1.0 - beta_two) * grads * grads
    first_hat = first_new / (1.0 - beta_one**STEP)
    second_hat = second_new / (1.0 - beta_two**STEP)
    updated = weights - learn_rate * (
        first_hat / (jnp.sqrt(second_hat) + adam_eps) + decay_rate * weights
    )
    return (updated, first_new, second_new)


def rounds_of(axes):
    rounds = []
    for axis in axes:
        count = lax.axis_size(axis)
        step = 1
        while step < count:
            rounds.append((axis, [(i, i ^ step) for i in range(count)]))
            step *= 2
    return rounds


def per_device(inputs, lengths, params, first_moment, second_moment, cotangent):
    rows_here, length_here, features = inputs.shape
    half_here = cotangent.shape[1]
    send_up = jnp.concatenate(
        [cotangent[:, half_here - 2 :], inputs[:, length_here - (PAD - 2) :]], axis=1
    )
    send_down = jnp.concatenate([inputs[:, : PAD - 3], cotangent[:, :3]], axis=1)
    up = passed_along(send_up, "group", 1)
    down = passed_along(send_down, "group", -1)
    base = (lax.axis_index("group") * length_here).astype(jnp.int32).reshape(1)
    output, matrices, grad_params = forward(base, lengths, inputs, cotangent, up, down, params)
    grad_inputs = None
    row = 0
    for axis, exchange in rounds_of(("group", "rows")):
        received = lax.ppermute(grad_params, axis, exchange)
        if row < rows_here:
            matrices, grad_params = lax.optimization_barrier((matrices, grad_params))
            grad_inputs = backward(
                row, base, lengths, cotangent, matrices, up, down, params, grad_inputs
            )
            row += 1
            received, grad_inputs = lax.optimization_barrier((received, grad_inputs))
        grad_params = grad_params + received
    while row < rows_here:
        grad_inputs = backward(row, base, lengths, cotangent, matrices, up, down, params, grad_inputs)
        row += 1
    grad_norm = jnp.sqrt(jnp.sum(grad_params * grad_params))
    clip_scale = jnp.minimum(1.0, clip_limit / (grad_norm + 1e-06))
    new_params, new_first, new_second = adam_update(
        grad_params * clip_scale, params, first_moment, second_moment
    )
    return (output, grad_inputs, grad_norm, new_params, new_first, new_second)


def solution(mesh):
    in_specs = (P("rows", "group", None), P("rows", None), P(), P(), P(), P("rows", "group", None))
    out_specs = (P("rows", "group", None), P("rows", "group", None), P(), P(), P(), P())
    return jax.shard_map(
        per_device, mesh=mesh, in_specs=in_specs, out_specs=out_specs, check_vma=False
    )
```

```python
import functools

import jax
import jax.numpy as jnp
from jax import lax
from jax.experimental import pallas as pl
from jax.experimental.pallas import tpu as pltpu
from jax.sharding import PartitionSpec as P

STEP = 10


beta_one = 0.9
beta_two = 0.999
learn_rate = 0.2
decay_rate = 0.01
adam_eps = 1e-08
clip_limit = 1.0

TAPS = 4
SLOTS = 64
OWN = 56
LEAD = 4
WINDOW = 128
PAD = 16
F32 = jnp.float32
BF16 = jnp.bfloat16


def passed_along(value, axis, steps):
    count = lax.axis_size(axis)
    initial, last = (max(0, -steps), min(count, count - steps))
    return lax.ppermute(value, axis, [(source, source + steps) for source in range(initial, last)])


def rotate_rows(x, amount):
    for bit in (1, 2, 4):
        x = jnp.where((amount & bit) != 0, pltpu.roll(x, 8 - bit, x.ndim - 2), x)
    return x


def split(x):
    high = x.astype(BF16)
    return high, (x - high.astype(F32)).astype(BF16)


def iota(shape, dim):
    return lax.broadcasted_iota(jnp.int32, shape, dim)


def ends_of(len_ref, r):
    one = len_ref[r, 0]
    two = one + len_ref[r, 1]
    three = two + len_ref[r, 2]
    return one, two, three, three + len_ref[r, 3]


def begin_of(at, ends):
    begin = jnp.where(at >= ends[0], ends[0], 0)
    begin = jnp.where(at >= ends[1], ends[1], begin)
    return jnp.where(at >= ends[2], ends[2], begin)


def end_of(at, ends):
    end = jnp.where(at >= ends[0], ends[1], ends[0])
    end = jnp.where(at >= ends[1], ends[2], end)
    return jnp.where(at >= ends[2], ends[3], end)


def lanes_of(c):
    return slice(128 * c, 128 * c + 128)


def pack_kernel(x_hbm, g_hbm, up_ref, down_ref, x_first, x_last, g_first, g_last, sems):
    rows, length, features = x_hbm.shape
    half = g_hbm.shape[1]
    copies = [
        pltpu.make_async_copy(x_hbm.at[:, pl.ds(length - PAD, PAD), :], x_last, sems.at[0]),
        pltpu.make_async_copy(g_hbm.at[:, pl.ds(half - PAD, PAD), :], g_last, sems.at[1]),
        pltpu.make_async_copy(x_hbm.at[:, pl.ds(0, PAD), :], x_first, sems.at[2]),
        pltpu.make_async_copy(g_hbm.at[:, pl.ds(0, PAD), :], g_first, sems.at[3]),
    ]
    for copy in copies:
        copy.start()
    sub = iota((PAD, features), 0)
    for copy in copies:
        copy.wait()
    for r in range(rows):
        moved = pltpu.roll(g_last[r].astype(F32), 2, 0)
        up_ref[r] = jnp.where(sub < 2, moved, x_last[r].astype(F32)).astype(BF16)
        moved = pltpu.roll(g_first[r].astype(F32), PAD - 3, 0)
        down_ref[r] = jnp.where(sub < PAD - 3, x_first[r].astype(F32), moved).astype(BF16)


def forward_kernel(
    shapes,
    base_ref,
    len_ref,
    x_ref,
    g_ref,
    up_ref,
    down_ref,
    par_ref,
    out_hbm,
    mat,
    g32,
    grad_ref,
    xb,
    xf,
    conv_high,
    conv_low,
    dots_ref,
    comp,
    cs,
    es,
    fac_a,
    fac_b,
    tot,
    rows_e_ref,
    out32,
    outb,
    carry_o,
    acc,
    sems,
):
    rows, length, half, features, tiles = shapes
    count = rows * tiles
    pairs = count // 2
    chunks = features // 128
    base = base_ref[0]
    padded = xb.shape[1]

    def copy_out(r):
        return pltpu.make_async_copy(outb.at[r], out_hbm.at[r], sems.at[r])

    sub8 = iota((8, 128), 0)
    lane8 = iota((8, 128), 1)
    slot8 = lane8 % SLOTS
    left = lane8 < SLOTS
    delta = sub8 - 3
    first = [2 * slot8 - 3 - (2 * p + lane8 // SLOTS) for p in range(2)]
    group_of = [(f + ((sub8 - f) & 7)) >> 3 for f in first]
    turn = [f & 7 for f in first]
    first_e = 2 * slot8 - 3
    group_of_e = (first_e + ((sub8 - first_e) & 7)) >> 3
    turn_e = first_e & 7

    def place(tile):
        return tile // tiles, tile % tiles

    def tile_start(m):
        return base + 2 * OWN * m - PAD

    acc[...] = jnp.zeros_like(acc)
    carry_o[...] = jnp.zeros_like(carry_o)

    def convolve(r, at, side, where, ends):
        keeps = []
        for j in range(2):
            position = base - PAD + at + 8 * j + sub8
            offset = position - begin_of(position, ends)
            keeps.append([offset >= k for k in range(TAPS)])
        for c in range(chunks):
            parts = []
            for j in range(2):
                row = where + 8 * j
                value = par_ref[4:5, lanes_of(c)] + par_ref[0:1, lanes_of(c)] * xf[side, c, row : row + 8, :]
                for k in range(1, TAPS):
                    shifted = xf[side, c, row - k : row - k + 8, :]
                    value = value + par_ref[k : k + 1, lanes_of(c)] * jnp.where(keeps[j][k], shifted, 0.0)
                parts.append(value)
            high, low = split(jnp.concatenate(parts, axis=0))
            conv_high[r, c, pl.ds(at, 16), :] = high
            conv_low[r, c, pl.ds(at, 16), :] = low

    subd = iota((8, features), 0)
    for r in range(rows):
        up = up_ref[r]
        down = down_ref[r]
        xb[r, 0:PAD, :] = up
        xb[r, PAD + length : 2 * PAD + length, :] = down
        rest = padded - 2 * PAD - length
        if rest > 0:
            xb[r, 2 * PAD + length :, :] = jnp.zeros((rest, features), BF16)
        xb[r, PAD : PAD + length, :] = x_ref[r]
        before = jnp.where(subd >= 6, pltpu.roll(up.astype(F32)[0:8], 6, 0), 0.0)
        after = jnp.where(subd < 3, pltpu.roll(down.astype(F32)[8:16], 3, 0), 0.0)
        rest = g32.shape[2] - PAD - half - 8
        for c in range(chunks):
            g32[r, c, 8:16, :] = before[:, lanes_of(c)]
            g32[r, c, PAD : PAD + half, :] = g_ref[r, :, lanes_of(c)].astype(F32)
            g32[r, c, PAD + half : PAD + half + 8, :] = after[:, lanes_of(c)]
            g32[r, c, PAD + half + 8 :, :] = jnp.zeros((rest, 128), F32)
        for c in range(chunks):
            xf[r % 2, c, 0:8, :] = jnp.zeros((8, 128), F32)
            xf[r % 2, c, 8:24, :] = up[:, lanes_of(c)].astype(F32)
        convolve(r, 0, r % 2, 8, ends_of(len_ref, r))

    scorer_high = [par_ref[5:6, lanes_of(c)].astype(BF16).astype(F32) for c in range(chunks)]
    scorer_low = [par_ref[5:6, lanes_of(c)] - scorer_high[c] for c in range(chunks)]

    def convolve_pair(pair):
        for side in range(2):
            r, m = place(2 * pair + side)
            ends = ends_of(len_ref, r)
            at = pl.multiple_of(2 * OWN * m, 16)
            for c in range(chunks):
                xf[side, c, 8 : 8 + WINDOW, :] = xb[r, pl.ds(at, WINDOW), lanes_of(c)].astype(F32)
            for b in range(1, WINDOW // 16):
                convolve(r, pl.multiple_of(at + 16 * b, 16), side, 8 + 16 * b, ends)

    def multiply_pair(pair):
        for side in range(2):
            r, m = place(2 * pair + side)
            start = pl.multiple_of(OWN * m + 8, 8)
            at = pl.multiple_of(2 * OWN * m, 16)
            streamed, held = [], []
            for c in range(chunks):
                g = g32[r, c, pl.ds(start, SLOTS), :]
                top = jnp.where(sub8 == 0, scorer_high[c], jnp.where(sub8 == 1, scorer_low[c], g[0:8]))
                streamed.append(jnp.concatenate([top, g[8:]], axis=0).astype(BF16))
                held.append(
                    jnp.concatenate(
                        [
                            conv_high[r, c, pl.ds(at, WINDOW), :],
                            conv_low[r, c, pl.ds(at, WINDOW), :],
                        ],
                        axis=0,
                    )
                )
            product = lax.dot_general(
                jnp.concatenate(streamed, axis=1),
                jnp.concatenate(held, axis=1),
                (((1,), (1,)), ((), ())),
                preferred_element_type=F32,
            )
            dots_ref[SLOTS * side : SLOTS * side + SLOTS, :] = product[:, :WINDOW] + product[:, WINDOW:]

    def extract_pair(pair):
        dots = dots_ref[...]
        scores = jnp.concatenate(
            [
                jnp.broadcast_to(dots[i : i + 1] + dots[i + 1 : i + 2], (SLOTS, WINDOW))
                for i in (0, SLOTS)
            ],
            axis=0,
        ).T
        dots = dots.T
        banded = jnp.zeros((8, 128), F32)
        scored = jnp.zeros((8, 128), F32)
        for v in range(WINDOW // 8):
            here = group_of_e == v
            banded = jnp.where(here, dots[8 * v : 8 * v + 8], banded)
            scored = jnp.where(here, scores[8 * v : 8 * v + 8], scored)
        comp[0, pair] = banded
        comp[1, pair] = scored

    convolve_pair(0)
    multiply_pair(0)
    convolve_pair(1)

    def first_loop(i, _):
        extract_pair(i - 1)
        multiply_pair(i)
        convolve_pair(i + 1)
        return 0

    lax.fori_loop(1, pairs - 1, first_loop, 0)
    extract_pair(pairs - 2)
    multiply_pair(pairs - 1)
    extract_pair(pairs - 1)

    ends = [ends_of(len_ref, r) for r in range(rows)]
    for pair in range(pairs):
        both = (2 * pair, 2 * pair + 1)
        dots = rotate_rows(comp[0, pair], turn_e)
        scores = rotate_rows(comp[1, pair], turn_e)
        coef = jnp.zeros((8, 128), F32)
        coef_e = jnp.zeros((8, 128), F32)
        for p in range(2):
            at = [tile_start(place(t)[1]) + 2 * slot8 + p for t in both]
            begin = [begin_of(a, ends[place(t)[0]]) for a, t in zip(at, both)]
            end = [end_of(a, ends[place(t)[0]]) for a, t in zip(at, both)]
            offset = jnp.maximum(jnp.where(left, at[0] - begin[0], at[1] - begin[1]), 0)
            remain = jnp.where(left, end[0] - at[0], end[1] - at[1])
            masks, inverses, logits, grads = [], [], [], []
            for b in range(1, TAPS + 1):
                if b == 3:
                    thirds = ((offset.astype(F32) + 0.5) * (1.0 / 3.0)).astype(jnp.int32)
                    within = offset - 3 * thirds
                else:
                    within = offset & (b - 1)
                upper = jnp.minimum(b - within, remain)
                mask = (delta >= p - within) & (delta < p + upper)
                inverse = 1.0 / jnp.maximum(within + upper, 1).astype(F32)
                masks.append(mask)
                inverses.append(inverse)
                logits.append(jnp.sum(jnp.where(mask, scores, 0.0), axis=0, keepdims=True) * inverse)
                grads.append(
                    jnp.sum(jnp.where(mask, dots, 0.0), axis=0, keepdims=True) * (0.5 * inverse)
                )
            largest = functools.reduce(jnp.maximum, logits)
            powers = [jnp.exp(logit - largest) for logit in logits]
            scale = 1.0 / sum(powers)
            shares = [power * scale for power in powers]
            mean = sum(share * grad for share, grad in zip(shares, grads))
            for mask, inverse, share, grad in zip(masks, inverses, shares, grads):
                coef = coef + jnp.where(mask, (0.5 * share) * inverse, 0.0)
                coef_e = coef_e + jnp.where(mask, share * (grad - mean) * inverse, 0.0)
        owned = (slot8 >= LEAD) & (slot8 < LEAD + OWN)
        coef = jnp.where(owned, coef, 0.0)
        coef_e = jnp.where(owned, coef_e, 0.0)
        es[pair] = rotate_rows(coef_e, (8 - turn_e) & 7)
        swapped = pltpu.roll(coef, SLOTS, 1)
        for side, tile in enumerate(both):
            r, m = place(tile)
            at = tile_start(m) + 2 * slot8 + delta
            offset = at - begin_of(at, ends[r])
            alone = jnp.where(left, coef, swapped) if side == 0 else jnp.where(left, swapped, coef)
            for p in range(2):
                kept = jnp.where((offset >= 2 * p + lane8 // SLOTS) & (at >= 0), alone, 0.0)
                cs[p, tile] = rotate_rows(kept, (8 - turn[p]) & 7)

    slots_down = iota((SLOTS, 128), 0)
    wide = 2 if chunks % 2 == 0 else 1
    factors = (fac_a, fac_b)

    def spread_pair(pair):
        spread = jnp.concatenate(
            [jnp.where(group_of_e == v, es[pair], 0.0) for v in range(WINDOW // 8)], axis=0
        ).T
        for side in range(2):
            _, m = place(2 * pair + side)
            from_row = OWN * m - 8
            part = spread[SLOTS * side : SLOTS * side + SLOTS]
            here = (from_row + slots_down >= 0) & (from_row + slots_down < half)
            own_e = jnp.sum(jnp.where(here, part, 0.0), axis=0, keepdims=True)
            all_e = jnp.sum(part, axis=0, keepdims=True)
            rows_e_ref[side, 0] = jnp.broadcast_to(own_e, (8, 128))
            rows_e_ref[side, 1] = jnp.broadcast_to(all_e, (8, 128))

    def build(pair, side):
        tile = 2 * pair + side
        r, m = place(tile)
        own_e = rows_e_ref[side, 0]
        all_e = rows_e_ref[side, 1]
        at = tile_start(m) + lane8
        offset = at - begin_of(at, ends_of(len_ref, r))
        bands = []
        for p in range(2):
            bands.append(
                jnp.concatenate(
                    [jnp.where(group_of[p] == v, cs[p, tile], 0.0) for v in range(WINDOW // 8)], axis=0
                ).T
            )
        for k in range(TAPS):
            row_k = jnp.where((offset >= k) & (at >= 0), own_e, 0.0)
            if k > 0:
                row_k = pltpu.roll(row_k, 128 - k, 1)
            matrix = bands[k // 2][SLOTS * (k % 2) : SLOTS * (k % 2) + SLOTS]
            if k == 0:
                back = jnp.concatenate([jnp.where(sub8 < 2, all_e, matrix[0:8]), matrix[8:]], axis=0)
                high, low = split(back)
                mat[tile, :, 0:WINDOW] = high
                mat[tile, :, WINDOW:] = low
            matrix = jnp.concatenate([jnp.where(sub8 == 0, row_k, matrix[0:8]), matrix[8:]], axis=0)
            if k == 0:
                total = jnp.sum(matrix, axis=1, keepdims=True)
                tot[side] = jnp.broadcast_to(total, (SLOTS, 128))
            high, low = split(matrix)
            factors[side][SLOTS * k : SLOTS * (k + 1), 0:WINDOW] = high
            factors[side][SLOTS * k : SLOTS * (k + 1), WINDOW:] = low

    def apply(pair, side):
        tile = 2 * pair + side
        r, m = place(tile)
        start = pl.multiple_of(OWN * m + 8, 8)
        window = pl.multiple_of(2 * OWN * m, 16)
        factor = factors[side][...]
        total = tot[side]
        from_row = OWN * m - 8
        mine = [from_row + 8 * i + sub8 < half for i in range(SLOTS // 8)]
        for w in range(chunks // wide):
            x = xb[r, pl.ds(window, WINDOW), 128 * wide * w : 128 * wide * (w + 1)]
            mixed = lax.dot_general(
                factor,
                jnp.concatenate([x, x], axis=0),
                (((1,), (0,)), ((), ())),
                preferred_element_type=F32,
            )
            for i in range(wide):
                c = wide * w + i
                lanes = lanes_of(c)
                g = g32[r, c, pl.ds(start, SLOTS), :]
                parts = [
                    jnp.where(
                        sub8 == 0,
                        par_ref[5:6, lanes],
                        jnp.where((sub8 >= LEAD) & (from_row + sub8 >= 0), g[0:8], 0.0),
                    )
                ]
                for j in range(1, SLOTS // 8):
                    parts.append(jnp.where(mine[j], g[8 * j : 8 * j + 8], 0.0))
                g = jnp.concatenate(parts, axis=0)
                value = total * par_ref[4:5, lanes]
                for k in range(TAPS):
                    taken = mixed[SLOTS * k : SLOTS * (k + 1), lanes_of(i)]
                    value = value + taken * par_ref[k : k + 1, lanes]
                    acc[k, :, lanes] += jnp.sum((taken * g).reshape(SLOTS // 8, 8, 128), axis=0)
                acc[4, :, lanes] += jnp.sum((total * g).reshape(SLOTS // 8, 8, 128), axis=0)
                acc[5, :, lanes] += jnp.where(sub8 == 0, value[0:8], 0.0)
                top = carry_o[:, lanes] + jnp.where(sub8 < LEAD, 0.0, value[0:8])
                out32[r % 2, c, pl.ds(start, 8), :] = top
                out32[r % 2, c, pl.ds(start + 8, OWN - 8), :] = value[8:OWN]
                carry_o[:, lanes] = jnp.where(m < tiles - 1, value[OWN:], 0.0)

    def finish(r):
        for c in range(chunks):
            outb[r, :, lanes_of(c)] = out32[r % 2, c, PAD : PAD + half, :].astype(BF16)
        copy_out(r).start()

    spread_pair(0)
    build(0, 0)
    build(0, 1)

    def second_loop(i, _):
        for side in range(2):
            r, m = place(2 * i - 1 + side)

            @pl.when((m == 0) & (i > 0))
            def _():
                finish(r - 1)

        spread_pair(i + 1)
        for side in range(2):
            apply(i, side)
            build(i + 1, side)
        return 0

    lax.fori_loop(0, pairs - 1, second_loop, 0)
    apply(pairs - 1, 0)
    apply(pairs - 1, 1)
    for r in range(rows):
        if r * tiles > 2 * (pairs - 2):
            finish(r - 1)
    finish(rows - 1)
    for k in range(TAPS + 2):
        grad_ref[k : k + 1, :] = jnp.sum(acc[k], axis=0, keepdims=True)
    for r in range(rows):
        copy_out(r).wait()


def backward_kernel(shapes, r, base_ref, len_ref, mat, g32, par_ref, *refs):
    gin_hbm, dc, ginb, sems = refs[-4:]
    rows, length, half, features, tiles = shapes
    chunks = features // 128
    wide = 2 if chunks % 2 == 0 else 1
    base = base_ref[0]
    sub8 = iota((8, 128), 0)
    ends = ends_of(len_ref, r)

    for m in range(tiles):
        tile = r * tiles + m
        streamed = jnp.concatenate([mat[tile, :, 0:WINDOW].T, mat[tile, :, WINDOW:].T], axis=1)
        at = 2 * OWN * m
        for w in range(chunks // wide):
            held = []
            for i in range(wide):
                lanes = lanes_of(wide * w + i)
                scorer = par_ref[5:6, lanes]
                scorer_high = scorer.astype(BF16).astype(F32)
                g = g32[r, wide * w + i, OWN * m + 8 : OWN * m + 8 + SLOTS, :]
                top = jnp.where(
                    sub8 == 0, scorer_high, jnp.where(sub8 == 1, scorer - scorer_high, g[0:8])
                )
                held.append(jnp.concatenate([top, g[8:]], axis=0).astype(BF16))
            held = jnp.concatenate(held, axis=1)
            part = lax.dot_general(
                streamed,
                jnp.concatenate([held, held], axis=0),
                (((1,), (0,)), ((), ())),
                preferred_element_type=F32,
            )
            for i in range(wide):
                c = wide * w + i
                before = dc[c, at : at + PAD, :] if m > 0 else 0.0
                dc[c, at : at + PAD, :] = before + part[0:PAD, lanes_of(i)]
                dc[c, at + PAD : at + WINDOW, :] = part[PAD:, lanes_of(i)]

    def taps(i, _):
        at = pl.multiple_of(i * 16, 16)
        keeps = []
        for j in range(2):
            position = base + at + 8 * j + sub8
            remain = end_of(position, ends) - position
            keeps.append([remain > k for k in range(TAPS)])
        for c in range(chunks):
            parts = []
            for j in range(2):
                value = par_ref[0:1, lanes_of(c)] * dc[c, pl.ds(at + PAD + 8 * j, 8), :]
                for k in range(1, TAPS):
                    shifted = dc[c, pl.ds(at + PAD + 8 * j + k, 8), :]
                    value = value + par_ref[k : k + 1, lanes_of(c)] * jnp.where(keeps[j][k], shifted, 0.0)
                parts.append(value)
            ginb[pl.ds(at, 16), lanes_of(c)] = jnp.concatenate(parts, axis=0).astype(BF16)
        return 0

    pieces = 2
    copies = []
    for piece in range(pieces):
        size = length // pieces
        lax.fori_loop(piece * size // 16, (piece + 1) * size // 16, taps, 0)
        copies.append(
            pltpu.make_async_copy(
                ginb.at[pl.ds(piece * size, size), :],
                gin_hbm.at[r, pl.ds(piece * size, size), :],
                sems.at[piece],
            )
        )
        copies[-1].start()
    for copy in copies:
        copy.wait()


SMEM = pl.BlockSpec(memory_space=pltpu.SMEM)
VMEM = pl.BlockSpec(memory_space=pltpu.VMEM)
HBM = pl.BlockSpec(memory_space=pltpu.HBM)


def sizes_of(length, half):
    tiles = -(-(half + 3 + LEAD) // OWN)
    x_rows = 2 * OWN * (tiles - 1) + WINDOW
    g_rows = -(-(OWN * (tiles - 1) + 8 + SLOTS) // 16) * 16
    return tiles, x_rows, g_rows


def packed(inputs, cotangent):
    rows, _, features = inputs.shape
    part = jax.ShapeDtypeStruct((rows, PAD, features), BF16)
    return pl.pallas_call(
        pack_kernel,
        out_shape=(part, part),
        in_specs=[HBM, HBM],
        out_specs=(VMEM, VMEM),
        scratch_shapes=[pltpu.VMEM((rows, PAD, features), BF16)] * 4 + [pltpu.SemaphoreType.DMA((4,))],
        compiler_params=pltpu.CompilerParams(vmem_limit_bytes=60 * 1024 * 1024),
    )(inputs, cotangent)


def forward(base, lengths, inputs, cotangent, up, down, params):
    rows, length, features = inputs.shape
    half = cotangent.shape[1]
    chunks = features // 128
    tiles, x_rows, g_rows = sizes_of(length, half)
    count = rows * tiles
    shapes = (rows, length, half, features, tiles)
    return pl.pallas_call(
        functools.partial(forward_kernel, shapes),
        out_shape=(
            jax.ShapeDtypeStruct((rows, half, features), BF16),
            jax.ShapeDtypeStruct((count, SLOTS, 2 * WINDOW), BF16),
            jax.ShapeDtypeStruct((rows, chunks, g_rows, 128), F32),
            jax.ShapeDtypeStruct((TAPS + 2, features), F32),
        ),
        in_specs=[SMEM, SMEM, VMEM, VMEM, VMEM, VMEM, VMEM],
        out_specs=(HBM, VMEM, VMEM, VMEM),
        scratch_shapes=[
            pltpu.VMEM((rows, x_rows, features), BF16),
            pltpu.VMEM((2, chunks, WINDOW + 8, 128), F32),
            pltpu.VMEM((rows, chunks, x_rows, 128), BF16),
            pltpu.VMEM((rows, chunks, x_rows, 128), BF16),
            pltpu.VMEM((2 * SLOTS, WINDOW), F32),
            pltpu.VMEM((2, count // 2, 8, 128), F32),
            pltpu.VMEM((2, count, 8, 128), F32),
            pltpu.VMEM((count // 2, 8, 128), F32),
            pltpu.VMEM((TAPS * SLOTS, 2 * WINDOW), BF16),
            pltpu.VMEM((TAPS * SLOTS, 2 * WINDOW), BF16),
            pltpu.VMEM((2, SLOTS, 128), F32),
            pltpu.VMEM((2, 2, 8, 128), F32),
            pltpu.VMEM((2, chunks, g_rows, 128), F32),
            pltpu.VMEM((rows, half, features), BF16),
            pltpu.VMEM((8, features), F32),
            pltpu.VMEM((TAPS + 2, 8, features), F32),
            pltpu.SemaphoreType.DMA((rows,)),
        ],
        compiler_params=pltpu.CompilerParams(vmem_limit_bytes=40 * 1024 * 1024),
        cost_estimate=pl.CostEstimate(
            flops=2 * count * SLOTS * WINDOW * features * 12,
            bytes_accessed=8 * inputs.size,
            transcendentals=0,
        ),
    )(base, lengths, inputs, cotangent, up, down, params)


def backward(r, base, lengths, shape, matrices, padded, params, grown):
    rows, length, features = shape
    half = length // 2
    chunks = features // 128
    tiles, x_rows, g_rows = sizes_of(length, half)
    shapes = (rows, length, half, features, tiles)
    operands = [base, lengths, matrices, padded, params]
    in_specs = [SMEM, SMEM, VMEM, VMEM, VMEM]
    if grown is not None:
        operands.append(grown)
        in_specs.append(HBM)
    return pl.pallas_call(
        functools.partial(backward_kernel, shapes, r),
        out_shape=jax.ShapeDtypeStruct(shape, BF16),
        in_specs=in_specs,
        out_specs=HBM,
        scratch_shapes=[
            pltpu.VMEM((chunks, x_rows, 128), F32),
            pltpu.VMEM((length, features), BF16),
            pltpu.SemaphoreType.DMA((2,)),
        ],
        input_output_aliases={} if grown is None else {5: 0},
        compiler_params=pltpu.CompilerParams(vmem_limit_bytes=12 * 1024 * 1024),
        cost_estimate=pl.CostEstimate(
            flops=2 * tiles * SLOTS * WINDOW * features * 4,
            bytes_accessed=4 * length * features,
            transcendentals=0,
        ),
    )(*operands)


def adam_update(grads, weights, first_old, second_old):
    first_new = beta_one * first_old + (1.0 - beta_one) * grads
    second_new = beta_two * second_old + (1.0 - beta_two) * grads * grads
    first_hat = first_new / (1.0 - beta_one**STEP)
    second_hat = second_new / (1.0 - beta_two**STEP)
    updated = weights - learn_rate * (
        first_hat / (jnp.sqrt(second_hat) + adam_eps) + decay_rate * weights
    )
    return (updated, first_new, second_new)


def rounds_of(axes):
    rounds = []
    for axis in axes:
        count = lax.axis_size(axis)
        step = 1
        while step < count:
            rounds.append((axis, [(i, i ^ step) for i in range(count)]))
            step *= 2
    return rounds


def per_device(inputs, lengths, params, first_moment, second_moment, cotangent):
    rows_here, length_here, _ = inputs.shape
    send_up, send_down = packed(inputs, cotangent)
    up = passed_along(send_up, "group", 1)
    down = passed_along(send_down, "group", -1)
    base = (lax.axis_index("group") * length_here).astype(jnp.int32).reshape(1)
    output, matrices, padded, grad_params = forward(
        base, lengths, inputs, cotangent, up, down, params
    )

    def backward_row(row, matrices, grown):
        return backward(row, base, lengths, inputs.shape, matrices, padded, params, grown)

    grad_inputs = None
    row = 0
    for axis, exchange in rounds_of(("group", "rows")):
        received = lax.ppermute(grad_params, axis, exchange)
        if row < rows_here:
            matrices, grad_params = lax.optimization_barrier((matrices, grad_params))
            grad_inputs = backward_row(row, matrices, grad_inputs)
            row += 1
            received, grad_inputs = lax.optimization_barrier((received, grad_inputs))
        grad_params = grad_params + received
    while row < rows_here:
        grad_inputs = backward_row(row, matrices, grad_inputs)
        row += 1
    grad_norm = jnp.sqrt(jnp.sum(grad_params * grad_params))
    clip_scale = jnp.minimum(1.0, clip_limit / (grad_norm + 1e-06))
    new_params, new_first, new_second = adam_update(
        grad_params * clip_scale, params, first_moment, second_moment
    )
    return (output, grad_inputs, grad_norm, new_params, new_first, new_second)


def solution(mesh):
    in_specs = (P("rows", "group", None), P("rows", None), P(), P(), P(), P("rows", "group", None))
    out_specs = (P("rows", "group", None), P("rows", "group", None), P(), P(), P(), P())
    return jax.shard_map(
        per_device, mesh=mesh, in_specs=in_specs, out_specs=out_specs, check_vma=False
    )
```

```python
import functools

import jax
import jax.numpy as jnp
from jax import lax
from jax.experimental import pallas as pl
from jax.experimental.pallas import tpu as pltpu
from jax.sharding import PartitionSpec as P

STEP = 10


beta_one = 0.9
beta_two = 0.999
learn_rate = 0.2
decay_rate = 0.01
adam_eps = 1e-08
clip_limit = 1.0

TAPS = 4
SLOTS = 64
PACK_LIMIT = 50 * 1024 * 1024
OWN = 56
LEAD = 4
WINDOW = 128
PAD = 16
F32 = jnp.float32
BF16 = jnp.bfloat16


def pairs_of(axis, first):
    count = lax.axis_size(axis)
    pairs = [(i, i + 1) for i in range(first, count - 1, 2)]
    return pairs + [(j, i) for i, j in pairs]


def rotate_rows(x, amount):
    for bit in (1, 2, 4):
        x = jnp.where((amount & bit) != 0, pltpu.roll(x, 8 - bit, x.ndim - 2), x)
    return x


def split(x):
    high = x.astype(BF16)
    return high, (x - high.astype(F32)).astype(BF16)


def iota(shape, dim):
    return lax.broadcasted_iota(jnp.int32, shape, dim)


def ends_of(len_ref, r):
    one = len_ref[r, 0]
    two = one + len_ref[r, 1]
    three = two + len_ref[r, 2]
    return one, two, three, three + len_ref[r, 3]


def begin_of(at, ends):
    begin = jnp.where(at >= ends[0], ends[0], 0)
    begin = jnp.where(at >= ends[1], ends[1], begin)
    return jnp.where(at >= ends[2], ends[2], begin)


def end_of(at, ends):
    end = jnp.where(at >= ends[0], ends[1], ends[0])
    end = jnp.where(at >= ends[1], ends[2], end)
    return jnp.where(at >= ends[2], ends[3], end)


def lanes_of(c):
    return slice(128 * c, 128 * c + 128)


def pack_kernel(base_ref, x_hbm, g_hbm, near_ref, far_ref, x_first, x_last, g_first, g_last, sems):
    rows, length, features = x_hbm.shape
    half = g_hbm.shape[1]
    copies = [
        pltpu.make_async_copy(x_hbm.at[:, pl.ds(length - PAD, PAD), :], x_last, sems.at[0]),
        pltpu.make_async_copy(g_hbm.at[:, pl.ds(half - PAD, PAD), :], g_last, sems.at[1]),
        pltpu.make_async_copy(x_hbm.at[:, pl.ds(0, PAD), :], x_first, sems.at[2]),
        pltpu.make_async_copy(g_hbm.at[:, pl.ds(0, PAD), :], g_first, sems.at[3]),
    ]
    for copy in copies:
        copy.start()
    even = (base_ref[0] // length) % 2 == 0
    sub = iota((PAD, features), 0)
    for copy in copies:
        copy.wait()
    for r in range(rows):
        moved = pltpu.roll(g_last[r].astype(F32), 2, 0)
        last = jnp.where(sub < 2, moved, x_last[r].astype(F32))
        moved = pltpu.roll(g_first[r].astype(F32), PAD - 3, 0)
        first = jnp.where(sub < PAD - 3, x_first[r].astype(F32), moved)
        near_ref[r] = jnp.where(even, last, first).astype(BF16)
        far_ref[r] = jnp.where(even, first, last).astype(BF16)


def forward_kernel(
    shapes,
    base_ref,
    len_ref,
    x_ref,
    g_ref,
    near_ref,
    far_ref,
    par_ref,
    out_hbm,
    mat,
    g32,
    grad_ref,
    xb,
    xf,
    conv_aa,
    conv_ab,
    conv_ba,
    conv_bb,
    edge,
    dots_a,
    dots_b,
    comp,
    cs,
    es,
    fac_a,
    fac_b,
    tot,
    rows_e_ref,
    out32,
    outb,
    carry_o,
    acc,
    sems,
):
    rows, length, half, features, tiles = shapes
    count = rows * tiles
    pairs = count // 2
    chunks = features // 128
    base = base_ref[0]

    def copy_out(r):
        return pltpu.make_async_copy(outb.at[r], out_hbm.at[r], sems.at[r])

    sub8 = iota((8, 128), 0)
    lane8 = iota((8, 128), 1)
    slot8 = lane8 % SLOTS
    left = lane8 < SLOTS
    delta = sub8 - 3
    first = [2 * slot8 - 3 - (2 * p + lane8 // SLOTS) for p in range(2)]
    group_of = [(f + ((sub8 - f) & 7)) >> 3 for f in first]
    turn = [f & 7 for f in first]
    first_e = 2 * slot8 - 3
    group_of_e = (first_e + ((sub8 - first_e) & 7)) >> 3
    turn_e = first_e & 7

    def place(tile):
        return tile // tiles, tile % tiles

    def tile_start(m):
        return base + 2 * OWN * m - PAD

    acc[...] = jnp.zeros_like(acc)
    carry_o[...] = jnp.zeros_like(carry_o)

    def convolve(r, at, side, where, ends, place_high, place_low):
        keeps = []
        for j in range(2):
            position = base - PAD + at + 8 * j + sub8
            offset = position - begin_of(position, ends)
            keeps.append([offset >= k for k in range(TAPS)])
        for c in range(chunks):
            parts = []
            for j in range(2):
                row = where + 8 * j
                value = par_ref[4:5, lanes_of(c)] + par_ref[0:1, lanes_of(c)] * xf[side, c, row : row + 8, :]
                for k in range(1, TAPS):
                    shifted = xf[side, c, row - k : row - k + 8, :]
                    value = value + par_ref[k : k + 1, lanes_of(c)] * jnp.where(keeps[j][k], shifted, 0.0)
                parts.append(value)
            high, low = split(jnp.concatenate(parts, axis=0))
            for ref, *index in place_high(c):
                ref[(*index, slice(None))] = high
            for ref, *index in place_low(c):
                ref[(*index, slice(None))] = low

    subd = iota((8, features), 0)
    even = (base // length) % 2 == 0
    for r in range(rows):
        near = near_ref[r].astype(F32)
        far = far_ref[r].astype(F32)
        up = jnp.where(even, far, near)
        down = jnp.where(even, near, far)
        xb[r, 0:PAD, :] = up.astype(BF16)
        xb[r, PAD + length : 2 * PAD + length, :] = down.astype(BF16)
        rest = xb.shape[1] - 2 * PAD - length
        if rest > 0:
            xb[r, 2 * PAD + length :, :] = jnp.zeros((rest, features), BF16)
        xb[r, PAD : PAD + length, :] = x_ref[r]
        before = jnp.where(subd >= 6, pltpu.roll(up[0:8], 6, 0), 0.0)
        after = jnp.where(subd < 3, pltpu.roll(down[8:16], 3, 0), 0.0)
        rest = g32.shape[2] - PAD - half - 8
        for c in range(chunks):
            g32[r, c, 8:16, :] = before[:, lanes_of(c)]
            g32[r, c, PAD : PAD + half, :] = g_ref[r, :, lanes_of(c)].astype(F32)
            g32[r, c, PAD + half : PAD + half + 8, :] = after[:, lanes_of(c)]
            g32[r, c, PAD + half + 8 :, :] = jnp.zeros((rest, 128), F32)
        for c in range(chunks):
            xf[r % 2, c, 0:8, :] = jnp.zeros((8, 128), F32)
            xf[r % 2, c, 8:24, :] = up[:, lanes_of(c)]
        convolve(
            r,
            0,
            r % 2,
            8,
            ends_of(len_ref, r),
            lambda c: [(edge, count + r, c, slice(0, 16))],
            lambda c: [(edge, count + r, c, slice(16, 32))],
        )

    scorer_high = [par_ref[5:6, lanes_of(c)].astype(BF16).astype(F32) for c in range(chunks)]
    scorer_low = [par_ref[5:6, lanes_of(c)] - scorer_high[c] for c in range(chunks)]

    convs = ((conv_aa, conv_ab), (conv_ba, conv_bb))
    dots_refs = (dots_a, dots_b)

    def convolve_pair(pair, parity):
        for side in range(2):
            tile = 2 * pair + side
            r, m = place(tile)
            ends = ends_of(len_ref, r)
            at = pl.multiple_of(2 * OWN * m, 16)
            conv = convs[parity][side]
            source = jnp.where(m == 0, count + r, tile - 1)
            for c in range(chunks):
                conv[c, 0:16, :] = edge[source, c, 0:16, :]
                conv[c, WINDOW : WINDOW + 16, :] = edge[source, c, 16:32, :]
                xf[2 * parity + side, c, 8 : 8 + WINDOW, :] = xb[r, pl.ds(at, WINDOW), lanes_of(c)].astype(F32)
            for b in range(1, WINDOW // 16):
                last = b == WINDOW // 16 - 1
                convolve(
                    r,
                    at + 16 * b,
                    2 * parity + side,
                    8 + 16 * b,
                    ends,
                    lambda c: [(conv, c, slice(16 * b, 16 * b + 16))]
                    + ([(edge, tile, c, slice(0, 16))] if last else []),
                    lambda c: [(conv, c, slice(WINDOW + 16 * b, WINDOW + 16 * b + 16))]
                    + ([(edge, tile, c, slice(16, 32))] if last else []),
                )

    def multiply_pair(pair, parity):
        for side in range(2):
            r, m = place(2 * pair + side)
            start = pl.multiple_of(OWN * m + 8, 8)
            streamed, held = [], []
            for c in range(chunks):
                g = g32[r, c, pl.ds(start, SLOTS), :]
                top = jnp.where(sub8 == 0, scorer_high[c], jnp.where(sub8 == 1, scorer_low[c], g[0:8]))
                streamed.append(jnp.concatenate([top, g[8:]], axis=0).astype(BF16))
                held.append(convs[parity][side][c])
            product = lax.dot_general(
                jnp.concatenate(streamed, axis=1),
                jnp.concatenate(held, axis=1),
                (((1,), (1,)), ((), ())),
                preferred_element_type=F32,
            )
            dots_refs[parity][SLOTS * side : SLOTS * side + SLOTS, :] = (
                product[:, :WINDOW] + product[:, WINDOW:]
            )

    def extract_pair(pair, parity):
        dots = dots_refs[parity][...]
        scores = jnp.concatenate(
            [
                jnp.broadcast_to(dots[i : i + 1] + dots[i + 1 : i + 2], (SLOTS, WINDOW))
                for i in (0, SLOTS)
            ],
            axis=0,
        ).T
        dots = dots.T
        banded = jnp.zeros((8, 128), F32)
        scored = jnp.zeros((8, 128), F32)
        for v in range(WINDOW // 8):
            here = group_of_e == v
            banded = jnp.where(here, dots[8 * v : 8 * v + 8], banded)
            scored = jnp.where(here, scores[8 * v : 8 * v + 8], scored)
        comp[0, pair] = banded
        comp[1, pair] = scored

    dots_b[...] = jnp.zeros_like(dots_b)
    convolve_pair(0, 0)

    def first_loop(i, _):
        extract_pair(jnp.maximum(2 * i - 1, 0), 1)
        multiply_pair(2 * i, 0)
        convolve_pair(2 * i + 1, 1)
        extract_pair(2 * i, 0)
        multiply_pair(2 * i + 1, 1)
        convolve_pair(jnp.minimum(2 * i + 2, pairs - 1), 0)
        return 0

    lax.fori_loop(0, pairs // 2, first_loop, 0)
    extract_pair(pairs - 1, 1)

    ends = [ends_of(len_ref, r) for r in range(rows)]
    for pair in range(pairs):
        both = (2 * pair, 2 * pair + 1)
        dots = rotate_rows(comp[0, pair], turn_e)
        scores = rotate_rows(comp[1, pair], turn_e)
        coef = jnp.zeros((8, 128), F32)
        coef_e = jnp.zeros((8, 128), F32)
        for p in range(2):
            at = [tile_start(place(t)[1]) + 2 * slot8 + p for t in both]
            begin = [begin_of(a, ends[place(t)[0]]) for a, t in zip(at, both)]
            end = [end_of(a, ends[place(t)[0]]) for a, t in zip(at, both)]
            offset = jnp.maximum(jnp.where(left, at[0] - begin[0], at[1] - begin[1]), 0)
            remain = jnp.where(left, end[0] - at[0], end[1] - at[1])
            masks, inverses, logits, grads = [], [], [], []
            for b in range(1, TAPS + 1):
                if b == 3:
                    thirds = ((offset.astype(F32) + 0.5) * (1.0 / 3.0)).astype(jnp.int32)
                    within = offset - 3 * thirds
                else:
                    within = offset & (b - 1)
                upper = jnp.minimum(b - within, remain)
                mask = (delta >= p - within) & (delta < p + upper)
                inverse = 1.0 / jnp.maximum(within + upper, 1).astype(F32)
                masks.append(mask)
                inverses.append(inverse)
                logits.append(jnp.sum(jnp.where(mask, scores, 0.0), axis=0, keepdims=True) * inverse)
                grads.append(
                    jnp.sum(jnp.where(mask, dots, 0.0), axis=0, keepdims=True) * (0.5 * inverse)
                )
            largest = functools.reduce(jnp.maximum, logits)
            powers = [jnp.exp(logit - largest) for logit in logits]
            scale = 1.0 / sum(powers)
            shares = [power * scale for power in powers]
            mean = sum(share * grad for share, grad in zip(shares, grads))
            for mask, inverse, share, grad in zip(masks, inverses, shares, grads):
                coef = coef + jnp.where(mask, (0.5 * share) * inverse, 0.0)
                coef_e = coef_e + jnp.where(mask, share * (grad - mean) * inverse, 0.0)
        owned = (slot8 >= LEAD) & (slot8 < LEAD + OWN)
        coef = jnp.where(owned, coef, 0.0)
        coef_e = jnp.where(owned, coef_e, 0.0)
        es[pair] = rotate_rows(coef_e, (8 - turn_e) & 7)
        swapped = pltpu.roll(coef, SLOTS, 1)
        for side, tile in enumerate(both):
            r, m = place(tile)
            at = tile_start(m) + 2 * slot8 + delta
            offset = at - begin_of(at, ends[r])
            alone = jnp.where(left, coef, swapped) if side == 0 else jnp.where(left, swapped, coef)
            for p in range(2):
                kept = jnp.where((offset >= 2 * p + lane8 // SLOTS) & (at >= 0), alone, 0.0)
                cs[p, tile] = rotate_rows(kept, (8 - turn[p]) & 7)

    slots_down = iota((SLOTS, 128), 0)
    wide = 2 if chunks % 2 == 0 else 1
    factors = (fac_a, fac_b)

    def spread_pair(pair):
        spread = jnp.concatenate(
            [jnp.where(group_of_e == v, es[pair], 0.0) for v in range(WINDOW // 8)], axis=0
        ).T
        for side in range(2):
            _, m = place(2 * pair + side)
            from_row = OWN * m - 8
            part = spread[SLOTS * side : SLOTS * side + SLOTS]
            here = (from_row + slots_down >= 0) & (from_row + slots_down < half)
            own_e = jnp.sum(jnp.where(here, part, 0.0), axis=0, keepdims=True)
            all_e = jnp.sum(part, axis=0, keepdims=True)
            rows_e_ref[side, 0] = jnp.broadcast_to(own_e, (8, 128))
            rows_e_ref[side, 1] = jnp.broadcast_to(all_e, (8, 128))

    def build(pair, side):
        tile = 2 * pair + side
        r, m = place(tile)
        own_e = rows_e_ref[side, 0]
        all_e = rows_e_ref[side, 1]
        at = tile_start(m) + lane8
        offset = at - begin_of(at, ends_of(len_ref, r))
        bands = []
        for p in range(2):
            bands.append(
                jnp.concatenate(
                    [jnp.where(group_of[p] == v, cs[p, tile], 0.0) for v in range(WINDOW // 8)], axis=0
                ).T
            )
        for k in range(TAPS):
            row_k = jnp.where((offset >= k) & (at >= 0), own_e, 0.0)
            if k > 0:
                row_k = pltpu.roll(row_k, 128 - k, 1)
            matrix = bands[k // 2][SLOTS * (k % 2) : SLOTS * (k % 2) + SLOTS]
            if k == 0:
                back = jnp.concatenate([jnp.where(sub8 < 2, all_e, matrix[0:8]), matrix[8:]], axis=0)
                high, low = split(back)
                mat[tile, :, 0:WINDOW] = high
                mat[tile, :, WINDOW:] = low
            matrix = jnp.concatenate([jnp.where(sub8 == 0, row_k, matrix[0:8]), matrix[8:]], axis=0)
            if k == 0:
                total = jnp.sum(matrix, axis=1, keepdims=True)
                tot[side] = jnp.broadcast_to(total, (SLOTS, 128))
            high, low = split(matrix)
            factors[side][SLOTS * k : SLOTS * (k + 1), 0:WINDOW] = high
            factors[side][SLOTS * k : SLOTS * (k + 1), WINDOW:] = low

    def apply(pair, side):
        tile = 2 * pair + side
        r, m = place(tile)
        start = pl.multiple_of(OWN * m + 8, 8)
        window = pl.multiple_of(2 * OWN * m, 16)
        factor = factors[side][...]
        total = tot[side]
        from_row = OWN * m - 8
        mine = [from_row + 8 * i + sub8 < half for i in range(SLOTS // 8)]
        for w in range(chunks // wide):
            x = xb[r, pl.ds(window, WINDOW), 128 * wide * w : 128 * wide * (w + 1)]
            mixed = lax.dot_general(
                factor,
                jnp.concatenate([x, x], axis=0),
                (((1,), (0,)), ((), ())),
                preferred_element_type=F32,
            )
            for i in range(wide):
                c = wide * w + i
                lanes = lanes_of(c)
                g = g32[r, c, pl.ds(start, SLOTS), :]
                parts = [
                    jnp.where(
                        sub8 == 0,
                        par_ref[5:6, lanes],
                        jnp.where((sub8 >= LEAD) & (from_row + sub8 >= 0), g[0:8], 0.0),
                    )
                ]
                for j in range(1, SLOTS // 8):
                    parts.append(jnp.where(mine[j], g[8 * j : 8 * j + 8], 0.0))
                g = jnp.concatenate(parts, axis=0)
                value = total * par_ref[4:5, lanes]
                for k in range(TAPS):
                    taken = mixed[SLOTS * k : SLOTS * (k + 1), lanes_of(i)]
                    value = value + taken * par_ref[k : k + 1, lanes]
                    acc[k, :, lanes] += jnp.sum((taken * g).reshape(SLOTS // 8, 8, 128), axis=0)
                acc[4, :, lanes] += jnp.sum((total * g).reshape(SLOTS // 8, 8, 128), axis=0)
                acc[5, :, lanes] += jnp.where(sub8 == 0, value[0:8], 0.0)
                top = carry_o[:, lanes] + jnp.where(sub8 < LEAD, 0.0, value[0:8])
                out32[r % 2, c, pl.ds(start, 8), :] = top
                out32[r % 2, c, pl.ds(start + 8, OWN - 8), :] = value[8:OWN]
                carry_o[:, lanes] = jnp.where(m < tiles - 1, value[OWN:], 0.0)

    def finish(r):
        for c in range(chunks):
            outb[r, :, lanes_of(c)] = out32[r % 2, c, PAD : PAD + half, :].astype(BF16)
        copy_out(r).start()

    spread_pair(0)
    build(0, 0)
    build(0, 1)

    def second_loop(i, _):
        for side in range(2):
            r, m = place(2 * i - 1 + side)

            @pl.when((m == 0) & (i > 0))
            def _():
                finish(r - 1)

        spread_pair(i + 1)
        for side in range(2):
            apply(i, side)
            build(i + 1, side)
        return 0

    lax.fori_loop(0, pairs - 1, second_loop, 0)
    apply(pairs - 1, 0)
    apply(pairs - 1, 1)
    for r in range(rows):
        if r * tiles > 2 * (pairs - 2):
            finish(r - 1)
    finish(rows - 1)
    for k in range(TAPS + 2):
        grad_ref[k : k + 1, :] = jnp.sum(acc[k], axis=0, keepdims=True)
    for r in range(rows):
        copy_out(r).wait()


def backward_kernel(shapes, r, base_ref, len_ref, mat, g32, par_ref, *refs):
    gin_hbm, dc, ginb, sems = refs[-4:]
    rows, length, half, features, tiles = shapes
    chunks = features // 128
    wide = 2 if chunks % 2 == 0 else 1
    base = base_ref[0]
    sub8 = iota((8, 128), 0)
    ends = ends_of(len_ref, r)

    for m in range(tiles):
        tile = r * tiles + m
        streamed = jnp.concatenate([mat[tile, :, 0:WINDOW].T, mat[tile, :, WINDOW:].T], axis=1)
        at = 2 * OWN * m
        for w in range(chunks // wide):
            held = []
            for i in range(wide):
                lanes = lanes_of(wide * w + i)
                scorer = par_ref[5:6, lanes]
                scorer_high = scorer.astype(BF16).astype(F32)
                g = g32[r, wide * w + i, OWN * m + 8 : OWN * m + 8 + SLOTS, :]
                top = jnp.where(
                    sub8 == 0, scorer_high, jnp.where(sub8 == 1, scorer - scorer_high, g[0:8])
                )
                held.append(jnp.concatenate([top, g[8:]], axis=0).astype(BF16))
            held = jnp.concatenate(held, axis=1)
            part = lax.dot_general(
                streamed,
                jnp.concatenate([held, held], axis=0),
                (((1,), (0,)), ((), ())),
                preferred_element_type=F32,
            )
            for i in range(wide):
                c = wide * w + i
                before = dc[c, at : at + PAD, :] if m > 0 else 0.0
                dc[c, at : at + PAD, :] = before + part[0:PAD, lanes_of(i)]
                dc[c, at + PAD : at + WINDOW, :] = part[PAD:, lanes_of(i)]

    def taps_at(at, masked):
        keeps = []
        if masked:
            for j in range(4):
                position = base + at + 8 * j + sub8
                remain = end_of(position, ends) - position
                keeps.append([remain > k for k in range(TAPS)])
        for c in range(chunks):
            parts = []
            for j in range(4):
                value = par_ref[0:1, lanes_of(c)] * dc[c, pl.ds(at + PAD + 8 * j, 8), :]
                for k in range(1, TAPS):
                    shifted = dc[c, pl.ds(at + PAD + 8 * j + k, 8), :]
                    if masked:
                        shifted = jnp.where(keeps[j][k], shifted, 0.0)
                    value = value + par_ref[k : k + 1, lanes_of(c)] * shifted
                parts.append(value)
            ginb[pl.ds(at, 32), lanes_of(c)] = jnp.concatenate(parts, axis=0).astype(BF16)

    def taps(i, _):
        at = pl.multiple_of(i * 32, 32)
        reach = [(end > base + at) & (end <= base + at + 32 + TAPS - 2) for end in ends]
        crosses = functools.reduce(jnp.logical_or, reach)

        @pl.when(crosses)
        def _():
            taps_at(at, True)

        @pl.when(jnp.logical_not(crosses))
        def _():
            taps_at(at, False)

        return 0

    pieces = 2
    copies = []
    for piece in range(pieces):
        size = length // pieces
        lax.fori_loop(piece * size // 32, (piece + 1) * size // 32, taps, 0)
        copies.append(
            pltpu.make_async_copy(
                ginb.at[pl.ds(piece * size, size), :],
                gin_hbm.at[r, pl.ds(piece * size, size), :],
                sems.at[piece],
            )
        )
        copies[-1].start()
    for copy in copies:
        copy.wait()


SMEM = pl.BlockSpec(memory_space=pltpu.SMEM)
VMEM = pl.BlockSpec(memory_space=pltpu.VMEM)
HBM = pl.BlockSpec(memory_space=pltpu.HBM)


def sizes_of(length, half):
    tiles = -(-(half + 3 + LEAD) // OWN)
    x_rows = 2 * OWN * (tiles - 1) + WINDOW
    g_rows = -(-(OWN * (tiles - 1) + 8 + SLOTS) // 16) * 16
    return tiles, x_rows, g_rows


def packed(base, inputs, cotangent):
    rows, _, features = inputs.shape
    part = jax.ShapeDtypeStruct((rows, PAD, features), BF16)
    return pl.pallas_call(
        pack_kernel,
        out_shape=(part, part),
        in_specs=[SMEM, HBM, HBM],
        out_specs=(VMEM, VMEM),
        scratch_shapes=[pltpu.VMEM((rows, PAD, features), BF16)] * 4 + [pltpu.SemaphoreType.DMA((4,))],
        compiler_params=pltpu.CompilerParams(vmem_limit_bytes=PACK_LIMIT),
    )(base, inputs, cotangent)


def forward(base, lengths, inputs, cotangent, near, far, params):
    rows, half, features = cotangent.shape
    length = 2 * half
    chunks = features // 128
    tiles, x_rows, g_rows = sizes_of(length, half)
    count = rows * tiles
    shapes = (rows, length, half, features, tiles)
    return pl.pallas_call(
        functools.partial(forward_kernel, shapes),
        out_shape=(
            jax.ShapeDtypeStruct((rows, half, features), BF16),
            jax.ShapeDtypeStruct((count, SLOTS, 2 * WINDOW), BF16),
            jax.ShapeDtypeStruct((rows, chunks, g_rows, 128), F32),
            jax.ShapeDtypeStruct((TAPS + 2, features), F32),
        ),
        in_specs=[SMEM, SMEM, VMEM, VMEM, VMEM, VMEM, VMEM],
        out_specs=(HBM, VMEM, VMEM, VMEM),
        scratch_shapes=[
            pltpu.VMEM((rows, x_rows, features), BF16),
            pltpu.VMEM((4, chunks, WINDOW + 8, 128), F32),
            pltpu.VMEM((chunks, 2 * WINDOW, 128), BF16),
            pltpu.VMEM((chunks, 2 * WINDOW, 128), BF16),
            pltpu.VMEM((chunks, 2 * WINDOW, 128), BF16),
            pltpu.VMEM((chunks, 2 * WINDOW, 128), BF16),
            pltpu.VMEM((count + rows, chunks, 32, 128), BF16),
            pltpu.VMEM((2 * SLOTS, WINDOW), F32),
            pltpu.VMEM((2 * SLOTS, WINDOW), F32),
            pltpu.VMEM((2, count // 2, 8, 128), F32),
            pltpu.VMEM((2, count, 8, 128), F32),
            pltpu.VMEM((count // 2, 8, 128), F32),
            pltpu.VMEM((TAPS * SLOTS, 2 * WINDOW), BF16),
            pltpu.VMEM((TAPS * SLOTS, 2 * WINDOW), BF16),
            pltpu.VMEM((2, SLOTS, 128), F32),
            pltpu.VMEM((2, 2, 8, 128), F32),
            pltpu.VMEM((2, chunks, g_rows, 128), F32),
            pltpu.VMEM((rows, half, features), BF16),
            pltpu.VMEM((8, features), F32),
            pltpu.VMEM((TAPS + 2, 8, features), F32),
            pltpu.SemaphoreType.DMA((rows,)),
        ],
        compiler_params=pltpu.CompilerParams(vmem_limit_bytes=40 * 1024 * 1024),
        cost_estimate=pl.CostEstimate(
            flops=2 * count * SLOTS * WINDOW * features * 12,
            bytes_accessed=8 * inputs.size,
            transcendentals=0,
        ),
    )(base, lengths, inputs, cotangent, near, far, params)


def backward(r, base, lengths, shape, matrices, padded, params, grown):
    rows, length, features = shape
    half = length // 2
    chunks = features // 128
    tiles, x_rows, g_rows = sizes_of(length, half)
    shapes = (rows, length, half, features, tiles)
    operands = [base, lengths, matrices, padded, params]
    in_specs = [SMEM, SMEM, VMEM, VMEM, VMEM]
    if grown is not None:
        operands.append(grown)
        in_specs.append(HBM)
    return pl.pallas_call(
        functools.partial(backward_kernel, shapes, r),
        out_shape=jax.ShapeDtypeStruct(shape, BF16),
        in_specs=in_specs,
        out_specs=HBM,
        scratch_shapes=[
            pltpu.VMEM((chunks, x_rows, 128), F32),
            pltpu.VMEM((length, features), BF16),
            pltpu.SemaphoreType.DMA((2,)),
        ],
        input_output_aliases={} if grown is None else {5: 0},
        compiler_params=pltpu.CompilerParams(vmem_limit_bytes=12 * 1024 * 1024),
        cost_estimate=pl.CostEstimate(
            flops=2 * tiles * SLOTS * WINDOW * features * 4,
            bytes_accessed=4 * length * features,
            transcendentals=0,
        ),
    )(*operands)


def adam_update(grads, weights, first_old, second_old):
    first_new = beta_one * first_old + (1.0 - beta_one) * grads
    second_new = beta_two * second_old + (1.0 - beta_two) * grads * grads
    first_hat = first_new / (1.0 - beta_one**STEP)
    second_hat = second_new / (1.0 - beta_two**STEP)
    updated = weights - learn_rate * (
        first_hat / (jnp.sqrt(second_hat) + adam_eps) + decay_rate * weights
    )
    return (updated, first_new, second_new)


def rounds_of(axes):
    rounds = []
    for axis in axes:
        count = lax.axis_size(axis)
        step = 1
        while step < count:
            rounds.append((axis, [(i, i ^ step) for i in range(count)]))
            step *= 2
    return rounds


def per_device(inputs, lengths, params, first_moment, second_moment, cotangent):
    rows_here, length_here, _ = inputs.shape
    base = (lax.axis_index("group") * length_here).astype(jnp.int32).reshape(1)
    near, far = packed(base, inputs, cotangent)
    far = lax.ppermute(far, "group", pairs_of("group", 1))
    near = lax.ppermute(near, "group", pairs_of("group", 0))
    output, matrices, padded, grad_params = forward(
        base, lengths, inputs, cotangent, near, far, params
    )

    def backward_row(row, matrices, grown):
        return backward(row, base, lengths, inputs.shape, matrices, padded, params, grown)

    grad_inputs = None
    row = 0
    for axis, exchange in rounds_of(("group", "rows")):
        received = lax.ppermute(grad_params, axis, exchange)
        if row < rows_here:
            matrices, grad_params = lax.optimization_barrier((matrices, grad_params))
            grad_inputs = backward_row(row, matrices, grad_inputs)
            row += 1
            received, grad_inputs = lax.optimization_barrier((received, grad_inputs))
        grad_params = grad_params + received
    while row < rows_here:
        grad_inputs = backward_row(row, matrices, grad_inputs)
        row += 1
    grad_norm = jnp.sqrt(jnp.sum(grad_params * grad_params))
    clip_scale = jnp.minimum(1.0, clip_limit / (grad_norm + 1e-06))
    new_params, new_first, new_second = adam_update(
        grad_params * clip_scale, params, first_moment, second_moment
    )
    return (output, grad_inputs, grad_norm, new_params, new_first, new_second)


def solution(mesh):
    in_specs = (P("rows", "group", None), P("rows", None), P(), P(), P(), P("rows", "group", None))
    out_specs = (P("rows", "group", None), P("rows", "group", None), P(), P(), P(), P())
    return jax.shard_map(
        per_device, mesh=mesh, in_specs=in_specs, out_specs=out_specs, check_vma=False
    )
```

```python
import functools

import jax
import jax.numpy as jnp
from jax import lax
from jax.experimental import pallas as pl
from jax.experimental.pallas import tpu as pltpu
from jax.sharding import PartitionSpec as P

STEP = 10


beta_one = 0.9
beta_two = 0.999
learn_rate = 0.2
decay_rate = 0.01
adam_eps = 1e-08
clip_limit = 1.0

TAPS = 4
SLOTS = 64
PACK_LIMIT = 50 * 1024 * 1024
OWN = 56
LEAD = 4
WINDOW = 128
PAD = 16
F32 = jnp.float32
BF16 = jnp.bfloat16


def pairs_of(axis, first):
    count = lax.axis_size(axis)
    pairs = [(i, i + 1) for i in range(first, count - 1, 2)]
    return pairs + [(j, i) for i, j in pairs]


def rotate_rows(x, amount):
    for bit in (1, 2, 4):
        x = jnp.where((amount & bit) != 0, pltpu.roll(x, 8 - bit, x.ndim - 2), x)
    return x


def split(x):
    high = x.astype(BF16)
    return high, (x - high.astype(F32)).astype(BF16)


def iota(shape, dim):
    return lax.broadcasted_iota(jnp.int32, shape, dim)


def ends_of(len_ref, r):
    one = len_ref[r, 0]
    two = one + len_ref[r, 1]
    three = two + len_ref[r, 2]
    return one, two, three, three + len_ref[r, 3]


def begin_of(at, ends):
    begin = jnp.where(at >= ends[0], ends[0], 0)
    begin = jnp.where(at >= ends[1], ends[1], begin)
    return jnp.where(at >= ends[2], ends[2], begin)


def end_of(at, ends):
    end = jnp.where(at >= ends[0], ends[1], ends[0])
    end = jnp.where(at >= ends[1], ends[2], end)
    return jnp.where(at >= ends[2], ends[3], end)


def lanes_of(c):
    return slice(128 * c, 128 * c + 128)


def pack_kernel(base_ref, x_hbm, g_hbm, near_ref, far_ref, x_first, x_last, g_first, g_last, sems):
    rows, length, features = x_hbm.shape
    half = g_hbm.shape[1]
    copies = [
        pltpu.make_async_copy(x_hbm.at[:, pl.ds(length - PAD, PAD), :], x_last, sems.at[0]),
        pltpu.make_async_copy(g_hbm.at[:, pl.ds(half - PAD, PAD), :], g_last, sems.at[1]),
        pltpu.make_async_copy(x_hbm.at[:, pl.ds(0, PAD), :], x_first, sems.at[2]),
        pltpu.make_async_copy(g_hbm.at[:, pl.ds(0, PAD), :], g_first, sems.at[3]),
    ]
    for copy in copies:
        copy.start()
    even = (base_ref[0] // length) % 2 == 0
    sub = iota((PAD, features), 0)
    for copy in copies:
        copy.wait()
    for r in range(rows):
        moved = pltpu.roll(g_last[r].astype(F32), 2, 0)
        last = jnp.where(sub < 2, moved, x_last[r].astype(F32))
        moved = pltpu.roll(g_first[r].astype(F32), PAD - 3, 0)
        first = jnp.where(sub < PAD - 3, x_first[r].astype(F32), moved)
        near_ref[r] = jnp.where(even, last, first).astype(BF16)
        far_ref[r] = jnp.where(even, first, last).astype(BF16)


def convolve_block(base, ends, par_ref, load, at, place_high, place_low):
    chunks = par_ref.shape[1] // 128
    sub8 = iota((8, 128), 0)
    keeps = []
    for j in range(2):
        position = base - PAD + at + 8 * j + sub8
        offset = position - begin_of(position, ends)
        keeps.append([offset >= k for k in range(TAPS)])
    for c in range(chunks):
        lanes = lanes_of(c)
        parts = []
        for j in range(2):
            value = par_ref[4:5, lanes] + par_ref[0:1, lanes] * load(c, 8 * j)
            for k in range(1, TAPS):
                shifted = jnp.where(keeps[j][k], load(c, 8 * j - k), 0.0)
                value = value + par_ref[k : k + 1, lanes] * shifted
            parts.append(value)
        high, low = split(jnp.concatenate(parts, axis=0))
        place_high(c, high)
        place_low(c, low)


def conv_kernel(shapes, base_ref, len_ref, x_ref, par_ref, conv_ref, xf):
    rows, length, half, features, tiles = shapes
    chunks = features // 128
    base = base_ref[0]
    blocks = 2 * OWN // 16
    for c in range(chunks):
        xf[c, 0 : 8 + PAD, :] = jnp.zeros((8 + PAD, 128), F32)
        rest = xf.shape[1] - 8 - PAD - length
        xf[c, 8 + PAD + length :, :] = jnp.zeros((rest, 128), F32)

    def one_row(r, _):
        ends = ends_of(len_ref, r)

        def widen(i, _):
            at = pl.multiple_of(i * 32, 32)
            for c in range(chunks):
                xf[c, pl.ds(at + 8 + PAD, 32), :] = x_ref[r, pl.ds(at, 32), lanes_of(c)].astype(F32)
            return 0

        lax.fori_loop(0, length // 32, widen, 0)

        def one_tile(m, _):
            tile = r * tiles + m
            before = jnp.maximum(tile - 1, 0)
            for b in range(blocks):
                at = pl.multiple_of(2 * OWN * m + 16 * b, 16)

                def put(first):
                    def store(c, value):
                        conv_ref[tile, c, first + 16 * b : first + 16 * b + 16, :] = value
                        if b == 0:
                            conv_ref[before, c, first + WINDOW - 16 : first + WINDOW, :] = value

                    return store

                convolve_block(
                    base,
                    ends,
                    par_ref,
                    lambda c, shift: xf[c, pl.ds(at + 8 + shift, 8), :],
                    at,
                    put(0),
                    put(WINDOW),
                )
            return 0

        lax.fori_loop(0, tiles, one_tile, 0)
        return 0

    lax.fori_loop(0, rows, one_row, 0)
    for r in range(rows):
        last = r * tiles + tiles - 1
        for c in range(chunks):
            for first in (0, WINDOW):
                conv_ref[last, c, first + WINDOW - 16 : first + WINDOW, :] = jnp.zeros((16, 128), BF16)


def forward_kernel(
    shapes,
    base_ref,
    len_ref,
    x_ref,
    g_ref,
    conv_ref,
    near_ref,
    far_ref,
    par_ref,
    out_hbm,
    mat,
    g32,
    grad_ref,
    xb,
    xf,
    edge,
    comp,
    cs,
    es,
    fac_a,
    fac_b,
    tot,
    rows_e_ref,
    out32,
    outb,
    carry_o,
    acc,
    sems,
):
    rows, length, half, features, tiles = shapes
    pairs = rows * tiles // 2
    chunks = features // 128
    base = base_ref[0]

    def copy_out(r):
        return pltpu.make_async_copy(outb.at[r], out_hbm.at[r], sems.at[r])

    sub8 = iota((8, 128), 0)
    lane8 = iota((8, 128), 1)
    slot8 = lane8 % SLOTS
    left = lane8 < SLOTS
    delta = sub8 - 3
    first = [2 * slot8 - 3 - (2 * p + lane8 // SLOTS) for p in range(2)]
    group_of = [(f + ((sub8 - f) & 7)) >> 3 for f in first]
    turn = [f & 7 for f in first]
    first_e = 2 * slot8 - 3
    group_of_e = (first_e + ((sub8 - first_e) & 7)) >> 3
    turn_e = first_e & 7

    def place(pair, side):
        r, m = 2 * (pair // tiles) + side, pair % tiles
        return r, m, r * tiles + m

    def tile_start(m):
        return base + 2 * OWN * m - PAD

    acc[...] = jnp.zeros_like(acc)
    carry_o[...] = jnp.zeros_like(carry_o)

    subd = iota((8, features), 0)
    even = (base // length) % 2 == 0
    for r in range(rows):
        near = near_ref[r].astype(F32)
        far = far_ref[r].astype(F32)
        up = jnp.where(even, far, near)
        down = jnp.where(even, near, far)
        xb[r, 0:PAD, :] = up.astype(BF16)
        xb[r, PAD + length : 2 * PAD + length, :] = down.astype(BF16)
        rest = xb.shape[1] - 2 * PAD - length
        if rest > 0:
            xb[r, 2 * PAD + length :, :] = jnp.zeros((rest, features), BF16)
        xb[r, PAD : PAD + length, :] = x_ref[r]
        before = jnp.where(subd >= 6, pltpu.roll(up[0:8], 6, 0), 0.0)
        after = jnp.where(subd < 3, pltpu.roll(down[8:16], 3, 0), 0.0)
        rest = g32.shape[2] - PAD - half - 8
        for c in range(chunks):
            g32[r, c, 8:16, :] = before[:, lanes_of(c)]
            g32[r, c, PAD : PAD + half, :] = g_ref[r, :, lanes_of(c)].astype(F32)
            g32[r, c, PAD + half : PAD + half + 8, :] = after[:, lanes_of(c)]
            g32[r, c, PAD + half + 8 :, :] = jnp.zeros((rest, 128), F32)
        for c in range(chunks):
            lanes = lanes_of(c)
            xf[c, 0:8, :] = jnp.zeros((8, 128), F32)
            xf[c, 8:24, :] = up[:, lanes]
            xf[c, 24:40, :] = x_ref[r, 0:16, lanes].astype(F32)
            xf[c, 40:56, :] = x_ref[r, length - 16 : length, lanes].astype(F32)
            xf[c, 56:72, :] = down[:, lanes]
        ends = ends_of(len_ref, r)
        for at, where, slot in ((0, 8, 0), (PAD, 24, 16), (PAD + length, 56, 32)):

            def put(first):
                def store(c, value):
                    edge[r, c, first : first + 16, :] = value

                return store

            convolve_block(
                base,
                ends,
                par_ref,
                lambda c, shift: xf[c, where + shift : where + shift + 8, :],
                at,
                put(slot),
                put(48 + slot),
            )

    scorer_high = [par_ref[5:6, lanes_of(c)].astype(BF16).astype(F32) for c in range(chunks)]
    scorer_low = [par_ref[5:6, lanes_of(c)] - scorer_high[c] for c in range(chunks)]

    def held_rows(r, m, c):
        tile = r * tiles + m
        parts = []
        for first, own in ((0, 0), (WINDOW, 48)):
            begin = 0
            if m == 0:
                parts.append(edge[r, c, own : own + 32, :])
                begin = 32
            if m == tiles - 1:
                end = PAD + length - 2 * OWN * m
                parts.append(conv_ref[tile, c, first + begin : first + end, :])
                parts.append(edge[r, c, own + 32 : own + 48, :])
                begin = end + 16
            if begin < WINDOW:
                parts.append(conv_ref[tile, c, first + begin : first + WINDOW, :])
        return jnp.concatenate(parts, axis=0)

    for pair in range(pairs):
        dots, scores = [], []
        for side in range(2):
            r, m, _ = place(pair, side)
            start = OWN * m + 8
            streamed, held = [], []
            for c in range(chunks):
                g = g32[r, c, start : start + SLOTS, :]
                top = jnp.where(sub8 == 0, scorer_high[c], jnp.where(sub8 == 1, scorer_low[c], g[0:8]))
                streamed.append(jnp.concatenate([top, g[8:]], axis=0).astype(BF16))
                held.append(held_rows(r, m, c))
            product = lax.dot_general(
                jnp.concatenate(streamed, axis=1),
                jnp.concatenate(held, axis=1),
                (((1,), (1,)), ((), ())),
                preferred_element_type=F32,
            )
            product = product[:, :WINDOW] + product[:, WINDOW:]
            dots.append(product)
            scores.append(jnp.broadcast_to(product[0:1] + product[1:2], (SLOTS, WINDOW)))
        dots = jnp.concatenate(dots, axis=0).T
        scores = jnp.concatenate(scores, axis=0).T
        banded = jnp.zeros((8, 128), F32)
        scored = jnp.zeros((8, 128), F32)
        for v in range(WINDOW // 8):
            here = group_of_e == v
            banded = jnp.where(here, dots[8 * v : 8 * v + 8], banded)
            scored = jnp.where(here, scores[8 * v : 8 * v + 8], scored)
        comp[0, pair] = banded
        comp[1, pair] = scored

    ends = [ends_of(len_ref, r) for r in range(rows)]
    for pair in range(pairs):
        both = [place(pair, side) for side in range(2)]
        dots = rotate_rows(comp[0, pair], turn_e)
        scores = rotate_rows(comp[1, pair], turn_e)
        coef = jnp.zeros((8, 128), F32)
        coef_e = jnp.zeros((8, 128), F32)
        for p in range(2):
            at = tile_start(both[0][1]) + 2 * slot8 + p
            begin = [begin_of(at, ends[r]) for r, _, _ in both]
            end = [end_of(at, ends[r]) for r, _, _ in both]
            offset = jnp.maximum(at - jnp.where(left, begin[0], begin[1]), 0)
            remain = jnp.where(left, end[0], end[1]) - at
            masks, inverses, logits, grads = [], [], [], []
            for b in range(1, TAPS + 1):
                if b == 3:
                    thirds = ((offset.astype(F32) + 0.5) * (1.0 / 3.0)).astype(jnp.int32)
                    within = offset - 3 * thirds
                else:
                    within = offset & (b - 1)
                upper = jnp.minimum(b - within, remain)
                mask = (delta >= p - within) & (delta < p + upper)
                inverse = 1.0 / jnp.maximum(within + upper, 1).astype(F32)
                masks.append(mask)
                inverses.append(inverse)
                logits.append(jnp.sum(jnp.where(mask, scores, 0.0), axis=0, keepdims=True) * inverse)
                grads.append(
                    jnp.sum(jnp.where(mask, dots, 0.0), axis=0, keepdims=True) * (0.5 * inverse)
                )
            largest = functools.reduce(jnp.maximum, logits)
            powers = [jnp.exp(logit - largest) for logit in logits]
            scale = 1.0 / sum(powers)
            shares = [power * scale for power in powers]
            mean = sum(share * grad for share, grad in zip(shares, grads))
            for mask, inverse, share, grad in zip(masks, inverses, shares, grads):
                coef = coef + jnp.where(mask, (0.5 * share) * inverse, 0.0)
                coef_e = coef_e + jnp.where(mask, share * (grad - mean) * inverse, 0.0)
        owned = (slot8 >= LEAD) & (slot8 < LEAD + OWN)
        coef = jnp.where(owned, coef, 0.0)
        coef_e = jnp.where(owned, coef_e, 0.0)
        es[pair] = rotate_rows(coef_e, (8 - turn_e) & 7)
        swapped = pltpu.roll(coef, SLOTS, 1)
        for side, (r, m, tile) in enumerate(both):
            at = tile_start(m) + 2 * slot8 + delta
            offset = at - begin_of(at, ends[r])
            alone = jnp.where(left, coef, swapped) if side == 0 else jnp.where(left, swapped, coef)
            for p in range(2):
                kept = jnp.where((offset >= 2 * p + lane8 // SLOTS) & (at >= 0), alone, 0.0)
                cs[p, tile] = rotate_rows(kept, (8 - turn[p]) & 7)

    slots_down = iota((SLOTS, 128), 0)
    wide = 2 if chunks % 2 == 0 else 1
    factors = (fac_a, fac_b)

    def spread_pair(pair):
        spread = jnp.concatenate(
            [jnp.where(group_of_e == v, es[pair], 0.0) for v in range(WINDOW // 8)], axis=0
        ).T
        for side in range(2):
            _, m, _ = place(pair, side)
            from_row = OWN * m - 8
            part = spread[SLOTS * side : SLOTS * side + SLOTS]
            here = (from_row + slots_down >= 0) & (from_row + slots_down < half)
            own_e = jnp.sum(jnp.where(here, part, 0.0), axis=0, keepdims=True)
            all_e = jnp.sum(part, axis=0, keepdims=True)
            rows_e_ref[side, 0] = jnp.broadcast_to(own_e, (8, 128))
            rows_e_ref[side, 1] = jnp.broadcast_to(all_e, (8, 128))

    def build(pair, side):
        r, m, tile = place(pair, side)
        own_e = rows_e_ref[side, 0]
        all_e = rows_e_ref[side, 1]
        at = tile_start(m) + lane8
        offset = at - begin_of(at, ends_of(len_ref, r))
        bands = []
        for p in range(2):
            bands.append(
                jnp.concatenate(
                    [jnp.where(group_of[p] == v, cs[p, tile], 0.0) for v in range(WINDOW // 8)], axis=0
                ).T
            )
        for k in range(TAPS):
            row_k = jnp.where((offset >= k) & (at >= 0), own_e, 0.0)
            if k > 0:
                row_k = pltpu.roll(row_k, 128 - k, 1)
            matrix = bands[k // 2][SLOTS * (k % 2) : SLOTS * (k % 2) + SLOTS]
            if k == 0:
                back = jnp.concatenate([jnp.where(sub8 < 2, all_e, matrix[0:8]), matrix[8:]], axis=0)
                high, low = split(back)
                mat[tile, :, 0:WINDOW] = high
                mat[tile, :, WINDOW:] = low
            matrix = jnp.concatenate([jnp.where(sub8 == 0, row_k, matrix[0:8]), matrix[8:]], axis=0)
            if k == 0:
                total = jnp.sum(matrix, axis=1, keepdims=True)
                tot[side] = jnp.broadcast_to(total, (SLOTS, 128))
            high, low = split(matrix)
            factors[side][SLOTS * k : SLOTS * (k + 1), 0:WINDOW] = high
            factors[side][SLOTS * k : SLOTS * (k + 1), WINDOW:] = low

    def apply(pair, side):
        r, m, _ = place(pair, side)
        start = pl.multiple_of(OWN * m + 8, 8)
        window = pl.multiple_of(2 * OWN * m, 16)
        factor = factors[side][...]
        total = tot[side]
        from_row = OWN * m - 8
        mine = [from_row + 8 * i + sub8 < half for i in range(SLOTS // 8)]
        for w in range(chunks // wide):
            x = xb[r, pl.ds(window, WINDOW), 128 * wide * w : 128 * wide * (w + 1)]
            mixed = lax.dot_general(
                factor,
                jnp.concatenate([x, x], axis=0),
                (((1,), (0,)), ((), ())),
                preferred_element_type=F32,
            )
            for i in range(wide):
                c = wide * w + i
                lanes = lanes_of(c)
                g = g32[r, c, pl.ds(start, SLOTS), :]
                parts = [
                    jnp.where(
                        sub8 == 0,
                        par_ref[5:6, lanes],
                        jnp.where((sub8 >= LEAD) & (from_row + sub8 >= 0), g[0:8], 0.0),
                    )
                ]
                for j in range(1, SLOTS // 8):
                    parts.append(jnp.where(mine[j], g[8 * j : 8 * j + 8], 0.0))
                g = jnp.concatenate(parts, axis=0)
                value = total * par_ref[4:5, lanes]
                for k in range(TAPS):
                    taken = mixed[SLOTS * k : SLOTS * (k + 1), lanes_of(i)]
                    value = value + taken * par_ref[k : k + 1, lanes]
                    acc[k, :, lanes] += jnp.sum((taken * g).reshape(SLOTS // 8, 8, 128), axis=0)
                acc[4, :, lanes] += jnp.sum((total * g).reshape(SLOTS // 8, 8, 128), axis=0)
                acc[5, :, lanes] += jnp.where(sub8 == 0, value[0:8], 0.0)
                top = carry_o[side, :, lanes] + jnp.where(sub8 < LEAD, 0.0, value[0:8])
                out32[side, c, pl.ds(start, 8), :] = top
                out32[side, c, pl.ds(start + 8, OWN - 8), :] = value[8:OWN]
                carry_o[side, :, lanes] = jnp.where(m < tiles - 1, value[OWN:], 0.0)

    def finish(r, side):
        for c in range(chunks):
            outb[r, :, lanes_of(c)] = out32[side, c, PAD : PAD + half, :].astype(BF16)
        copy_out(r).start()

    spread_pair(0)
    build(0, 0)
    build(0, 1)

    def second_loop(i, _):
        @pl.when((i % tiles == 0) & (i > 0))
        def _():
            for side in range(2):
                finish(2 * (i // tiles) - 2 + side, side)

        spread_pair(i + 1)
        for side in range(2):
            apply(i, side)
            build(i + 1, side)
        return 0

    lax.fori_loop(0, pairs - 1, second_loop, 0)
    apply(pairs - 1, 0)
    apply(pairs - 1, 1)
    for side in range(2):
        finish(rows - 2 + side, side)
    for k in range(TAPS + 2):
        grad_ref[k : k + 1, :] = jnp.sum(acc[k], axis=0, keepdims=True)
    for r in range(rows):
        copy_out(r).wait()


def backward_kernel(shapes, r, base_ref, len_ref, mat, g32, par_ref, *refs):
    gin_hbm, dc, ginb, sems = refs[-4:]
    rows, length, half, features, tiles = shapes
    chunks = features // 128
    wide = 2 if chunks % 2 == 0 else 1
    base = base_ref[0]
    sub8 = iota((8, 128), 0)
    ends = ends_of(len_ref, r)

    for m in range(tiles):
        tile = r * tiles + m
        streamed = jnp.concatenate([mat[tile, :, 0:WINDOW].T, mat[tile, :, WINDOW:].T], axis=1)
        at = 2 * OWN * m
        for w in range(chunks // wide):
            held = []
            for i in range(wide):
                lanes = lanes_of(wide * w + i)
                scorer = par_ref[5:6, lanes]
                scorer_high = scorer.astype(BF16).astype(F32)
                g = g32[r, wide * w + i, OWN * m + 8 : OWN * m + 8 + SLOTS, :]
                top = jnp.where(
                    sub8 == 0, scorer_high, jnp.where(sub8 == 1, scorer - scorer_high, g[0:8])
                )
                held.append(jnp.concatenate([top, g[8:]], axis=0).astype(BF16))
            held = jnp.concatenate(held, axis=1)
            part = lax.dot_general(
                streamed,
                jnp.concatenate([held, held], axis=0),
                (((1,), (0,)), ((), ())),
                preferred_element_type=F32,
            )
            for i in range(wide):
                c = wide * w + i
                before = dc[c, at : at + PAD, :] if m > 0 else 0.0
                dc[c, at : at + PAD, :] = before + part[0:PAD, lanes_of(i)]
                dc[c, at + PAD : at + WINDOW, :] = part[PAD:, lanes_of(i)]

    def taps_at(at, masked):
        keeps = []
        if masked:
            for j in range(4):
                position = base + at + 8 * j + sub8
                remain = end_of(position, ends) - position
                keeps.append([remain > k for k in range(TAPS)])
        for c in range(chunks):
            parts = []
            for j in range(4):
                value = par_ref[0:1, lanes_of(c)] * dc[c, pl.ds(at + PAD + 8 * j, 8), :]
                for k in range(1, TAPS):
                    shifted = dc[c, pl.ds(at + PAD + 8 * j + k, 8), :]
                    if masked:
                        shifted = jnp.where(keeps[j][k], shifted, 0.0)
                    value = value + par_ref[k : k + 1, lanes_of(c)] * shifted
                parts.append(value)
            ginb[pl.ds(at, 32), lanes_of(c)] = jnp.concatenate(parts, axis=0).astype(BF16)

    def taps(i, _):
        at = pl.multiple_of(i * 32, 32)
        reach = [(end > base + at) & (end <= base + at + 32 + TAPS - 2) for end in ends]
        crosses = functools.reduce(jnp.logical_or, reach)

        @pl.when(crosses)
        def _():
            taps_at(at, True)

        @pl.when(jnp.logical_not(crosses))
        def _():
            taps_at(at, False)

        return 0

    pieces = 2
    copies = []
    for piece in range(pieces):
        size = length // pieces
        lax.fori_loop(piece * size // 32, (piece + 1) * size // 32, taps, 0)
        copies.append(
            pltpu.make_async_copy(
                ginb.at[pl.ds(piece * size, size), :],
                gin_hbm.at[r, pl.ds(piece * size, size), :],
                sems.at[piece],
            )
        )
        copies[-1].start()
    for copy in copies:
        copy.wait()


SMEM = pl.BlockSpec(memory_space=pltpu.SMEM)
VMEM = pl.BlockSpec(memory_space=pltpu.VMEM)
HBM = pl.BlockSpec(memory_space=pltpu.HBM)


def sizes_of(length, half):
    tiles = -(-(half + 3 + LEAD) // OWN)
    x_rows = 2 * OWN * (tiles - 1) + WINDOW
    g_rows = -(-(OWN * (tiles - 1) + 8 + SLOTS) // 16) * 16
    return tiles, x_rows, g_rows


def packed(base, inputs, cotangent):
    rows, _, features = inputs.shape
    part = jax.ShapeDtypeStruct((rows, PAD, features), BF16)
    return pl.pallas_call(
        pack_kernel,
        out_shape=(part, part),
        in_specs=[SMEM, HBM, HBM],
        out_specs=(VMEM, VMEM),
        scratch_shapes=[pltpu.VMEM((rows, PAD, features), BF16)] * 4 + [pltpu.SemaphoreType.DMA((4,))],
        compiler_params=pltpu.CompilerParams(vmem_limit_bytes=PACK_LIMIT),
    )(base, inputs, cotangent)


def convolved(base, lengths, inputs, params):
    rows, length, features = inputs.shape
    half = length // 2
    chunks = features // 128
    tiles, x_rows, _ = sizes_of(length, half)
    shapes = (rows, length, half, features, tiles)
    return pl.pallas_call(
        functools.partial(conv_kernel, shapes),
        out_shape=jax.ShapeDtypeStruct((rows * tiles, chunks, 2 * WINDOW, 128), BF16),
        in_specs=[SMEM, SMEM, VMEM, VMEM],
        out_specs=VMEM,
        scratch_shapes=[pltpu.VMEM((chunks, 8 + x_rows, 128), F32)],
        compiler_params=pltpu.CompilerParams(vmem_limit_bytes=24 * 1024 * 1024),
        cost_estimate=pl.CostEstimate(
            flops=24 * inputs.size, bytes_accessed=8 * inputs.size, transcendentals=0
        ),
    )(base, lengths, inputs, params)


def forward(base, lengths, inputs, cotangent, conv, near, far, params):
    rows, half, features = cotangent.shape
    length = 2 * half
    chunks = features // 128
    tiles, x_rows, g_rows = sizes_of(length, half)
    count = rows * tiles
    shapes = (rows, length, half, features, tiles)
    return pl.pallas_call(
        functools.partial(forward_kernel, shapes),
        out_shape=(
            jax.ShapeDtypeStruct((rows, half, features), BF16),
            jax.ShapeDtypeStruct((count, SLOTS, 2 * WINDOW), BF16),
            jax.ShapeDtypeStruct((rows, chunks, g_rows, 128), F32),
            jax.ShapeDtypeStruct((TAPS + 2, features), F32),
        ),
        in_specs=[SMEM, SMEM, VMEM, VMEM, VMEM, VMEM, VMEM, VMEM],
        out_specs=(HBM, VMEM, VMEM, VMEM),
        scratch_shapes=[
            pltpu.VMEM((rows, x_rows, features), BF16),
            pltpu.VMEM((chunks, 72, 128), F32),
            pltpu.VMEM((rows, chunks, 96, 128), BF16),
            pltpu.VMEM((2, count // 2, 8, 128), F32),
            pltpu.VMEM((2, count, 8, 128), F32),
            pltpu.VMEM((count // 2, 8, 128), F32),
            pltpu.VMEM((TAPS * SLOTS, 2 * WINDOW), BF16),
            pltpu.VMEM((TAPS * SLOTS, 2 * WINDOW), BF16),
            pltpu.VMEM((2, SLOTS, 128), F32),
            pltpu.VMEM((2, 2, 8, 128), F32),
            pltpu.VMEM((2, chunks, g_rows, 128), F32),
            pltpu.VMEM((rows, half, features), BF16),
            pltpu.VMEM((2, 8, features), F32),
            pltpu.VMEM((TAPS + 2, 8, features), F32),
            pltpu.SemaphoreType.DMA((rows,)),
        ],
        compiler_params=pltpu.CompilerParams(vmem_limit_bytes=28 * 1024 * 1024),
        cost_estimate=pl.CostEstimate(
            flops=2 * count * SLOTS * WINDOW * features * 12,
            bytes_accessed=8 * inputs.size,
            transcendentals=0,
        ),
    )(base, lengths, inputs, cotangent, conv, near, far, params)


def backward(r, base, lengths, shape, matrices, padded, params, grown):
    rows, length, features = shape
    half = length // 2
    chunks = features // 128
    tiles, x_rows, g_rows = sizes_of(length, half)
    shapes = (rows, length, half, features, tiles)
    operands = [base, lengths, matrices, padded, params]
    in_specs = [SMEM, SMEM, VMEM, VMEM, VMEM]
    if grown is not None:
        operands.append(grown)
        in_specs.append(HBM)
    return pl.pallas_call(
        functools.partial(backward_kernel, shapes, r),
        out_shape=jax.ShapeDtypeStruct(shape, BF16),
        in_specs=in_specs,
        out_specs=HBM,
        scratch_shapes=[
            pltpu.VMEM((chunks, x_rows, 128), F32),
            pltpu.VMEM((length, features), BF16),
            pltpu.SemaphoreType.DMA((2,)),
        ],
        input_output_aliases={} if grown is None else {5: 0},
        compiler_params=pltpu.CompilerParams(vmem_limit_bytes=12 * 1024 * 1024),
        cost_estimate=pl.CostEstimate(
            flops=2 * tiles * SLOTS * WINDOW * features * 4,
            bytes_accessed=4 * length * features,
            transcendentals=0,
        ),
    )(*operands)


def adam_update(grads, weights, first_old, second_old):
    first_new = beta_one * first_old + (1.0 - beta_one) * grads
    second_new = beta_two * second_old + (1.0 - beta_two) * grads * grads
    first_hat = first_new / (1.0 - beta_one**STEP)
    second_hat = second_new / (1.0 - beta_two**STEP)
    updated = weights - learn_rate * (
        first_hat / (jnp.sqrt(second_hat) + adam_eps) + decay_rate * weights
    )
    return (updated, first_new, second_new)


def rounds_of(axes):
    rounds = []
    for axis in axes:
        count = lax.axis_size(axis)
        step = 1
        while step < count:
            rounds.append((axis, [(i, i ^ step) for i in range(count)]))
            step *= 2
    return rounds


def per_device(inputs, lengths, params, first_moment, second_moment, cotangent):
    rows_here, length_here, _ = inputs.shape
    base = (lax.axis_index("group") * length_here).astype(jnp.int32).reshape(1)
    near, far = packed(base, inputs, cotangent)
    far = lax.ppermute(far, "group", pairs_of("group", 1))
    near = lax.ppermute(near, "group", pairs_of("group", 0))
    conv = convolved(base, lengths, inputs, params)
    output, matrices, padded, grad_params = forward(
        base, lengths, inputs, cotangent, conv, near, far, params
    )

    def backward_row(row, matrices, grown):
        return backward(row, base, lengths, inputs.shape, matrices, padded, params, grown)

    grad_inputs = None
    row = 0
    for axis, exchange in rounds_of(("group", "rows")):
        received = lax.ppermute(grad_params, axis, exchange)
        if row < rows_here:
            matrices, grad_params = lax.optimization_barrier((matrices, grad_params))
            grad_inputs = backward_row(row, matrices, grad_inputs)
            row += 1
            received, grad_inputs = lax.optimization_barrier((received, grad_inputs))
        grad_params = grad_params + received
    while row < rows_here:
        grad_inputs = backward_row(row, matrices, grad_inputs)
        row += 1
    grad_norm = jnp.sqrt(jnp.sum(grad_params * grad_params))
    clip_scale = jnp.minimum(1.0, clip_limit / (grad_norm + 1e-06))
    new_params, new_first, new_second = adam_update(
        grad_params * clip_scale, params, first_moment, second_moment
    )
    return (output, grad_inputs, grad_norm, new_params, new_first, new_second)


def solution(mesh):
    in_specs = (P("rows", "group", None), P("rows", None), P(), P(), P(), P("rows", "group", None))
    out_specs = (P("rows", "group", None), P("rows", "group", None), P(), P(), P(), P())
    return jax.shard_map(
        per_device, mesh=mesh, in_specs=in_specs, out_specs=out_specs, check_vma=False
    )
```

```python
import functools

import jax
import jax.numpy as jnp
from jax import lax
from jax.experimental import pallas as pl
from jax.experimental.pallas import tpu as pltpu
from jax.sharding import PartitionSpec as P

STEP = 10


beta_one = 0.9
beta_two = 0.999
learn_rate = 0.2
decay_rate = 0.01
adam_eps = 1e-08
clip_limit = 1.0

TAPS = 4
SLOTS = 64
PACK_LIMIT = 53 * 1024 * 1024
OWN = 56
LEAD = 4
WINDOW = 128
PAD = 16
F32 = jnp.float32
BF16 = jnp.bfloat16


def pairs_of(axis, first):
    count = lax.axis_size(axis)
    pairs = [(i, i + 1) for i in range(first, count - 1, 2)]
    return pairs + [(j, i) for i, j in pairs]


def rotate_rows(x, amount):
    for bit in (1, 2, 4):
        x = jnp.where((amount & bit) != 0, pltpu.roll(x, 8 - bit, x.ndim - 2), x)
    return x


def split(x):
    high = x.astype(BF16)
    return high, (x - high.astype(F32)).astype(BF16)


def iota(shape, dim):
    return lax.broadcasted_iota(jnp.int32, shape, dim)


def ends_of(len_ref, r):
    one = len_ref[r, 0]
    two = one + len_ref[r, 1]
    three = two + len_ref[r, 2]
    return one, two, three, three + len_ref[r, 3]


def begin_of(at, ends):
    begin = jnp.where(at >= ends[0], ends[0], 0)
    begin = jnp.where(at >= ends[1], ends[1], begin)
    return jnp.where(at >= ends[2], ends[2], begin)


def end_of(at, ends):
    end = jnp.where(at >= ends[0], ends[1], ends[0])
    end = jnp.where(at >= ends[1], ends[2], end)
    return jnp.where(at >= ends[2], ends[3], end)


def lanes_of(c):
    return slice(128 * c, 128 * c + 128)


def pack_kernel(base_ref, x_hbm, g_hbm, near_ref, far_ref, x_first, x_last, g_first, g_last, sems):
    rows, length, features = x_hbm.shape
    half = g_hbm.shape[1]
    copies = [
        pltpu.make_async_copy(x_hbm.at[:, pl.ds(length - PAD, PAD), :], x_last, sems.at[0]),
        pltpu.make_async_copy(g_hbm.at[:, pl.ds(half - PAD, PAD), :], g_last, sems.at[1]),
        pltpu.make_async_copy(x_hbm.at[:, pl.ds(0, PAD), :], x_first, sems.at[2]),
        pltpu.make_async_copy(g_hbm.at[:, pl.ds(0, PAD), :], g_first, sems.at[3]),
    ]
    for copy in copies:
        copy.start()
    even = (base_ref[0] // length) % 2 == 0
    sub = iota((PAD, features), 0)
    for copy in copies:
        copy.wait()
    for r in range(rows):
        moved = pltpu.roll(g_last[r].astype(F32), 2, 0)
        last = jnp.where(sub < 2, moved, x_last[r].astype(F32))
        moved = pltpu.roll(g_first[r].astype(F32), PAD - 3, 0)
        first = jnp.where(sub < PAD - 3, x_first[r].astype(F32), moved)
        near_ref[r] = jnp.where(even, last, first).astype(BF16)
        far_ref[r] = jnp.where(even, first, last).astype(BF16)


def convolve_block(base, ends, par_ref, load, at, place_high, place_low, masked=True):
    chunks = par_ref.shape[1] // 128
    sub8 = iota((8, 128), 0)
    keeps = []
    for j in range(2 if masked else 0):
        position = base - PAD + at + 8 * j + sub8
        offset = position - begin_of(position, ends)
        keeps.append([offset >= k for k in range(TAPS)])
    for c in range(chunks):
        lanes = lanes_of(c)
        parts = []
        for j in range(2):
            value = par_ref[4:5, lanes] + par_ref[0:1, lanes] * load(c, 8 * j)
            for k in range(1, TAPS):
                shifted = load(c, 8 * j - k)
                if masked:
                    shifted = jnp.where(keeps[j][k], shifted, 0.0)
                value = value + par_ref[k : k + 1, lanes] * shifted
            parts.append(value)
        high, low = split(jnp.concatenate(parts, axis=0))
        place_high(c, high)
        place_low(c, low)


def conv_kernel(shapes, base_ref, len_ref, x_ref, par_ref, high_ref, low_ref, xf):
    rows, length, half, features, tiles = shapes
    chunks = features // 128
    base = base_ref[0]
    step = 64
    for c in range(chunks):
        xf[c, 0:8, :] = jnp.zeros((8, 128), F32)
    rest = high_ref.shape[2] - PAD - length
    for r in range(rows):
        for c in range(chunks):
            for ref in (high_ref, low_ref):
                ref[r, c, 0:PAD, :] = jnp.zeros((PAD, 128), BF16)
                ref[r, c, PAD + length :, :] = jnp.zeros((rest, 128), BF16)

    def one_row(r, _):
        ends = ends_of(len_ref, r)

        def widen(i, _):
            at = pl.multiple_of(i * step, step)
            for c in range(chunks):
                xf[c, pl.ds(at + 8, step), :] = x_ref[r, pl.ds(at, step), lanes_of(c)].astype(F32)
            return 0

        lax.fori_loop(0, length // step, widen, 0)

        def blocks(at, masked):
            for b in range(step // 16):

                def put(ref):
                    def store(c, value):
                        ref[r, c, pl.ds(at + PAD + 16 * b, 16), :] = value

                    return store

                convolve_block(
                    base,
                    ends,
                    par_ref,
                    lambda c, shift: xf[c, pl.ds(at + 8 + 16 * b + shift, 8), :],
                    at + PAD + 16 * b,
                    put(high_ref),
                    put(low_ref),
                    masked,
                )

        def one_step(i, _):
            at = pl.multiple_of(i * step, step)
            reach = [(end > base + at - TAPS + 1) & (end < base + at + step) for end in ends]
            starts = functools.reduce(jnp.logical_or, reach)

            @pl.when(starts)
            def _():
                blocks(at, True)

            @pl.when(jnp.logical_not(starts))
            def _():
                blocks(at, False)

            return 0

        lax.fori_loop(0, length // step, one_step, 0)
        return 0

    lax.fori_loop(0, rows, one_row, 0)


def forward_kernel(
    shapes,
    base_ref,
    len_ref,
    x_ref,
    g_ref,
    high_ref,
    low_ref,
    near_ref,
    far_ref,
    par_ref,
    out_hbm,
    mat,
    g32,
    grad_ref,
    xb,
    xf,
    edge,
    comp,
    cs,
    es,
    fac_a,
    fac_b,
    tot,
    rows_e_ref,
    out32,
    outb,
    carry_o,
    acc,
    sems,
):
    rows, length, half, features, tiles = shapes
    pairs = rows * tiles // 2
    chunks = features // 128
    base = base_ref[0]

    def copy_out(r):
        return pltpu.make_async_copy(outb.at[r], out_hbm.at[r], sems.at[r])

    sub8 = iota((8, 128), 0)
    lane8 = iota((8, 128), 1)
    slot8 = lane8 % SLOTS
    left = lane8 < SLOTS
    delta = sub8 - 3
    first = [2 * slot8 - 3 - (2 * p + lane8 // SLOTS) for p in range(2)]
    group_of = [(f + ((sub8 - f) & 7)) >> 3 for f in first]
    turn = [f & 7 for f in first]
    first_e = 2 * slot8 - 3
    group_of_e = (first_e + ((sub8 - first_e) & 7)) >> 3
    turn_e = first_e & 7

    def place(pair, side):
        r, m = 2 * (pair // tiles) + side, pair % tiles
        return r, m, r * tiles + m

    def tile_start(m):
        return base + 2 * OWN * m - PAD

    acc[...] = jnp.zeros_like(acc)
    carry_o[...] = jnp.zeros_like(carry_o)

    subd = iota((8, features), 0)
    even = (base // length) % 2 == 0
    for r in range(rows):
        near = near_ref[r].astype(F32)
        far = far_ref[r].astype(F32)
        up = jnp.where(even, far, near)
        down = jnp.where(even, near, far)
        xb[r, 0:PAD, :] = up.astype(BF16)
        xb[r, PAD + length : 2 * PAD + length, :] = down.astype(BF16)
        rest = xb.shape[1] - 2 * PAD - length
        if rest > 0:
            xb[r, 2 * PAD + length :, :] = jnp.zeros((rest, features), BF16)
        xb[r, PAD : PAD + length, :] = x_ref[r]
        before = jnp.where(subd >= 6, pltpu.roll(up[0:8], 6, 0), 0.0)
        after = jnp.where(subd < 3, pltpu.roll(down[8:16], 3, 0), 0.0)
        rest = g32.shape[2] - PAD - half - 8
        for c in range(chunks):
            g32[r, c, 8:16, :] = before[:, lanes_of(c)]
            g32[r, c, PAD : PAD + half, :] = g_ref[r, :, lanes_of(c)].astype(F32)
            g32[r, c, PAD + half : PAD + half + 8, :] = after[:, lanes_of(c)]
            g32[r, c, PAD + half + 8 :, :] = jnp.zeros((rest, 128), F32)
        for c in range(chunks):
            lanes = lanes_of(c)
            xf[c, 0:8, :] = jnp.zeros((8, 128), F32)
            xf[c, 8:24, :] = up[:, lanes]
            xf[c, 24:40, :] = x_ref[r, 0:16, lanes].astype(F32)
            xf[c, 40:56, :] = x_ref[r, length - 16 : length, lanes].astype(F32)
            xf[c, 56:72, :] = down[:, lanes]
        ends = ends_of(len_ref, r)
        for at, where, slot in ((0, 8, 0), (PAD, 24, 16), (PAD + length, 56, 32)):

            def put(first):
                def store(c, value):
                    edge[r, c, first : first + 16, :] = value

                return store

            convolve_block(
                base,
                ends,
                par_ref,
                lambda c, shift: xf[c, where + shift : where + shift + 8, :],
                at,
                put(slot),
                put(48 + slot),
            )

    scorer_high = [par_ref[5:6, lanes_of(c)].astype(BF16).astype(F32) for c in range(chunks)]
    scorer_low = [par_ref[5:6, lanes_of(c)] - scorer_high[c] for c in range(chunks)]

    def held_rows(r, m, c):
        parts = []
        at = 2 * OWN * m
        for ref, own in ((high_ref, 0), (low_ref, 48)):
            begin = 0
            if m == 0:
                parts.append(edge[r, c, own : own + 32, :])
                begin = 32
            if m == tiles - 1:
                end = PAD + length - at
                parts.append(ref[r, c, at + begin : at + end, :])
                parts.append(edge[r, c, own + 32 : own + 48, :])
                begin = end + 16
            if begin < WINDOW:
                parts.append(ref[r, c, at + begin : at + WINDOW, :])
        return jnp.concatenate(parts, axis=0)

    for pair in range(pairs):
        dots, scores = [], []
        for side in range(2):
            r, m, _ = place(pair, side)
            start = OWN * m + 8
            streamed, held = [], []
            for c in range(chunks):
                g = g32[r, c, start : start + SLOTS, :]
                top = jnp.where(sub8 == 0, scorer_high[c], jnp.where(sub8 == 1, scorer_low[c], g[0:8]))
                streamed.append(jnp.concatenate([top, g[8:]], axis=0).astype(BF16))
                held.append(held_rows(r, m, c))
            product = lax.dot_general(
                jnp.concatenate(streamed, axis=1),
                jnp.concatenate(held, axis=1),
                (((1,), (1,)), ((), ())),
                preferred_element_type=F32,
            )
            product = product[:, :WINDOW] + product[:, WINDOW:]
            dots.append(product)
            scores.append(jnp.broadcast_to(product[0:1] + product[1:2], (SLOTS, WINDOW)))
        dots = jnp.concatenate(dots, axis=0).T
        scores = jnp.concatenate(scores, axis=0).T
        banded = jnp.zeros((8, 128), F32)
        scored = jnp.zeros((8, 128), F32)
        for v in range(WINDOW // 8):
            here = group_of_e == v
            banded = jnp.where(here, dots[8 * v : 8 * v + 8], banded)
            scored = jnp.where(here, scores[8 * v : 8 * v + 8], scored)
        comp[0, pair] = banded
        comp[1, pair] = scored

    ends = [ends_of(len_ref, r) for r in range(rows)]
    for pair in range(pairs):
        both = [place(pair, side) for side in range(2)]
        dots = rotate_rows(comp[0, pair], turn_e)
        scores = rotate_rows(comp[1, pair], turn_e)
        coef = jnp.zeros((8, 128), F32)
        coef_e = jnp.zeros((8, 128), F32)
        for p in range(2):
            at = tile_start(both[0][1]) + 2 * slot8 + p
            begin = [begin_of(at, ends[r]) for r, _, _ in both]
            end = [end_of(at, ends[r]) for r, _, _ in both]
            offset = jnp.maximum(at - jnp.where(left, begin[0], begin[1]), 0)
            remain = jnp.where(left, end[0], end[1]) - at
            masks, inverses, logits, grads = [], [], [], []
            for b in range(1, TAPS + 1):
                if b == 3:
                    thirds = ((offset.astype(F32) + 0.5) * (1.0 / 3.0)).astype(jnp.int32)
                    within = offset - 3 * thirds
                else:
                    within = offset & (b - 1)
                upper = jnp.minimum(b - within, remain)
                mask = (delta >= p - within) & (delta < p + upper)
                inverse = 1.0 / jnp.maximum(within + upper, 1).astype(F32)
                masks.append(mask)
                inverses.append(inverse)
                logits.append(jnp.sum(jnp.where(mask, scores, 0.0), axis=0, keepdims=True) * inverse)
                grads.append(
                    jnp.sum(jnp.where(mask, dots, 0.0), axis=0, keepdims=True) * (0.5 * inverse)
                )
            largest = functools.reduce(jnp.maximum, logits)
            powers = [jnp.exp(logit - largest) for logit in logits]
            scale = 1.0 / sum(powers)
            shares = [power * scale for power in powers]
            mean = sum(share * grad for share, grad in zip(shares, grads))
            for mask, inverse, share, grad in zip(masks, inverses, shares, grads):
                coef = coef + jnp.where(mask, (0.5 * share) * inverse, 0.0)
                coef_e = coef_e + jnp.where(mask, share * (grad - mean) * inverse, 0.0)
        owned = (slot8 >= LEAD) & (slot8 < LEAD + OWN)
        coef = jnp.where(owned, coef, 0.0)
        coef_e = jnp.where(owned, coef_e, 0.0)
        es[pair] = rotate_rows(coef_e, (8 - turn_e) & 7)
        swapped = pltpu.roll(coef, SLOTS, 1)
        for side, (r, m, tile) in enumerate(both):
            at = tile_start(m) + 2 * slot8 + delta
            offset = at - begin_of(at, ends[r])
            alone = jnp.where(left, coef, swapped) if side == 0 else jnp.where(left, swapped, coef)
            for p in range(2):
                kept = jnp.where((offset >= 2 * p + lane8 // SLOTS) & (at >= 0), alone, 0.0)
                cs[p, tile] = rotate_rows(kept, (8 - turn[p]) & 7)

    slots_down = iota((SLOTS, 128), 0)
    wide = 2 if chunks % 2 == 0 else 1
    factors = (fac_a, fac_b)

    def spread_pair(pair):
        spread = jnp.concatenate(
            [jnp.where(group_of_e == v, es[pair], 0.0) for v in range(WINDOW // 8)], axis=0
        ).T
        for side in range(2):
            _, m, _ = place(pair, side)
            from_row = OWN * m - 8
            part = spread[SLOTS * side : SLOTS * side + SLOTS]
            here = (from_row + slots_down >= 0) & (from_row + slots_down < half)
            own_e = jnp.sum(jnp.where(here, part, 0.0), axis=0, keepdims=True)
            all_e = jnp.sum(part, axis=0, keepdims=True)
            rows_e_ref[side, 0] = jnp.broadcast_to(own_e, (8, 128))
            rows_e_ref[side, 1] = jnp.broadcast_to(all_e, (8, 128))

    def build(pair, side):
        r, m, tile = place(pair, side)
        own_e = rows_e_ref[side, 0]
        all_e = rows_e_ref[side, 1]
        at = tile_start(m) + lane8
        offset = at - begin_of(at, ends_of(len_ref, r))
        bands = []
        for p in range(2):
            bands.append(
                jnp.concatenate(
                    [jnp.where(group_of[p] == v, cs[p, tile], 0.0) for v in range(WINDOW // 8)], axis=0
                ).T
            )
        for k in range(TAPS):
            row_k = jnp.where((offset >= k) & (at >= 0), own_e, 0.0)
            if k > 0:
                row_k = pltpu.roll(row_k, 128 - k, 1)
            matrix = bands[k // 2][SLOTS * (k % 2) : SLOTS * (k % 2) + SLOTS]
            if k == 0:
                back = jnp.concatenate([jnp.where(sub8 < 2, all_e, matrix[0:8]), matrix[8:]], axis=0)
                high, low = split(back)
                mat[tile, :, 0:WINDOW] = high
                mat[tile, :, WINDOW:] = low
            matrix = jnp.concatenate([jnp.where(sub8 == 0, row_k, matrix[0:8]), matrix[8:]], axis=0)
            if k == 0:
                total = jnp.sum(matrix, axis=1, keepdims=True)
                tot[side] = jnp.broadcast_to(total, (SLOTS, 128))
            high, low = split(matrix)
            factors[side][SLOTS * k : SLOTS * (k + 1), 0:WINDOW] = high
            factors[side][SLOTS * k : SLOTS * (k + 1), WINDOW:] = low

    def apply(pair, side):
        r, m, _ = place(pair, side)
        start = pl.multiple_of(OWN * m + 8, 8)
        window = pl.multiple_of(2 * OWN * m, 16)
        factor = factors[side][...]
        total = tot[side]
        from_row = OWN * m - 8
        mine = [from_row + 8 * i + sub8 < half for i in range(SLOTS // 8)]
        for w in range(chunks // wide):
            x = xb[r, pl.ds(window, WINDOW), 128 * wide * w : 128 * wide * (w + 1)]
            mixed = lax.dot_general(
                factor,
                jnp.concatenate([x, x], axis=0),
                (((1,), (0,)), ((), ())),
                preferred_element_type=F32,
            )
            for i in range(wide):
                c = wide * w + i
                lanes = lanes_of(c)
                g = g32[r, c, pl.ds(start, SLOTS), :]
                parts = [
                    jnp.where(
                        sub8 == 0,
                        par_ref[5:6, lanes],
                        jnp.where((sub8 >= LEAD) & (from_row + sub8 >= 0), g[0:8], 0.0),
                    )
                ]
                for j in range(1, SLOTS // 8):
                    parts.append(jnp.where(mine[j], g[8 * j : 8 * j + 8], 0.0))
                g = jnp.concatenate(parts, axis=0)
                value = total * par_ref[4:5, lanes]
                for k in range(TAPS):
                    taken = mixed[SLOTS * k : SLOTS * (k + 1), lanes_of(i)]
                    value = value + taken * par_ref[k : k + 1, lanes]
                    acc[k, :, lanes] += jnp.sum((taken * g).reshape(SLOTS // 8, 8, 128), axis=0)
                acc[4, :, lanes] += jnp.sum((total * g).reshape(SLOTS // 8, 8, 128), axis=0)
                acc[5, :, lanes] += jnp.where(sub8 == 0, value[0:8], 0.0)
                top = carry_o[side, :, lanes] + jnp.where(sub8 < LEAD, 0.0, value[0:8])
                out32[side, c, pl.ds(start, 8), :] = top
                out32[side, c, pl.ds(start + 8, OWN - 8), :] = value[8:OWN]
                carry_o[side, :, lanes] = jnp.where(m < tiles - 1, value[OWN:], 0.0)

    def finish(r, side):
        for c in range(chunks):
            outb[r, :, lanes_of(c)] = out32[side, c, PAD : PAD + half, :].astype(BF16)
        copy_out(r).start()

    spread_pair(0)
    build(0, 0)
    build(0, 1)

    def second_loop(i, _):
        @pl.when((i % tiles == 0) & (i > 0))
        def _():
            for side in range(2):
                finish(2 * (i // tiles) - 2 + side, side)

        spread_pair(i + 1)
        for side in range(2):
            apply(i, side)
            build(i + 1, side)
        return 0

    lax.fori_loop(0, pairs - 1, second_loop, 0)
    apply(pairs - 1, 0)
    apply(pairs - 1, 1)
    for side in range(2):
        finish(rows - 2 + side, side)
    for k in range(TAPS + 2):
        grad_ref[k : k + 1, :] = jnp.sum(acc[k], axis=0, keepdims=True)
    for r in range(rows):
        copy_out(r).wait()


def backward_kernel(shapes, r, base_ref, len_ref, mat, g32, par_ref, *refs):
    gin_hbm, dc, ginb, sems = refs[-4:]
    rows, length, half, features, tiles = shapes
    chunks = features // 128
    wide = 2 if chunks % 2 == 0 else 1
    base = base_ref[0]
    sub8 = iota((8, 128), 0)
    ends = ends_of(len_ref, r)

    for m in range(tiles):
        tile = r * tiles + m
        streamed = jnp.concatenate([mat[tile, :, 0:WINDOW].T, mat[tile, :, WINDOW:].T], axis=1)
        at = 2 * OWN * m
        for w in range(chunks // wide):
            held = []
            for i in range(wide):
                lanes = lanes_of(wide * w + i)
                scorer = par_ref[5:6, lanes]
                scorer_high = scorer.astype(BF16).astype(F32)
                g = g32[r, wide * w + i, OWN * m + 8 : OWN * m + 8 + SLOTS, :]
                top = jnp.where(
                    sub8 == 0, scorer_high, jnp.where(sub8 == 1, scorer - scorer_high, g[0:8])
                )
                held.append(jnp.concatenate([top, g[8:]], axis=0).astype(BF16))
            held = jnp.concatenate(held, axis=1)
            part = lax.dot_general(
                streamed,
                jnp.concatenate([held, held], axis=0),
                (((1,), (0,)), ((), ())),
                preferred_element_type=F32,
            )
            for i in range(wide):
                c = wide * w + i
                before = dc[c, at : at + PAD, :] if m > 0 else 0.0
                dc[c, at : at + PAD, :] = before + part[0:PAD, lanes_of(i)]
                dc[c, at + PAD : at + WINDOW, :] = part[PAD:, lanes_of(i)]

    def taps_at(at, masked):
        keeps = []
        if masked:
            for j in range(4):
                position = base + at + 8 * j + sub8
                remain = end_of(position, ends) - position
                keeps.append([remain > k for k in range(TAPS)])
        for c in range(chunks):
            parts = []
            for j in range(4):
                value = par_ref[0:1, lanes_of(c)] * dc[c, pl.ds(at + PAD + 8 * j, 8), :]
                for k in range(1, TAPS):
                    shifted = dc[c, pl.ds(at + PAD + 8 * j + k, 8), :]
                    if masked:
                        shifted = jnp.where(keeps[j][k], shifted, 0.0)
                    value = value + par_ref[k : k + 1, lanes_of(c)] * shifted
                parts.append(value)
            ginb[pl.ds(at, 32), lanes_of(c)] = jnp.concatenate(parts, axis=0).astype(BF16)

    def taps(i, _):
        at = pl.multiple_of(i * 32, 32)
        reach = [(end > base + at) & (end <= base + at + 32 + TAPS - 2) for end in ends]
        crosses = functools.reduce(jnp.logical_or, reach)

        @pl.when(crosses)
        def _():
            taps_at(at, True)

        @pl.when(jnp.logical_not(crosses))
        def _():
            taps_at(at, False)

        return 0

    pieces = 2
    copies = []
    for piece in range(pieces):
        size = length // pieces
        lax.fori_loop(piece * size // 32, (piece + 1) * size // 32, taps, 0)
        copies.append(
            pltpu.make_async_copy(
                ginb.at[pl.ds(piece * size, size), :],
                gin_hbm.at[r, pl.ds(piece * size, size), :],
                sems.at[piece],
            )
        )
        copies[-1].start()
    for copy in copies:
        copy.wait()


SMEM = pl.BlockSpec(memory_space=pltpu.SMEM)
VMEM = pl.BlockSpec(memory_space=pltpu.VMEM)
HBM = pl.BlockSpec(memory_space=pltpu.HBM)


def sizes_of(length, half):
    tiles = -(-(half + 3 + LEAD) // OWN)
    x_rows = 2 * OWN * (tiles - 1) + WINDOW
    g_rows = -(-(OWN * (tiles - 1) + 8 + SLOTS) // 16) * 16
    return tiles, x_rows, g_rows


def packed(base, inputs, cotangent):
    rows, _, features = inputs.shape
    part = jax.ShapeDtypeStruct((rows, PAD, features), BF16)
    return pl.pallas_call(
        pack_kernel,
        out_shape=(part, part),
        in_specs=[SMEM, HBM, HBM],
        out_specs=(VMEM, VMEM),
        scratch_shapes=[pltpu.VMEM((rows, PAD, features), BF16)] * 4 + [pltpu.SemaphoreType.DMA((4,))],
        compiler_params=pltpu.CompilerParams(vmem_limit_bytes=PACK_LIMIT),
    )(base, inputs, cotangent)


def convolved(base, lengths, inputs, params):
    rows, length, features = inputs.shape
    half = length // 2
    chunks = features // 128
    tiles, x_rows, _ = sizes_of(length, half)
    shapes = (rows, length, half, features, tiles)
    part = jax.ShapeDtypeStruct((rows, chunks, x_rows, 128), BF16)
    return pl.pallas_call(
        functools.partial(conv_kernel, shapes),
        out_shape=(part, part),
        in_specs=[SMEM, SMEM, VMEM, VMEM],
        out_specs=(VMEM, VMEM),
        scratch_shapes=[pltpu.VMEM((chunks, 8 + length, 128), F32)],
        compiler_params=pltpu.CompilerParams(vmem_limit_bytes=24 * 1024 * 1024),
        cost_estimate=pl.CostEstimate(
            flops=24 * inputs.size, bytes_accessed=8 * inputs.size, transcendentals=0
        ),
    )(base, lengths, inputs, params)


def forward(base, lengths, inputs, cotangent, high, low, near, far, params):
    rows, half, features = cotangent.shape
    length = 2 * half
    chunks = features // 128
    tiles, x_rows, g_rows = sizes_of(length, half)
    count = rows * tiles
    shapes = (rows, length, half, features, tiles)
    return pl.pallas_call(
        functools.partial(forward_kernel, shapes),
        out_shape=(
            jax.ShapeDtypeStruct((rows, half, features), BF16),
            jax.ShapeDtypeStruct((count, SLOTS, 2 * WINDOW), BF16),
            jax.ShapeDtypeStruct((rows, chunks, g_rows, 128), F32),
            jax.ShapeDtypeStruct((TAPS + 2, features), F32),
        ),
        in_specs=[SMEM, SMEM, VMEM, VMEM, VMEM, VMEM, VMEM, VMEM, VMEM],
        out_specs=(HBM, VMEM, VMEM, VMEM),
        scratch_shapes=[
            pltpu.VMEM((rows, x_rows, features), BF16),
            pltpu.VMEM((chunks, 72, 128), F32),
            pltpu.VMEM((rows, chunks, 96, 128), BF16),
            pltpu.VMEM((2, count // 2, 8, 128), F32),
            pltpu.VMEM((2, count, 8, 128), F32),
            pltpu.VMEM((count // 2, 8, 128), F32),
            pltpu.VMEM((TAPS * SLOTS, 2 * WINDOW), BF16),
            pltpu.VMEM((TAPS * SLOTS, 2 * WINDOW), BF16),
            pltpu.VMEM((2, SLOTS, 128), F32),
            pltpu.VMEM((2, 2, 8, 128), F32),
            pltpu.VMEM((2, chunks, g_rows, 128), F32),
            pltpu.VMEM((rows, half, features), BF16),
            pltpu.VMEM((2, 8, features), F32),
            pltpu.VMEM((TAPS + 2, 8, features), F32),
            pltpu.SemaphoreType.DMA((rows,)),
        ],
        compiler_params=pltpu.CompilerParams(vmem_limit_bytes=28 * 1024 * 1024),
        cost_estimate=pl.CostEstimate(
            flops=2 * count * SLOTS * WINDOW * features * 12,
            bytes_accessed=8 * inputs.size,
            transcendentals=0,
        ),
    )(base, lengths, inputs, cotangent, high, low, near, far, params)


def backward(r, base, lengths, shape, matrices, padded, params, grown):
    rows, length, features = shape
    half = length // 2
    chunks = features // 128
    tiles, x_rows, g_rows = sizes_of(length, half)
    shapes = (rows, length, half, features, tiles)
    operands = [base, lengths, matrices, padded, params]
    in_specs = [SMEM, SMEM, VMEM, VMEM, VMEM]
    if grown is not None:
        operands.append(grown)
        in_specs.append(HBM)
    return pl.pallas_call(
        functools.partial(backward_kernel, shapes, r),
        out_shape=jax.ShapeDtypeStruct(shape, BF16),
        in_specs=in_specs,
        out_specs=HBM,
        scratch_shapes=[
            pltpu.VMEM((chunks, x_rows, 128), F32),
            pltpu.VMEM((length, features), BF16),
            pltpu.SemaphoreType.DMA((2,)),
        ],
        input_output_aliases={} if grown is None else {5: 0},
        compiler_params=pltpu.CompilerParams(vmem_limit_bytes=12 * 1024 * 1024),
        cost_estimate=pl.CostEstimate(
            flops=2 * tiles * SLOTS * WINDOW * features * 4,
            bytes_accessed=4 * length * features,
            transcendentals=0,
        ),
    )(*operands)


def update_kernel(
    grad_ref, other_ref, par_ref, first_ref, second_ref, norm_ref, new_ref, new_first_ref, new_second_ref
):
    grads = grad_ref[...] + other_ref[...]
    norm = jnp.sqrt(jnp.sum(grads * grads, keepdims=True))
    norm_ref[...] = norm
    grads = grads * jnp.minimum(1.0, clip_limit / (norm + 1e-06))
    weights = par_ref[...]
    first_new = beta_one * first_ref[...] + (1.0 - beta_one) * grads
    second_new = beta_two * second_ref[...] + (1.0 - beta_two) * grads * grads
    first_hat = first_new / (1.0 - beta_one**STEP)
    second_hat = second_new / (1.0 - beta_two**STEP)
    new_ref[...] = weights - learn_rate * (
        first_hat / (jnp.sqrt(second_hat) + adam_eps) + decay_rate * weights
    )
    new_first_ref[...] = first_new
    new_second_ref[...] = second_new


def update(grads, other, weights, first_old, second_old):
    like = jax.ShapeDtypeStruct(weights.shape, F32)
    return pl.pallas_call(
        update_kernel,
        out_shape=(jax.ShapeDtypeStruct((1, 1), F32), like, like, like),
        in_specs=[VMEM] * 5,
        out_specs=(VMEM,) * 4,
        compiler_params=pltpu.CompilerParams(vmem_limit_bytes=4 * 1024 * 1024),
    )(grads, other, weights, first_old, second_old)


def rounds_of(axes):
    rounds = []
    for axis in axes:
        count = lax.axis_size(axis)
        step = 1
        while step < count:
            rounds.append((axis, [(i, i ^ step) for i in range(count)]))
            step *= 2
    return rounds


def per_device(inputs, lengths, params, first_moment, second_moment, cotangent):
    rows_here, length_here, _ = inputs.shape
    base = (lax.axis_index("group") * length_here).astype(jnp.int32).reshape(1)
    near, far = packed(base, inputs, cotangent)
    far = lax.ppermute(far, "group", pairs_of("group", 1))
    near = lax.ppermute(near, "group", pairs_of("group", 0))
    high, low = convolved(base, lengths, inputs, params)
    output, matrices, padded, grad_params = forward(
        base, lengths, inputs, cotangent, high, low, near, far, params
    )

    def backward_row(row, matrices, grown):
        return backward(row, base, lengths, inputs.shape, matrices, padded, params, grown)

    grad_inputs = None
    row = 0
    received = jnp.zeros_like(grad_params)
    for axis, exchange in rounds_of(("group", "rows")):
        if row > 0:
            grad_params = grad_params + received
        received = lax.ppermute(grad_params, axis, exchange)
        if row < rows_here:
            matrices, grad_params = lax.optimization_barrier((matrices, grad_params))
            grad_inputs = backward_row(row, matrices, grad_inputs)
            received, grad_inputs = lax.optimization_barrier((received, grad_inputs))
        row += 1
    while row < rows_here:
        grad_inputs = backward_row(row, matrices, grad_inputs)
        row += 1
    grad_norm, new_params, new_first, new_second = update(
        grad_params, received, params, first_moment, second_moment
    )
    grad_norm = grad_norm.reshape(())
    return (output, grad_inputs, grad_norm, new_params, new_first, new_second)


def solution(mesh):
    in_specs = (P("rows", "group", None), P("rows", None), P(), P(), P(), P("rows", "group", None))
    out_specs = (P("rows", "group", None), P("rows", "group", None), P(), P(), P(), P())
    return jax.shard_map(
        per_device, mesh=mesh, in_specs=in_specs, out_specs=out_specs, check_vma=False
    )
```

```python
import functools

import jax
import jax.numpy as jnp
from jax import lax
from jax.experimental import pallas as pl
from jax.experimental.pallas import tpu as pltpu
from jax.sharding import PartitionSpec as P

STEP = 10


beta_one = 0.9
beta_two = 0.999
learn_rate = 0.2
decay_rate = 0.01
adam_eps = 1e-08
clip_limit = 1.0

TAPS = 4
SLOTS = 64
PACK_LIMIT = 53 * 1024 * 1024
OWN = 56
LEAD = 4
WINDOW = 128
PAD = 16
F32 = jnp.float32
BF16 = jnp.bfloat16


def pairs_of(axis, first):
    count = lax.axis_size(axis)
    pairs = [(i, i + 1) for i in range(first, count - 1, 2)]
    return pairs + [(j, i) for i, j in pairs]


def rotate_rows(x, amount):
    for bit in (1, 2, 4):
        x = jnp.where((amount & bit) != 0, pltpu.roll(x, 8 - bit, x.ndim - 2), x)
    return x


def split(x):
    high = x.astype(BF16)
    return high, (x - high.astype(F32)).astype(BF16)


def iota(shape, dim):
    return lax.broadcasted_iota(jnp.int32, shape, dim)


def ends_of(len_ref, r):
    one = len_ref[r, 0]
    two = one + len_ref[r, 1]
    three = two + len_ref[r, 2]
    return one, two, three, three + len_ref[r, 3]


def begin_of(at, ends):
    begin = jnp.where(at >= ends[0], ends[0], 0)
    begin = jnp.where(at >= ends[1], ends[1], begin)
    return jnp.where(at >= ends[2], ends[2], begin)


def end_of(at, ends):
    end = jnp.where(at >= ends[0], ends[1], ends[0])
    end = jnp.where(at >= ends[1], ends[2], end)
    return jnp.where(at >= ends[2], ends[3], end)


def lanes_of(c):
    return slice(128 * c, 128 * c + 128)


def pack_kernel(base_ref, x_hbm, g_hbm, near_ref, far_ref, x_first, x_last, g_first, g_last, sems):
    rows, length, features = x_hbm.shape
    half = g_hbm.shape[1]
    copies = [
        pltpu.make_async_copy(x_hbm.at[:, pl.ds(length - PAD, PAD), :], x_last, sems.at[0]),
        pltpu.make_async_copy(g_hbm.at[:, pl.ds(half - PAD, PAD), :], g_last, sems.at[1]),
        pltpu.make_async_copy(x_hbm.at[:, pl.ds(0, PAD), :], x_first, sems.at[2]),
        pltpu.make_async_copy(g_hbm.at[:, pl.ds(0, PAD), :], g_first, sems.at[3]),
    ]
    for copy in copies:
        copy.start()
    even = (base_ref[0] // length) % 2 == 0
    sub = iota((PAD, features), 0)
    for copy in copies:
        copy.wait()
    for r in range(rows):
        moved = pltpu.roll(g_last[r].astype(F32), 2, 0)
        last = jnp.where(sub < 2, moved, x_last[r].astype(F32))
        moved = pltpu.roll(g_first[r].astype(F32), PAD - 3, 0)
        first = jnp.where(sub < PAD - 3, x_first[r].astype(F32), moved)
        near_ref[r] = jnp.where(even, last, first).astype(BF16)
        far_ref[r] = jnp.where(even, first, last).astype(BF16)


def convolve_block(base, ends, par_ref, load, at, place_high, place_low, masked=True):
    chunks = par_ref.shape[1] // 128
    sub8 = iota((8, 128), 0)
    keeps = []
    for j in range(2 if masked else 0):
        position = base - PAD + at + 8 * j + sub8
        offset = position - begin_of(position, ends)
        keeps.append([offset >= k for k in range(TAPS)])
    for c in range(chunks):
        lanes = lanes_of(c)
        parts = []
        for j in range(2):
            value = par_ref[4:5, lanes] + par_ref[0:1, lanes] * load(c, 8 * j)
            for k in range(1, TAPS):
                shifted = load(c, 8 * j - k)
                if masked:
                    shifted = jnp.where(keeps[j][k], shifted, 0.0)
                value = value + par_ref[k : k + 1, lanes] * shifted
            parts.append(value)
        high, low = split(jnp.concatenate(parts, axis=0))
        place_high(c, high)
        place_low(c, low)


def conv_kernel(shapes, base_ref, len_ref, x_ref, par_ref, high_ref, low_ref, xf):
    rows, length, half, features, tiles = shapes
    chunks = features // 128
    base = base_ref[0]
    step = 64
    for c in range(chunks):
        xf[c, 0:8, :] = jnp.zeros((8, 128), F32)
    rest = high_ref.shape[2] - PAD - length
    for r in range(rows):
        for c in range(chunks):
            for ref in (high_ref, low_ref):
                ref[r, c, 0:PAD, :] = jnp.zeros((PAD, 128), BF16)
                ref[r, c, PAD + length :, :] = jnp.zeros((rest, 128), BF16)

    def one_row(r, _):
        ends = ends_of(len_ref, r)

        def widen(i, _):
            at = pl.multiple_of(i * step, step)
            for c in range(chunks):
                xf[c, pl.ds(at + 8, step), :] = x_ref[r, pl.ds(at, step), lanes_of(c)].astype(F32)
            return 0

        lax.fori_loop(0, length // step, widen, 0)

        def blocks(at, masked):
            for b in range(step // 16):

                def put(ref):
                    def store(c, value):
                        ref[r, c, pl.ds(at + PAD + 16 * b, 16), :] = value

                    return store

                convolve_block(
                    base,
                    ends,
                    par_ref,
                    lambda c, shift: xf[c, pl.ds(at + 8 + 16 * b + shift, 8), :],
                    at + PAD + 16 * b,
                    put(high_ref),
                    put(low_ref),
                    masked,
                )

        def one_step(i, _):
            at = pl.multiple_of(i * step, step)
            reach = [(end > base + at - TAPS + 1) & (end < base + at + step) for end in ends]
            starts = functools.reduce(jnp.logical_or, reach)

            @pl.when(starts)
            def _():
                blocks(at, True)

            @pl.when(jnp.logical_not(starts))
            def _():
                blocks(at, False)

            return 0

        lax.fori_loop(0, length // step, one_step, 0)
        return 0

    lax.fori_loop(0, rows, one_row, 0)


def forward_kernel(
    shapes,
    base_ref,
    len_ref,
    x_ref,
    g_ref,
    high_ref,
    low_ref,
    near_ref,
    far_ref,
    par_ref,
    out_hbm,
    mat,
    g32,
    grad_ref,
    xb,
    xf,
    edge,
    comp,
    cs,
    es,
    fac_a,
    fac_b,
    tot,
    rows_e_ref,
    out32,
    outb,
    carry_o,
    acc,
    sems,
):
    rows, length, half, features, tiles = shapes
    pairs = rows * tiles // 2
    chunks = features // 128
    base = base_ref[0]

    def copy_out(r):
        return pltpu.make_async_copy(outb.at[r], out_hbm.at[r], sems.at[r])

    sub8 = iota((8, 128), 0)
    lane8 = iota((8, 128), 1)
    slot8 = lane8 % SLOTS
    left = lane8 < SLOTS
    delta = sub8 - 3
    first = [2 * slot8 - 3 - (2 * p + lane8 // SLOTS) for p in range(2)]
    group_of = [(f + ((sub8 - f) & 7)) >> 3 for f in first]
    turn = [f & 7 for f in first]
    first_e = 2 * slot8 - 3
    group_of_e = (first_e + ((sub8 - first_e) & 7)) >> 3
    turn_e = first_e & 7

    def place(pair, side):
        r, m = 2 * (pair // tiles) + side, pair % tiles
        return r, m, r * tiles + m

    def tile_start(m):
        return base + 2 * OWN * m - PAD

    acc[...] = jnp.zeros_like(acc)
    carry_o[...] = jnp.zeros_like(carry_o)

    subd = iota((8, features), 0)
    even = (base // length) % 2 == 0
    for r in range(rows):
        near = near_ref[r].astype(F32)
        far = far_ref[r].astype(F32)
        up = jnp.where(even, far, near)
        down = jnp.where(even, near, far)
        xb[r, 0:PAD, :] = up.astype(BF16)
        xb[r, PAD + length : 2 * PAD + length, :] = down.astype(BF16)
        rest = xb.shape[1] - 2 * PAD - length
        if rest > 0:
            xb[r, 2 * PAD + length :, :] = jnp.zeros((rest, features), BF16)
        xb[r, PAD : PAD + length, :] = x_ref[r]
        before = jnp.where(subd >= 6, pltpu.roll(up[0:8], 6, 0), 0.0)
        after = jnp.where(subd < 3, pltpu.roll(down[8:16], 3, 0), 0.0)
        rest = g32.shape[2] - PAD - half - 8
        for c in range(chunks):
            g32[r, c, 8:16, :] = before[:, lanes_of(c)]
            g32[r, c, PAD : PAD + half, :] = g_ref[r, :, lanes_of(c)].astype(F32)
            g32[r, c, PAD + half : PAD + half + 8, :] = after[:, lanes_of(c)]
            g32[r, c, PAD + half + 8 :, :] = jnp.zeros((rest, 128), F32)
        for c in range(chunks):
            lanes = lanes_of(c)
            xf[c, 0:8, :] = jnp.zeros((8, 128), F32)
            xf[c, 8:24, :] = up[:, lanes]
            xf[c, 24:40, :] = x_ref[r, 0:16, lanes].astype(F32)
            xf[c, 40:56, :] = x_ref[r, length - 16 : length, lanes].astype(F32)
            xf[c, 56:72, :] = down[:, lanes]
        ends = ends_of(len_ref, r)
        for at, where, slot in ((0, 8, 0), (PAD, 24, 16), (PAD + length, 56, 32)):

            def put(first):
                def store(c, value):
                    edge[r, c, first : first + 16, :] = value

                return store

            convolve_block(
                base,
                ends,
                par_ref,
                lambda c, shift: xf[c, where + shift : where + shift + 8, :],
                at,
                put(slot),
                put(48 + slot),
            )

    scorer_high = [par_ref[5:6, lanes_of(c)].astype(BF16).astype(F32) for c in range(chunks)]
    scorer_low = [par_ref[5:6, lanes_of(c)] - scorer_high[c] for c in range(chunks)]

    def held_rows(r, m, c):
        parts = []
        at = 2 * OWN * m
        for ref, own in ((high_ref, 0), (low_ref, 48)):
            begin = 0
            if m == 0:
                parts.append(edge[r, c, own : own + 32, :])
                begin = 32
            if m == tiles - 1:
                end = PAD + length - at
                parts.append(ref[r, c, at + begin : at + end, :])
                parts.append(edge[r, c, own + 32 : own + 48, :])
                begin = end + 16
            if begin < WINDOW:
                parts.append(ref[r, c, at + begin : at + WINDOW, :])
        return jnp.concatenate(parts, axis=0)

    for pair in range(pairs):
        dots, scores = [], []
        for side in range(2):
            r, m, _ = place(pair, side)
            start = OWN * m + 8
            streamed, held = [], []
            for c in range(chunks):
                g = g32[r, c, start : start + SLOTS, :]
                top = jnp.where(sub8 == 0, scorer_high[c], jnp.where(sub8 == 1, scorer_low[c], g[0:8]))
                streamed.append(jnp.concatenate([top, g[8:]], axis=0).astype(BF16))
                held.append(held_rows(r, m, c))
            product = lax.dot_general(
                jnp.concatenate(streamed, axis=1),
                jnp.concatenate(held, axis=1),
                (((1,), (1,)), ((), ())),
                preferred_element_type=F32,
            )
            product = product[:, :WINDOW] + product[:, WINDOW:]
            dots.append(product)
            scores.append(jnp.broadcast_to(product[0:1] + product[1:2], (SLOTS, WINDOW)))
        dots = jnp.concatenate(dots, axis=0).T
        scores = jnp.concatenate(scores, axis=0).T
        banded = jnp.zeros((8, 128), F32)
        scored = jnp.zeros((8, 128), F32)
        for v in range(WINDOW // 8):
            here = group_of_e == v
            banded = jnp.where(here, dots[8 * v : 8 * v + 8], banded)
            scored = jnp.where(here, scores[8 * v : 8 * v + 8], scored)
        comp[0, pair] = banded
        comp[1, pair] = scored

    ends = [ends_of(len_ref, r) for r in range(rows)]
    for pair in range(pairs):
        both = [place(pair, side) for side in range(2)]
        dots = rotate_rows(comp[0, pair], turn_e)
        scores = rotate_rows(comp[1, pair], turn_e)
        coef = jnp.zeros((8, 128), F32)
        coef_e = jnp.zeros((8, 128), F32)
        for p in range(2):
            at = tile_start(both[0][1]) + 2 * slot8 + p
            begin = [begin_of(at, ends[r]) for r, _, _ in both]
            end = [end_of(at, ends[r]) for r, _, _ in both]
            offset = jnp.maximum(at - jnp.where(left, begin[0], begin[1]), 0)
            remain = jnp.where(left, end[0], end[1]) - at
            masks, inverses, logits, grads = [], [], [], []
            for b in range(1, TAPS + 1):
                if b == 3:
                    thirds = ((offset.astype(F32) + 0.5) * (1.0 / 3.0)).astype(jnp.int32)
                    within = offset - 3 * thirds
                else:
                    within = offset & (b - 1)
                upper = jnp.minimum(b - within, remain)
                mask = (delta >= p - within) & (delta < p + upper)
                inverse = 1.0 / jnp.maximum(within + upper, 1).astype(F32)
                masks.append(mask)
                inverses.append(inverse)
                logits.append(jnp.sum(jnp.where(mask, scores, 0.0), axis=0, keepdims=True) * inverse)
                grads.append(
                    jnp.sum(jnp.where(mask, dots, 0.0), axis=0, keepdims=True) * (0.5 * inverse)
                )
            largest = functools.reduce(jnp.maximum, logits)
            powers = [jnp.exp(logit - largest) for logit in logits]
            scale = 1.0 / sum(powers)
            shares = [power * scale for power in powers]
            mean = sum(share * grad for share, grad in zip(shares, grads))
            for mask, inverse, share, grad in zip(masks, inverses, shares, grads):
                coef = coef + jnp.where(mask, (0.5 * share) * inverse, 0.0)
                coef_e = coef_e + jnp.where(mask, share * (grad - mean) * inverse, 0.0)
        owned = (slot8 >= LEAD) & (slot8 < LEAD + OWN)
        coef = jnp.where(owned, coef, 0.0)
        coef_e = jnp.where(owned, coef_e, 0.0)
        es[pair] = rotate_rows(coef_e, (8 - turn_e) & 7)
        swapped = pltpu.roll(coef, SLOTS, 1)
        for side, (r, m, tile) in enumerate(both):
            at = tile_start(m) + 2 * slot8 + delta
            offset = at - begin_of(at, ends[r])
            alone = jnp.where(left, coef, swapped) if side == 0 else jnp.where(left, swapped, coef)
            for p in range(2):
                kept = jnp.where((offset >= 2 * p + lane8 // SLOTS) & (at >= 0), alone, 0.0)
                cs[p, tile] = rotate_rows(kept, (8 - turn[p]) & 7)

    slots_down = iota((SLOTS, 128), 0)
    wide = 2 if chunks % 2 == 0 else 1
    factors = (fac_a, fac_b)

    def spread_pair(pair):
        spread = jnp.concatenate(
            [jnp.where(group_of_e == v, es[pair], 0.0) for v in range(WINDOW // 8)], axis=0
        ).T
        for side in range(2):
            _, m, _ = place(pair, side)
            from_row = OWN * m - 8
            part = spread[SLOTS * side : SLOTS * side + SLOTS]
            here = (from_row + slots_down >= 0) & (from_row + slots_down < half)
            own_e = jnp.sum(jnp.where(here, part, 0.0), axis=0, keepdims=True)
            all_e = jnp.sum(part, axis=0, keepdims=True)
            rows_e_ref[side, 0] = jnp.broadcast_to(own_e, (8, 128))
            rows_e_ref[side, 1] = jnp.broadcast_to(all_e, (8, 128))

    def build(pair, side):
        r, m, tile = place(pair, side)
        own_e = rows_e_ref[side, 0]
        all_e = rows_e_ref[side, 1]
        at = tile_start(m) + lane8
        offset = at - begin_of(at, ends_of(len_ref, r))
        bands = []
        for p in range(2):
            bands.append(
                jnp.concatenate(
                    [jnp.where(group_of[p] == v, cs[p, tile], 0.0) for v in range(WINDOW // 8)], axis=0
                ).T
            )
        for k in range(TAPS):
            row_k = jnp.where((offset >= k) & (at >= 0), own_e, 0.0)
            if k > 0:
                row_k = pltpu.roll(row_k, 128 - k, 1)
            matrix = bands[k // 2][SLOTS * (k % 2) : SLOTS * (k % 2) + SLOTS]
            if k == 0:
                back = jnp.concatenate([jnp.where(sub8 < 2, all_e, matrix[0:8]), matrix[8:]], axis=0)
                high, low = split(back)
                mat[tile, :, 0:WINDOW] = high
                mat[tile, :, WINDOW:] = low
            matrix = jnp.concatenate([jnp.where(sub8 == 0, row_k, matrix[0:8]), matrix[8:]], axis=0)
            if k == 0:
                total = jnp.sum(matrix, axis=1, keepdims=True)
                tot[side] = jnp.broadcast_to(total, (SLOTS, 128))
            high, low = split(matrix)
            factors[side][SLOTS * k : SLOTS * (k + 1), 0:WINDOW] = high
            factors[side][SLOTS * k : SLOTS * (k + 1), WINDOW:] = low

    def apply(pair, side):
        r, m, _ = place(pair, side)
        start = pl.multiple_of(OWN * m + 8, 8)
        window = pl.multiple_of(2 * OWN * m, 16)
        factor = factors[side][...]
        total = tot[side]
        from_row = OWN * m - 8
        mine = [from_row + 8 * i + sub8 < half for i in range(SLOTS // 8)]
        for w in range(chunks // wide):
            x = xb[r, pl.ds(window, WINDOW), 128 * wide * w : 128 * wide * (w + 1)]
            mixed = lax.dot_general(
                factor,
                jnp.concatenate([x, x], axis=0),
                (((1,), (0,)), ((), ())),
                preferred_element_type=F32,
            )
            for i in range(wide):
                c = wide * w + i
                lanes = lanes_of(c)
                g = g32[r, c, pl.ds(start, SLOTS), :]
                parts = [
                    jnp.where(
                        sub8 == 0,
                        par_ref[5:6, lanes],
                        jnp.where((sub8 >= LEAD) & (from_row + sub8 >= 0), g[0:8], 0.0),
                    )
                ]
                for j in range(1, SLOTS // 8):
                    parts.append(jnp.where(mine[j], g[8 * j : 8 * j + 8], 0.0))
                g = jnp.concatenate(parts, axis=0)
                value = total * par_ref[4:5, lanes]
                for k in range(TAPS):
                    taken = mixed[SLOTS * k : SLOTS * (k + 1), lanes_of(i)]
                    value = value + taken * par_ref[k : k + 1, lanes]
                    acc[k, :, lanes] += jnp.sum((taken * g).reshape(SLOTS // 8, 8, 128), axis=0)
                acc[4, :, lanes] += jnp.sum((total * g).reshape(SLOTS // 8, 8, 128), axis=0)
                acc[5, :, lanes] += jnp.where(sub8 == 0, value[0:8], 0.0)
                top = carry_o[side, :, lanes] + jnp.where(sub8 < LEAD, 0.0, value[0:8])
                out32[side, c, pl.ds(start, 8), :] = top
                out32[side, c, pl.ds(start + 8, OWN - 8), :] = value[8:OWN]
                carry_o[side, :, lanes] = jnp.where(m < tiles - 1, value[OWN:], 0.0)

    def finish(r, side):
        for c in range(chunks):
            outb[r, :, lanes_of(c)] = out32[side, c, PAD : PAD + half, :].astype(BF16)
        copy_out(r).start()

    spread_pair(0)
    build(0, 0)
    build(0, 1)

    def second_loop(i, _):
        @pl.when((i % tiles == 0) & (i > 0))
        def _():
            for side in range(2):
                finish(2 * (i // tiles) - 2 + side, side)

        spread_pair(i + 1)
        for side in range(2):
            apply(i, side)
            build(i + 1, side)
        return 0

    lax.fori_loop(0, pairs - 1, second_loop, 0)
    apply(pairs - 1, 0)
    apply(pairs - 1, 1)
    for side in range(2):
        finish(rows - 2 + side, side)
    for k in range(TAPS + 2):
        grad_ref[k : k + 1, :] = jnp.sum(acc[k], axis=0, keepdims=True)
    for r in range(rows):
        copy_out(r).wait()


def backward_kernel(shapes, r, base_ref, len_ref, mat, g32, par_ref, *refs):
    gin_hbm, dc, ginb, sems = refs[-4:]
    rows, length, half, features, tiles = shapes
    chunks = features // 128
    wide = 2 if chunks % 2 == 0 else 1
    base = base_ref[0]
    sub8 = iota((8, 128), 0)
    ends = ends_of(len_ref, r)

    for m in range(tiles):
        tile = r * tiles + m
        streamed = jnp.concatenate([mat[tile, :, 0:WINDOW].T, mat[tile, :, WINDOW:].T], axis=1)
        at = 2 * OWN * m
        for w in range(chunks // wide):
            held = []
            for i in range(wide):
                lanes = lanes_of(wide * w + i)
                scorer = par_ref[5:6, lanes]
                scorer_high = scorer.astype(BF16).astype(F32)
                g = g32[r, wide * w + i, OWN * m + 8 : OWN * m + 8 + SLOTS, :]
                top = jnp.where(
                    sub8 == 0, scorer_high, jnp.where(sub8 == 1, scorer - scorer_high, g[0:8])
                )
                held.append(jnp.concatenate([top, g[8:]], axis=0).astype(BF16))
            held = jnp.concatenate(held, axis=1)
            part = lax.dot_general(
                streamed,
                jnp.concatenate([held, held], axis=0),
                (((1,), (0,)), ((), ())),
                preferred_element_type=F32,
            )
            for i in range(wide):
                c = wide * w + i
                before = dc[c, at : at + PAD, :] if m > 0 else 0.0
                dc[c, at : at + PAD, :] = before + part[0:PAD, lanes_of(i)]
                dc[c, at + PAD : at + WINDOW, :] = part[PAD:, lanes_of(i)]

    def taps_at(at, masked):
        keeps = []
        if masked:
            for j in range(4):
                position = base + at + 8 * j + sub8
                remain = end_of(position, ends) - position
                keeps.append([remain > k for k in range(TAPS)])
        for c in range(chunks):
            parts = []
            for j in range(4):
                value = par_ref[0:1, lanes_of(c)] * dc[c, pl.ds(at + PAD + 8 * j, 8), :]
                for k in range(1, TAPS):
                    shifted = dc[c, pl.ds(at + PAD + 8 * j + k, 8), :]
                    if masked:
                        shifted = jnp.where(keeps[j][k], shifted, 0.0)
                    value = value + par_ref[k : k + 1, lanes_of(c)] * shifted
                parts.append(value)
            ginb[pl.ds(at, 32), lanes_of(c)] = jnp.concatenate(parts, axis=0).astype(BF16)

    def taps(i, _):
        at = pl.multiple_of(i * 32, 32)
        reach = [(end > base + at) & (end <= base + at + 32 + TAPS - 2) for end in ends]
        crosses = functools.reduce(jnp.logical_or, reach)

        @pl.when(crosses)
        def _():
            taps_at(at, True)

        @pl.when(jnp.logical_not(crosses))
        def _():
            taps_at(at, False)

        return 0

    pieces = 2
    copies = []
    for piece in range(pieces):
        size = length // pieces
        lax.fori_loop(piece * size // 32, (piece + 1) * size // 32, taps, 0)
        copies.append(
            pltpu.make_async_copy(
                ginb.at[pl.ds(piece * size, size), :],
                gin_hbm.at[r, pl.ds(piece * size, size), :],
                sems.at[piece],
            )
        )
        copies[-1].start()
    for copy in copies:
        copy.wait()


SMEM = pl.BlockSpec(memory_space=pltpu.SMEM)
VMEM = pl.BlockSpec(memory_space=pltpu.VMEM)
HBM = pl.BlockSpec(memory_space=pltpu.HBM)


def sizes_of(length, half):
    tiles = -(-(half + 3 + LEAD) // OWN)
    x_rows = 2 * OWN * (tiles - 1) + WINDOW
    g_rows = -(-(OWN * (tiles - 1) + 8 + SLOTS) // 16) * 16
    return tiles, x_rows, g_rows


def packed(base, inputs, cotangent):
    rows, _, features = inputs.shape
    part = jax.ShapeDtypeStruct((rows, PAD, features), BF16)
    return pl.pallas_call(
        pack_kernel,
        out_shape=(part, part),
        in_specs=[SMEM, HBM, HBM],
        out_specs=(VMEM, VMEM),
        scratch_shapes=[pltpu.VMEM((rows, PAD, features), BF16)] * 4 + [pltpu.SemaphoreType.DMA((4,))],
        compiler_params=pltpu.CompilerParams(vmem_limit_bytes=PACK_LIMIT),
    )(base, inputs, cotangent)


def convolved(base, lengths, inputs, params):
    rows, length, features = inputs.shape
    half = length // 2
    chunks = features // 128
    tiles, x_rows, _ = sizes_of(length, half)
    shapes = (rows, length, half, features, tiles)
    part = jax.ShapeDtypeStruct((rows, chunks, x_rows, 128), BF16)
    return pl.pallas_call(
        functools.partial(conv_kernel, shapes),
        out_shape=(part, part),
        in_specs=[SMEM, SMEM, VMEM, VMEM],
        out_specs=(VMEM, VMEM),
        scratch_shapes=[pltpu.VMEM((chunks, 8 + length, 128), F32)],
        compiler_params=pltpu.CompilerParams(vmem_limit_bytes=24 * 1024 * 1024),
        cost_estimate=pl.CostEstimate(
            flops=24 * inputs.size, bytes_accessed=8 * inputs.size, transcendentals=0
        ),
    )(base, lengths, inputs, params)


def forward(base, lengths, inputs, cotangent, high, low, near, far, params):
    rows, half, features = cotangent.shape
    length = 2 * half
    chunks = features // 128
    tiles, x_rows, g_rows = sizes_of(length, half)
    count = rows * tiles
    shapes = (rows, length, half, features, tiles)
    return pl.pallas_call(
        functools.partial(forward_kernel, shapes),
        out_shape=(
            jax.ShapeDtypeStruct((rows, half, features), BF16),
            jax.ShapeDtypeStruct((count, SLOTS, 2 * WINDOW), BF16),
            jax.ShapeDtypeStruct((rows, chunks, g_rows, 128), F32),
            jax.ShapeDtypeStruct((TAPS + 2, features), F32),
        ),
        in_specs=[SMEM, SMEM, VMEM, VMEM, VMEM, VMEM, VMEM, VMEM, VMEM],
        out_specs=(HBM, VMEM, VMEM, VMEM),
        scratch_shapes=[
            pltpu.VMEM((rows, x_rows, features), BF16),
            pltpu.VMEM((chunks, 72, 128), F32),
            pltpu.VMEM((rows, chunks, 96, 128), BF16),
            pltpu.VMEM((2, count // 2, 8, 128), F32),
            pltpu.VMEM((2, count, 8, 128), F32),
            pltpu.VMEM((count // 2, 8, 128), F32),
            pltpu.VMEM((TAPS * SLOTS, 2 * WINDOW), BF16),
            pltpu.VMEM((TAPS * SLOTS, 2 * WINDOW), BF16),
            pltpu.VMEM((2, SLOTS, 128), F32),
            pltpu.VMEM((2, 2, 8, 128), F32),
            pltpu.VMEM((2, chunks, g_rows, 128), F32),
            pltpu.VMEM((rows, half, features), BF16),
            pltpu.VMEM((2, 8, features), F32),
            pltpu.VMEM((TAPS + 2, 8, features), F32),
            pltpu.SemaphoreType.DMA((rows,)),
        ],
        compiler_params=pltpu.CompilerParams(vmem_limit_bytes=28 * 1024 * 1024),
        cost_estimate=pl.CostEstimate(
            flops=2 * count * SLOTS * WINDOW * features * 12,
            bytes_accessed=8 * inputs.size,
            transcendentals=0,
        ),
    )(base, lengths, inputs, cotangent, high, low, near, far, params)


def backward(r, base, lengths, shape, matrices, padded, params, grown):
    rows, length, features = shape
    half = length // 2
    chunks = features // 128
    tiles, x_rows, g_rows = sizes_of(length, half)
    shapes = (rows, length, half, features, tiles)
    operands = [base, lengths, matrices, padded, params]
    in_specs = [SMEM, SMEM, VMEM, VMEM, VMEM]
    if grown is not None:
        operands.append(grown)
        in_specs.append(HBM)
    return pl.pallas_call(
        functools.partial(backward_kernel, shapes, r),
        out_shape=jax.ShapeDtypeStruct(shape, BF16),
        in_specs=in_specs,
        out_specs=HBM,
        scratch_shapes=[
            pltpu.VMEM((chunks, x_rows, 128), F32),
            pltpu.VMEM((length, features), BF16),
            pltpu.SemaphoreType.DMA((2,)),
        ],
        input_output_aliases={} if grown is None else {5: 0},
        compiler_params=pltpu.CompilerParams(vmem_limit_bytes=12 * 1024 * 1024),
        cost_estimate=pl.CostEstimate(
            flops=2 * tiles * SLOTS * WINDOW * features * 4,
            bytes_accessed=4 * length * features,
            transcendentals=0,
        ),
    )(*operands)


def update_kernel(
    grad_ref, other_ref, par_ref, first_ref, second_ref, norm_ref, new_ref, new_first_ref, new_second_ref
):
    grads = grad_ref[...] + other_ref[...]
    norm = jnp.sqrt(jnp.sum(grads * grads, keepdims=True))
    norm_ref[...] = norm
    grads = grads * jnp.minimum(1.0, clip_limit / (norm + 1e-06))
    weights = par_ref[...]
    first_new = beta_one * first_ref[...] + (1.0 - beta_one) * grads
    second_new = beta_two * second_ref[...] + (1.0 - beta_two) * grads * grads
    first_hat = first_new / (1.0 - beta_one**STEP)
    second_hat = second_new / (1.0 - beta_two**STEP)
    new_ref[...] = weights - learn_rate * (
        first_hat / (jnp.sqrt(second_hat) + adam_eps) + decay_rate * weights
    )
    new_first_ref[...] = first_new
    new_second_ref[...] = second_new


def update(grads, other, weights, first_old, second_old):
    like = jax.ShapeDtypeStruct(weights.shape, F32)
    return pl.pallas_call(
        update_kernel,
        out_shape=(jax.ShapeDtypeStruct((1, 1), F32), like, like, like),
        in_specs=[VMEM] * 5,
        out_specs=(VMEM,) * 4,
        compiler_params=pltpu.CompilerParams(vmem_limit_bytes=4 * 1024 * 1024),
    )(grads, other, weights, first_old, second_old)


def rounds_of(axes):
    rounds = []
    for axis in axes:
        count = lax.axis_size(axis)
        step = 1
        while step < count:
            rounds.append((axis, [(i, i ^ step) for i in range(count)]))
            step *= 2
    return rounds


def per_device(inputs, lengths, params, first_moment, second_moment, cotangent):
    rows_here, length_here, _ = inputs.shape
    base = (lax.axis_index("group") * length_here).astype(jnp.int32).reshape(1)
    near, far = packed(base, inputs, cotangent)
    far = lax.ppermute(far, "group", pairs_of("group", 1))
    near = lax.ppermute(near, "group", pairs_of("group", 0))
    high, low = convolved(base, lengths, inputs, params)
    output, matrices, padded, grad_params = forward(
        base, lengths, inputs, cotangent, high, low, near, far, params
    )

    def backward_row(row, matrices, grown):
        return backward(row, base, lengths, inputs.shape, matrices, padded, params, grown)

    grad_inputs = None
    row = 0
    received = None
    for axis, exchange in rounds_of(("group", "rows")):
        if received is not None:
            grad_params = grad_params + received
            if row < rows_here:
                matrices, grad_params = lax.optimization_barrier((matrices, grad_params))
                grown = backward_row(row, matrices, grad_inputs)
                received = lax.ppermute(grad_params, axis, exchange)
                received, grad_inputs = lax.optimization_barrier((received, grown))
                row += 1
                continue
        received = lax.ppermute(grad_params, axis, exchange)
    while row < rows_here:
        grad_inputs = backward_row(row, matrices, grad_inputs)
        row += 1
    grad_norm, new_params, new_first, new_second = update(
        grad_params, received, params, first_moment, second_moment
    )
    grad_norm = grad_norm.reshape(())
    return (output, grad_inputs, grad_norm, new_params, new_first, new_second)


def solution(mesh):
    in_specs = (P("rows", "group", None), P("rows", None), P(), P(), P(), P("rows", "group", None))
    out_specs = (P("rows", "group", None), P("rows", "group", None), P(), P(), P(), P())
    return jax.shard_map(
        per_device, mesh=mesh, in_specs=in_specs, out_specs=out_specs, check_vma=False
    )
```

```python
import functools

import jax
import jax.numpy as jnp
from jax import lax
from jax.experimental import pallas as pl
from jax.experimental.pallas import tpu as pltpu
from jax.sharding import PartitionSpec as P

STEP = 10


beta_one = 0.9
beta_two = 0.999
learn_rate = 0.2
decay_rate = 0.01
adam_eps = 1e-08
clip_limit = 1.0

TAPS = 4
SLOTS = 64
PACK_LIMIT = 53 * 1024 * 1024
OWN = 56
LEAD = 4
WINDOW = 128
PAD = 16
F32 = jnp.float32
BF16 = jnp.bfloat16


def pairs_of(axis, first):
    count = lax.axis_size(axis)
    pairs = [(i, i + 1) for i in range(first, count - 1, 2)]
    return pairs + [(j, i) for i, j in pairs]


def rotate_rows(x, amount):
    for bit in (1, 2, 4):
        x = jnp.where((amount & bit) != 0, pltpu.roll(x, 8 - bit, x.ndim - 2), x)
    return x


def split(x):
    high = x.astype(BF16)
    return high, (x - high.astype(F32)).astype(BF16)


def iota(shape, dim):
    return lax.broadcasted_iota(jnp.int32, shape, dim)


def ends_of(len_ref, r):
    one = len_ref[r, 0]
    two = one + len_ref[r, 1]
    three = two + len_ref[r, 2]
    return one, two, three, three + len_ref[r, 3]


def begin_of(at, ends):
    begin = jnp.where(at >= ends[0], ends[0], 0)
    begin = jnp.where(at >= ends[1], ends[1], begin)
    return jnp.where(at >= ends[2], ends[2], begin)


def end_of(at, ends):
    end = jnp.where(at >= ends[0], ends[1], ends[0])
    end = jnp.where(at >= ends[1], ends[2], end)
    return jnp.where(at >= ends[2], ends[3], end)


def lanes_of(c):
    return slice(128 * c, 128 * c + 128)


def pack_kernel(base_ref, x_hbm, g_hbm, near_ref, far_ref, x_first, x_last, g_first, g_last, sems):
    rows, length, features = x_hbm.shape
    half = g_hbm.shape[1]
    copies = [
        pltpu.make_async_copy(x_hbm.at[:, pl.ds(length - PAD, PAD), :], x_last, sems.at[0]),
        pltpu.make_async_copy(g_hbm.at[:, pl.ds(half - PAD, PAD), :], g_last, sems.at[1]),
        pltpu.make_async_copy(x_hbm.at[:, pl.ds(0, PAD), :], x_first, sems.at[2]),
        pltpu.make_async_copy(g_hbm.at[:, pl.ds(0, PAD), :], g_first, sems.at[3]),
    ]
    for copy in copies:
        copy.start()
    even = (base_ref[0] // length) % 2 == 0
    sub = iota((PAD, features), 0)
    for copy in copies:
        copy.wait()
    for r in range(rows):
        moved = pltpu.roll(g_last[r].astype(F32), 2, 0)
        last = jnp.where(sub < 2, moved, x_last[r].astype(F32))
        moved = pltpu.roll(g_first[r].astype(F32), PAD - 3, 0)
        first = jnp.where(sub < PAD - 3, x_first[r].astype(F32), moved)
        near_ref[r] = jnp.where(even, last, first).astype(BF16)
        far_ref[r] = jnp.where(even, first, last).astype(BF16)


def convolve_block(base, ends, par_ref, load, at, place_high, place_low, masked=True):
    chunks = par_ref.shape[1] // 128
    sub8 = iota((8, 128), 0)
    keeps = []
    for j in range(2 if masked else 0):
        position = base - PAD + at + 8 * j + sub8
        offset = position - begin_of(position, ends)
        keeps.append([offset >= k for k in range(TAPS)])
    for c in range(chunks):
        lanes = lanes_of(c)
        parts = []
        for j in range(2):
            value = par_ref[4:5, lanes] + par_ref[0:1, lanes] * load(c, 8 * j)
            for k in range(1, TAPS):
                shifted = load(c, 8 * j - k)
                if masked:
                    shifted = jnp.where(keeps[j][k], shifted, 0.0)
                value = value + par_ref[k : k + 1, lanes] * shifted
            parts.append(value)
        high, low = split(jnp.concatenate(parts, axis=0))
        place_high(c, high)
        place_low(c, low)


def conv_kernel(shapes, base_ref, len_hbm, x_ref, par_ref, high_ref, low_ref, xf, len_ref, sem):
    rows, length, half, features, tiles = shapes
    chunks = features // 128
    base = base_ref[0]
    step = 64
    copy_len = pltpu.make_async_copy(len_hbm, len_ref, sem.at[0])
    copy_len.start()
    begin = 2 * PAD + length
    rest = high_ref.shape[2] - begin
    for r in range(rows):
        for c in range(chunks):
            xf[r, c, 0:8, :] = jnp.zeros((8, 128), F32)
            if rest > 0:
                for ref in (high_ref, low_ref):
                    ref[r, c, begin:, :] = jnp.zeros((rest, 128), BF16)

    def widen(i, _):
        r = i // (length // step)
        at = pl.multiple_of((i % (length // step)) * step, step)
        for c in range(chunks):
            xf[r, c, pl.ds(at + 8, step), :] = x_ref[r, pl.ds(at, step), lanes_of(c)].astype(F32)
        return 0

    lax.fori_loop(0, rows * (length // step), widen, 0)
    copy_len.wait()

    def one_row(r, _):
        ends = ends_of(len_ref, r)

        def blocks(at, masked):
            for b in range(step // 16):

                def put(ref):
                    def store(c, value):
                        ref[r, c, pl.ds(at + PAD + 16 * b, 16), :] = value

                    return store

                convolve_block(
                    base,
                    ends,
                    par_ref,
                    lambda c, shift: xf[r, c, pl.ds(at + 8 + 16 * b + shift, 8), :],
                    at + PAD + 16 * b,
                    put(high_ref),
                    put(low_ref),
                    masked,
                )

        def one_step(i, _):
            at = pl.multiple_of(i * step, step)
            reach = [(end > base + at - TAPS + 1) & (end < base + at + step) for end in ends]
            starts = functools.reduce(jnp.logical_or, reach)

            @pl.when(starts)
            def _():
                blocks(at, True)

            @pl.when(jnp.logical_not(starts))
            def _():
                blocks(at, False)

            return 0

        lax.fori_loop(0, length // step, one_step, 0)
        return 0

    lax.fori_loop(0, rows, one_row, 0)


def forward_kernel(
    shapes,
    base_ref,
    len_ref,
    x_ref,
    g_ref,
    high_ref,
    low_ref,
    near_ref,
    far_ref,
    par_ref,
    out32,
    mat,
    g32,
    grad_ref,
    xb,
    xf,
    edge,
    comp,
    cs,
    es,
    fac_a,
    fac_b,
    tot,
    rows_e_ref,
    carry_o,
    acc,
):
    rows, length, half, features, tiles = shapes
    pairs = rows * tiles // 2
    chunks = features // 128
    base = base_ref[0]

    sub8 = iota((8, 128), 0)
    lane8 = iota((8, 128), 1)
    slot8 = lane8 % SLOTS
    left = lane8 < SLOTS
    delta = sub8 - 3
    first = [2 * slot8 - 3 - (2 * p + lane8 // SLOTS) for p in range(2)]
    group_of = [(f + ((sub8 - f) & 7)) >> 3 for f in first]
    turn = [f & 7 for f in first]
    first_e = 2 * slot8 - 3
    group_of_e = (first_e + ((sub8 - first_e) & 7)) >> 3
    turn_e = first_e & 7

    def place(pair, side):
        r, m = 2 * (pair // tiles) + side, pair % tiles
        return r, m, r * tiles + m

    def tile_start(m):
        return base + 2 * OWN * m - PAD

    acc[...] = jnp.zeros_like(acc)
    carry_o[...] = jnp.zeros_like(carry_o)

    subd = iota((8, features), 0)
    even = (base // length) % 2 == 0
    for r in range(rows):
        near = near_ref[r].astype(F32)
        far = far_ref[r].astype(F32)
        up = jnp.where(even, far, near)
        down = jnp.where(even, near, far)
        xb[r, 0:PAD, :] = up.astype(BF16)
        xb[r, PAD + length : 2 * PAD + length, :] = down.astype(BF16)
        rest = xb.shape[1] - 2 * PAD - length
        if rest > 0:
            xb[r, 2 * PAD + length :, :] = jnp.zeros((rest, features), BF16)
        xb[r, PAD : PAD + length, :] = x_ref[r]
        before = jnp.where(subd >= 6, pltpu.roll(up[0:8], 6, 0), 0.0)
        after = jnp.where(subd < 3, pltpu.roll(down[8:16], 3, 0), 0.0)
        rest = g32.shape[2] - PAD - half - 8
        for c in range(chunks):
            g32[r, c, 8:16, :] = before[:, lanes_of(c)]
            g32[r, c, PAD : PAD + half, :] = g_ref[r, :, lanes_of(c)].astype(F32)
            g32[r, c, PAD + half : PAD + half + 8, :] = after[:, lanes_of(c)]
            g32[r, c, PAD + half + 8 :, :] = jnp.zeros((rest, 128), F32)
        for c in range(chunks):
            lanes = lanes_of(c)
            xf[c, 0:8, :] = jnp.zeros((8, 128), F32)
            xf[c, 8:24, :] = up[:, lanes]
            xf[c, 24:40, :] = x_ref[r, 0:16, lanes].astype(F32)
            xf[c, 40:56, :] = x_ref[r, length - 16 : length, lanes].astype(F32)
            xf[c, 56:72, :] = down[:, lanes]
        ends = ends_of(len_ref, r)
        for at, where, slot in ((0, 8, 0), (PAD, 24, 16), (PAD + length, 56, 32)):

            def put(first):
                def store(c, value):
                    edge[r, c, first : first + 16, :] = value

                return store

            convolve_block(
                base,
                ends,
                par_ref,
                lambda c, shift: xf[c, where + shift : where + shift + 8, :],
                at,
                put(slot),
                put(48 + slot),
            )

    scorer_high = [par_ref[5:6, lanes_of(c)].astype(BF16).astype(F32) for c in range(chunks)]
    scorer_low = [par_ref[5:6, lanes_of(c)] - scorer_high[c] for c in range(chunks)]

    def held_rows(r, m, c):
        parts = []
        at = 2 * OWN * m
        for ref, own in ((high_ref, 0), (low_ref, 48)):
            begin = 0
            if m == 0:
                parts.append(edge[r, c, own : own + 32, :])
                begin = 32
            if m == tiles - 1:
                end = PAD + length - at
                parts.append(ref[r, c, at + begin : at + end, :])
                parts.append(edge[r, c, own + 32 : own + 48, :])
                begin = end + 16
            if begin < WINDOW:
                parts.append(ref[r, c, at + begin : at + WINDOW, :])
        return jnp.concatenate(parts, axis=0)

    for pair in range(pairs):
        dots, scores = [], []
        for side in range(2):
            r, m, _ = place(pair, side)
            start = OWN * m + 8
            streamed, held = [], []
            for c in range(chunks):
                g = g32[r, c, start : start + SLOTS, :]
                top = jnp.where(sub8 == 0, scorer_high[c], jnp.where(sub8 == 1, scorer_low[c], g[0:8]))
                streamed.append(jnp.concatenate([top, g[8:]], axis=0).astype(BF16))
                held.append(held_rows(r, m, c))
            product = lax.dot_general(
                jnp.concatenate(streamed, axis=1),
                jnp.concatenate(held, axis=1),
                (((1,), (1,)), ((), ())),
                preferred_element_type=F32,
            )
            product = product[:, :WINDOW] + product[:, WINDOW:]
            dots.append(product)
            scores.append(jnp.broadcast_to(product[0:1] + product[1:2], (SLOTS, WINDOW)))
        dots = jnp.concatenate(dots, axis=0).T
        scores = jnp.concatenate(scores, axis=0).T
        banded = jnp.zeros((8, 128), F32)
        scored = jnp.zeros((8, 128), F32)
        for v in range(WINDOW // 8):
            here = group_of_e == v
            banded = jnp.where(here, dots[8 * v : 8 * v + 8], banded)
            scored = jnp.where(here, scores[8 * v : 8 * v + 8], scored)
        comp[0, pair] = banded
        comp[1, pair] = scored

    ends = [ends_of(len_ref, r) for r in range(rows)]
    for pair in range(pairs):
        both = [place(pair, side) for side in range(2)]
        dots = rotate_rows(comp[0, pair], turn_e)
        scores = rotate_rows(comp[1, pair], turn_e)
        coef = jnp.zeros((8, 128), F32)
        coef_e = jnp.zeros((8, 128), F32)
        for p in range(2):
            at = tile_start(both[0][1]) + 2 * slot8 + p
            begin = [begin_of(at, ends[r]) for r, _, _ in both]
            end = [end_of(at, ends[r]) for r, _, _ in both]
            offset = jnp.maximum(at - jnp.where(left, begin[0], begin[1]), 0)
            remain = jnp.where(left, end[0], end[1]) - at
            masks, inverses, logits, grads = [], [], [], []
            for b in range(1, TAPS + 1):
                if b == 3:
                    thirds = ((offset.astype(F32) + 0.5) * (1.0 / 3.0)).astype(jnp.int32)
                    within = offset - 3 * thirds
                else:
                    within = offset & (b - 1)
                upper = jnp.minimum(b - within, remain)
                mask = (delta >= p - within) & (delta < p + upper)
                inverse = 1.0 / jnp.maximum(within + upper, 1).astype(F32)
                masks.append(mask)
                inverses.append(inverse)
                logits.append(jnp.sum(jnp.where(mask, scores, 0.0), axis=0, keepdims=True) * inverse)
                grads.append(
                    jnp.sum(jnp.where(mask, dots, 0.0), axis=0, keepdims=True) * (0.5 * inverse)
                )
            largest = functools.reduce(jnp.maximum, logits)
            powers = [jnp.exp(logit - largest) for logit in logits]
            scale = 1.0 / sum(powers)
            shares = [power * scale for power in powers]
            mean = sum(share * grad for share, grad in zip(shares, grads))
            for mask, inverse, share, grad in zip(masks, inverses, shares, grads):
                coef = coef + jnp.where(mask, (0.5 * share) * inverse, 0.0)
                coef_e = coef_e + jnp.where(mask, share * (grad - mean) * inverse, 0.0)
        owned = (slot8 >= LEAD) & (slot8 < LEAD + OWN)
        coef = jnp.where(owned, coef, 0.0)
        coef_e = jnp.where(owned, coef_e, 0.0)
        es[pair] = rotate_rows(coef_e, (8 - turn_e) & 7)
        swapped = pltpu.roll(coef, SLOTS, 1)
        for side, (r, m, tile) in enumerate(both):
            at = tile_start(m) + 2 * slot8 + delta
            offset = at - begin_of(at, ends[r])
            alone = jnp.where(left, coef, swapped) if side == 0 else jnp.where(left, swapped, coef)
            for p in range(2):
                kept = jnp.where((offset >= 2 * p + lane8 // SLOTS) & (at >= 0), alone, 0.0)
                cs[p, tile] = rotate_rows(kept, (8 - turn[p]) & 7)

    slots_down = iota((SLOTS, 128), 0)
    wide = 2 if chunks % 2 == 0 else 1
    factors = (fac_a, fac_b)

    def spread_pair(pair):
        spread = jnp.concatenate(
            [jnp.where(group_of_e == v, es[pair], 0.0) for v in range(WINDOW // 8)], axis=0
        ).T
        for side in range(2):
            _, m, _ = place(pair, side)
            from_row = OWN * m - 8
            part = spread[SLOTS * side : SLOTS * side + SLOTS]
            here = (from_row + slots_down >= 0) & (from_row + slots_down < half)
            own_e = jnp.sum(jnp.where(here, part, 0.0), axis=0, keepdims=True)
            all_e = jnp.sum(part, axis=0, keepdims=True)
            rows_e_ref[side, 0] = jnp.broadcast_to(own_e, (8, 128))
            rows_e_ref[side, 1] = jnp.broadcast_to(all_e, (8, 128))

    def build(pair, side):
        r, m, tile = place(pair, side)
        own_e = rows_e_ref[side, 0]
        all_e = rows_e_ref[side, 1]
        from_row = OWN * m - 8
        mine = [
            (from_row + 8 * i + sub8 >= 0) & (from_row + 8 * i + sub8 < half) for i in range(SLOTS // 8)
        ]
        at = tile_start(m) + lane8
        offset = at - begin_of(at, ends_of(len_ref, r))
        bands = []
        for p in range(2):
            bands.append(
                jnp.concatenate(
                    [jnp.where(group_of[p] == v, cs[p, tile], 0.0) for v in range(WINDOW // 8)], axis=0
                ).T
            )
        for k in range(TAPS):
            row_k = jnp.where((offset >= k) & (at >= 0), own_e, 0.0)
            if k > 0:
                row_k = pltpu.roll(row_k, 128 - k, 1)
            matrix = bands[k // 2][SLOTS * (k % 2) : SLOTS * (k % 2) + SLOTS]
            if k == 0:
                back = jnp.concatenate([jnp.where(sub8 < 2, all_e, matrix[0:8]), matrix[8:]], axis=0)
                high, low = split(back)
                mat[tile, :, 0:WINDOW] = high
                mat[tile, :, WINDOW:] = low
            parts = [jnp.where(mine[i], matrix[8 * i : 8 * i + 8], 0.0) for i in range(SLOTS // 8)]
            parts[0] = jnp.where(sub8 == 0, row_k, parts[0])
            matrix = jnp.concatenate(parts, axis=0)
            if k == 0:
                total = jnp.sum(matrix, axis=1, keepdims=True)
                tot[side] = jnp.broadcast_to(total, (SLOTS, 128))
            high, low = split(matrix)
            factors[side][SLOTS * k : SLOTS * (k + 1), 0:WINDOW] = high
            factors[side][SLOTS * k : SLOTS * (k + 1), WINDOW:] = low

    def apply(pair, side):
        r, m, _ = place(pair, side)
        start = pl.multiple_of(OWN * m + 8, 8)
        window = pl.multiple_of(2 * OWN * m, 16)
        factor = factors[side][...]
        total = tot[side]
        for w in range(chunks // wide):
            x = xb[r, pl.ds(window, WINDOW), 128 * wide * w : 128 * wide * (w + 1)]
            mixed = lax.dot_general(
                factor,
                jnp.concatenate([x, x], axis=0),
                (((1,), (0,)), ((), ())),
                preferred_element_type=F32,
            )
            for i in range(wide):
                c = wide * w + i
                lanes = lanes_of(c)
                g = g32[r, c, pl.ds(start, SLOTS), :]
                g = jnp.concatenate([jnp.where(sub8 == 0, par_ref[5:6, lanes], g[0:8]), g[8:]], axis=0)
                value = total * par_ref[4:5, lanes]
                for k in range(TAPS):
                    taken = mixed[SLOTS * k : SLOTS * (k + 1), lanes_of(i)]
                    value = value + taken * par_ref[k : k + 1, lanes]
                    acc[k, :, lanes] += jnp.sum((taken * g).reshape(SLOTS // 8, 8, 128), axis=0)
                acc[4, :, lanes] += jnp.sum((total * g).reshape(SLOTS // 8, 8, 128), axis=0)
                acc[5, :, lanes] += jnp.where(sub8 == 0, value[0:8], 0.0)
                top = carry_o[side, :, lanes] + jnp.where(sub8 < LEAD, 0.0, value[0:8])
                out32[r, c, pl.ds(start, 8), :] = top
                out32[r, c, pl.ds(start + 8, OWN - 8), :] = value[8:OWN]
                carry_o[side, :, lanes] = jnp.where(m < tiles - 1, value[OWN:], 0.0)

    spread_pair(0)
    build(0, 0)
    build(0, 1)

    def second_loop(i, _):
        spread_pair(i + 1)
        for side in range(2):
            apply(i, side)
            build(i + 1, side)
        return 0

    lax.fori_loop(0, pairs - 1, second_loop, 0)
    apply(pairs - 1, 0)
    apply(pairs - 1, 1)
    for k in range(TAPS + 2):
        grad_ref[k : k + 1, :] = jnp.sum(acc[k], axis=0, keepdims=True)


def backward_kernel(shapes, r, base_ref, len_ref, mat, g32, out32, par_ref, *refs):
    out_hbm, gin_hbm, outb, dc, ginb, sems = refs[-6:]
    rows, length, half, features, tiles = shapes
    chunks = features // 128
    wide = 2 if chunks % 2 == 0 else 1
    base = base_ref[0]
    sub8 = iota((8, 128), 0)
    ends = ends_of(len_ref, r)
    for c in range(chunks):
        outb[:, lanes_of(c)] = out32[r, c, PAD : PAD + half, :].astype(BF16)
    copies = [pltpu.make_async_copy(outb, out_hbm.at[r], sems.at[2])]
    copies[0].start()

    for m in range(tiles):
        tile = r * tiles + m
        streamed = jnp.concatenate([mat[tile, :, 0:WINDOW].T, mat[tile, :, WINDOW:].T], axis=1)
        at = 2 * OWN * m
        for w in range(chunks // wide):
            held = []
            for i in range(wide):
                lanes = lanes_of(wide * w + i)
                scorer = par_ref[5:6, lanes]
                scorer_high = scorer.astype(BF16).astype(F32)
                g = g32[r, wide * w + i, OWN * m + 8 : OWN * m + 8 + SLOTS, :]
                top = jnp.where(
                    sub8 == 0, scorer_high, jnp.where(sub8 == 1, scorer - scorer_high, g[0:8])
                )
                held.append(jnp.concatenate([top, g[8:]], axis=0).astype(BF16))
            held = jnp.concatenate(held, axis=1)
            part = lax.dot_general(
                streamed,
                jnp.concatenate([held, held], axis=0),
                (((1,), (0,)), ((), ())),
                preferred_element_type=F32,
            )
            for i in range(wide):
                c = wide * w + i
                before = dc[c, at : at + PAD, :] if m > 0 else 0.0
                dc[c, at : at + PAD, :] = before + part[0:PAD, lanes_of(i)]
                dc[c, at + PAD : at + WINDOW, :] = part[PAD:, lanes_of(i)]

    def taps_at(at, masked):
        keeps = []
        if masked:
            for j in range(4):
                position = base + at + 8 * j + sub8
                remain = end_of(position, ends) - position
                keeps.append([remain > k for k in range(TAPS)])
        for c in range(chunks):
            parts = []
            for j in range(4):
                value = par_ref[0:1, lanes_of(c)] * dc[c, pl.ds(at + PAD + 8 * j, 8), :]
                for k in range(1, TAPS):
                    shifted = dc[c, pl.ds(at + PAD + 8 * j + k, 8), :]
                    if masked:
                        shifted = jnp.where(keeps[j][k], shifted, 0.0)
                    value = value + par_ref[k : k + 1, lanes_of(c)] * shifted
                parts.append(value)
            ginb[pl.ds(at, 32), lanes_of(c)] = jnp.concatenate(parts, axis=0).astype(BF16)

    def taps(i, _):
        at = pl.multiple_of(i * 32, 32)
        reach = [(end > base + at) & (end <= base + at + 32 + TAPS - 2) for end in ends]
        crosses = functools.reduce(jnp.logical_or, reach)

        @pl.when(crosses)
        def _():
            taps_at(at, True)

        @pl.when(jnp.logical_not(crosses))
        def _():
            taps_at(at, False)

        return 0

    pieces = 2
    for piece in range(pieces):
        size = length // pieces
        lax.fori_loop(piece * size // 32, (piece + 1) * size // 32, taps, 0)
        copies.append(
            pltpu.make_async_copy(
                ginb.at[pl.ds(piece * size, size), :],
                gin_hbm.at[r, pl.ds(piece * size, size), :],
                sems.at[piece],
            )
        )
        copies[-1].start()
    for copy in copies:
        copy.wait()


SMEM = pl.BlockSpec(memory_space=pltpu.SMEM)
VMEM = pl.BlockSpec(memory_space=pltpu.VMEM)
HBM = pl.BlockSpec(memory_space=pltpu.HBM)


def sizes_of(length, half):
    tiles = -(-(half + 3 + LEAD) // OWN)
    x_rows = 2 * OWN * (tiles - 1) + WINDOW
    g_rows = -(-(OWN * (tiles - 1) + 8 + SLOTS) // 16) * 16
    return tiles, x_rows, g_rows


def packed(base, inputs, cotangent):
    rows, _, features = inputs.shape
    part = jax.ShapeDtypeStruct((rows, PAD, features), BF16)
    return pl.pallas_call(
        pack_kernel,
        out_shape=(part, part),
        in_specs=[SMEM, HBM, HBM],
        out_specs=(VMEM, VMEM),
        scratch_shapes=[pltpu.VMEM((rows, PAD, features), BF16)] * 4 + [pltpu.SemaphoreType.DMA((4,))],
        compiler_params=pltpu.CompilerParams(vmem_limit_bytes=PACK_LIMIT),
    )(base, inputs, cotangent)


def convolved(base, lengths, inputs, params):
    rows, length, features = inputs.shape
    half = length // 2
    chunks = features // 128
    tiles, x_rows, _ = sizes_of(length, half)
    shapes = (rows, length, half, features, tiles)
    part = jax.ShapeDtypeStruct((rows, chunks, x_rows, 128), BF16)
    return pl.pallas_call(
        functools.partial(conv_kernel, shapes),
        out_shape=(part, part),
        in_specs=[SMEM, HBM, VMEM, VMEM],
        out_specs=(VMEM, VMEM),
        scratch_shapes=[
            pltpu.VMEM((rows, chunks, 8 + length, 128), F32),
            pltpu.SMEM(lengths.shape, jnp.int32),
            pltpu.SemaphoreType.DMA((1,)),
        ],
        compiler_params=pltpu.CompilerParams(vmem_limit_bytes=24 * 1024 * 1024),
        cost_estimate=pl.CostEstimate(
            flops=24 * inputs.size, bytes_accessed=8 * inputs.size, transcendentals=0
        ),
    )(base, lengths, inputs, params)


def forward(base, lengths, inputs, cotangent, high, low, near, far, params):
    rows, half, features = cotangent.shape
    length = 2 * half
    chunks = features // 128
    tiles, x_rows, g_rows = sizes_of(length, half)
    count = rows * tiles
    shapes = (rows, length, half, features, tiles)
    return pl.pallas_call(
        functools.partial(forward_kernel, shapes),
        out_shape=(
            jax.ShapeDtypeStruct((rows, chunks, g_rows, 128), F32),
            jax.ShapeDtypeStruct((count, SLOTS, 2 * WINDOW), BF16),
            jax.ShapeDtypeStruct((rows, chunks, g_rows, 128), F32),
            jax.ShapeDtypeStruct((TAPS + 2, features), F32),
        ),
        in_specs=[SMEM, SMEM, VMEM, VMEM, VMEM, VMEM, VMEM, VMEM, VMEM],
        out_specs=(VMEM, VMEM, VMEM, VMEM),
        scratch_shapes=[
            pltpu.VMEM((rows, x_rows, features), BF16),
            pltpu.VMEM((chunks, 72, 128), F32),
            pltpu.VMEM((rows, chunks, 96, 128), BF16),
            pltpu.VMEM((2, count // 2, 8, 128), F32),
            pltpu.VMEM((2, count, 8, 128), F32),
            pltpu.VMEM((count // 2, 8, 128), F32),
            pltpu.VMEM((TAPS * SLOTS, 2 * WINDOW), BF16),
            pltpu.VMEM((TAPS * SLOTS, 2 * WINDOW), BF16),
            pltpu.VMEM((2, SLOTS, 128), F32),
            pltpu.VMEM((2, 2, 8, 128), F32),
            pltpu.VMEM((2, 8, features), F32),
            pltpu.VMEM((TAPS + 2, 8, features), F32),
        ],
        compiler_params=pltpu.CompilerParams(vmem_limit_bytes=28 * 1024 * 1024),
        cost_estimate=pl.CostEstimate(
            flops=2 * count * SLOTS * WINDOW * features * 12,
            bytes_accessed=8 * inputs.size,
            transcendentals=0,
        ),
    )(base, lengths, inputs, cotangent, high, low, near, far, params)


def backward(r, base, lengths, shape, matrices, padded, outputs, params, grown):
    rows, length, features = shape
    half = length // 2
    chunks = features // 128
    tiles, x_rows, g_rows = sizes_of(length, half)
    shapes = (rows, length, half, features, tiles)
    operands = [base, lengths, matrices, padded, outputs, params]
    in_specs = [SMEM, SMEM, VMEM, VMEM, VMEM, VMEM]
    if grown is not None:
        operands.extend(grown)
        in_specs.extend([HBM, HBM])
    return pl.pallas_call(
        functools.partial(backward_kernel, shapes, r),
        out_shape=(
            jax.ShapeDtypeStruct((rows, half, features), BF16),
            jax.ShapeDtypeStruct(shape, BF16),
        ),
        in_specs=in_specs,
        out_specs=(HBM, HBM),
        scratch_shapes=[
            pltpu.VMEM((half, features), BF16),
            pltpu.VMEM((chunks, x_rows, 128), F32),
            pltpu.VMEM((length, features), BF16),
            pltpu.SemaphoreType.DMA((3,)),
        ],
        input_output_aliases={} if grown is None else {6: 0, 7: 1},
        compiler_params=pltpu.CompilerParams(vmem_limit_bytes=12 * 1024 * 1024),
        cost_estimate=pl.CostEstimate(
            flops=2 * tiles * SLOTS * WINDOW * features * 4,
            bytes_accessed=4 * length * features,
            transcendentals=0,
        ),
    )(*operands)


def update_kernel(
    grad_ref, other_ref, par_ref, first_ref, second_ref, norm_ref, new_ref, new_first_ref, new_second_ref
):
    grads = grad_ref[...] + other_ref[...]
    norm = jnp.sqrt(jnp.sum(grads * grads, keepdims=True))
    norm_ref[...] = norm
    grads = grads * jnp.minimum(1.0, clip_limit / (norm + 1e-06))
    weights = par_ref[...]
    first_new = beta_one * first_ref[...] + (1.0 - beta_one) * grads
    second_new = beta_two * second_ref[...] + (1.0 - beta_two) * grads * grads
    first_hat = first_new / (1.0 - beta_one**STEP)
    second_hat = second_new / (1.0 - beta_two**STEP)
    new_ref[...] = weights - learn_rate * (
        first_hat / (jnp.sqrt(second_hat) + adam_eps) + decay_rate * weights
    )
    new_first_ref[...] = first_new
    new_second_ref[...] = second_new


def update(grads, other, weights, first_old, second_old):
    like = jax.ShapeDtypeStruct(weights.shape, F32)
    return pl.pallas_call(
        update_kernel,
        out_shape=(jax.ShapeDtypeStruct((1, 1), F32), like, like, like),
        in_specs=[VMEM] * 5,
        out_specs=(VMEM,) * 4,
        compiler_params=pltpu.CompilerParams(vmem_limit_bytes=4 * 1024 * 1024),
    )(grads, other, weights, first_old, second_old)


def rounds_of(axes):
    rounds = []
    for axis in axes:
        count = lax.axis_size(axis)
        step = 1
        while step < count:
            rounds.append((axis, [(i, i ^ step) for i in range(count)]))
            step *= 2
    return rounds


def per_device(inputs, lengths, params, first_moment, second_moment, cotangent):
    rows_here, length_here, _ = inputs.shape
    base = (lax.axis_index("group") * length_here).astype(jnp.int32).reshape(1)
    near, far = packed(base, inputs, cotangent)
    far = lax.ppermute(far, "group", pairs_of("group", 1))
    near = lax.ppermute(near, "group", pairs_of("group", 0))
    high, low = convolved(base, lengths, inputs, params)
    outputs, matrices, padded, grad_params = forward(
        base, lengths, inputs, cotangent, high, low, near, far, params
    )

    def backward_row(row, matrices, grown):
        return backward(row, base, lengths, inputs.shape, matrices, padded, outputs, params, grown)

    grown = None
    row = 0
    received = None
    for axis, exchange in rounds_of(("group", "rows")):
        if received is not None:
            grad_params = grad_params + received
            if row < rows_here:
                matrices, grad_params = lax.optimization_barrier((matrices, grad_params))
                grown = backward_row(row, matrices, grown)
                received = lax.ppermute(grad_params, axis, exchange)
                received, grown = lax.optimization_barrier((received, grown))
                row += 1
                continue
        received = lax.ppermute(grad_params, axis, exchange)
    while row < rows_here:
        grown = backward_row(row, matrices, grown)
        row += 1
    output, grad_inputs = grown
    grad_norm, new_params, new_first, new_second = update(
        grad_params, received, params, first_moment, second_moment
    )
    grad_norm = grad_norm.reshape(())
    return (output, grad_inputs, grad_norm, new_params, new_first, new_second)


def solution(mesh):
    in_specs = (P("rows", "group", None), P("rows", None), P(), P(), P(), P("rows", "group", None))
    out_specs = (P("rows", "group", None), P("rows", "group", None), P(), P(), P(), P())
    return jax.shard_map(
        per_device, mesh=mesh, in_specs=in_specs, out_specs=out_specs, check_vma=False
    )
```

```python
import functools

import jax
import jax.numpy as jnp
from jax import lax
from jax.experimental import pallas as pl
from jax.experimental.pallas import tpu as pltpu
from jax.sharding import PartitionSpec as P

STEP = 10


beta_one = 0.9
beta_two = 0.999
learn_rate = 0.2
decay_rate = 0.01
adam_eps = 1e-08
clip_limit = 1.0

TAPS = 4
SLOTS = 64
PACK_LIMIT = 53 * 1024 * 1024
OWN = 56
LEAD = 4
WINDOW = 128
PAD = 16
F32 = jnp.float32
BF16 = jnp.bfloat16


def pairs_of(axis, first):
    count = lax.axis_size(axis)
    pairs = [(i, i + 1) for i in range(first, count - 1, 2)]
    return pairs + [(j, i) for i, j in pairs]


def rotate_rows(x, amount):
    for bit in (1, 2, 4):
        x = jnp.where((amount & bit) != 0, pltpu.roll(x, 8 - bit, x.ndim - 2), x)
    return x


def split(x):
    high = x.astype(BF16)
    return high, (x - high.astype(F32)).astype(BF16)


def iota(shape, dim):
    return lax.broadcasted_iota(jnp.int32, shape, dim)


def ends_of(len_ref, r):
    one = len_ref[r, 0]
    two = one + len_ref[r, 1]
    three = two + len_ref[r, 2]
    return one, two, three, three + len_ref[r, 3]


def begin_of(at, ends):
    begin = jnp.where(at >= ends[0], ends[0], 0)
    begin = jnp.where(at >= ends[1], ends[1], begin)
    return jnp.where(at >= ends[2], ends[2], begin)


def end_of(at, ends):
    end = jnp.where(at >= ends[0], ends[1], ends[0])
    end = jnp.where(at >= ends[1], ends[2], end)
    return jnp.where(at >= ends[2], ends[3], end)


def lanes_of(c):
    return slice(128 * c, 128 * c + 128)


def pack_kernel(base_ref, x_hbm, g_hbm, near_ref, far_ref, x_first, x_last, g_first, g_last, sems):
    rows, length, features = x_hbm.shape
    half = g_hbm.shape[1]
    copies = [
        pltpu.make_async_copy(x_hbm.at[:, pl.ds(length - PAD, PAD), :], x_last, sems.at[0]),
        pltpu.make_async_copy(g_hbm.at[:, pl.ds(half - PAD, PAD), :], g_last, sems.at[1]),
        pltpu.make_async_copy(x_hbm.at[:, pl.ds(0, PAD), :], x_first, sems.at[2]),
        pltpu.make_async_copy(g_hbm.at[:, pl.ds(0, PAD), :], g_first, sems.at[3]),
    ]
    for copy in copies:
        copy.start()
    even = (base_ref[0] // length) % 2 == 0
    sub = iota((PAD, features), 0)
    for copy in copies:
        copy.wait()
    for r in range(rows):
        moved = pltpu.roll(g_last[r].astype(F32), 2, 0)
        last = jnp.where(sub < 2, moved, x_last[r].astype(F32))
        moved = pltpu.roll(g_first[r].astype(F32), PAD - 3, 0)
        first = jnp.where(sub < PAD - 3, x_first[r].astype(F32), moved)
        near_ref[r] = jnp.where(even, last, first).astype(BF16)
        far_ref[r] = jnp.where(even, first, last).astype(BF16)


def convolve_block(base, ends, par_ref, load, at, place_high, place_low, masked=True):
    chunks = par_ref.shape[1] // 128
    sub8 = iota((8, 128), 0)
    keeps = []
    for j in range(2 if masked else 0):
        position = base - PAD + at + 8 * j + sub8
        offset = position - begin_of(position, ends)
        keeps.append([offset >= k for k in range(TAPS)])
    for c in range(chunks):
        lanes = lanes_of(c)
        parts = []
        for j in range(2):
            value = par_ref[4:5, lanes] + par_ref[0:1, lanes] * load(c, 8 * j)
            for k in range(1, TAPS):
                shifted = load(c, 8 * j - k)
                if masked:
                    shifted = jnp.where(keeps[j][k], shifted, 0.0)
                value = value + par_ref[k : k + 1, lanes] * shifted
            parts.append(value)
        high, low = split(jnp.concatenate(parts, axis=0))
        place_high(c, high)
        place_low(c, low)


def conv_kernel(shapes, base_ref, len_hbm, x_ref, par_ref, high_ref, low_ref, xf, len_ref, sem):
    rows, length, half, features, tiles = shapes
    chunks = features // 128
    base = base_ref[0]
    step = 64
    copy_len = pltpu.make_async_copy(len_hbm, len_ref, sem.at[0])
    copy_len.start()
    begin = 2 * PAD + length
    rest = high_ref.shape[2] - begin
    for r in range(rows):
        for c in range(chunks):
            xf[r, c, 0:8, :] = jnp.zeros((8, 128), F32)
            if rest > 0:
                for ref in (high_ref, low_ref):
                    ref[r, c, begin:, :] = jnp.zeros((rest, 128), BF16)

    def widen(i, _):
        r = i // (length // step)
        at = pl.multiple_of((i % (length // step)) * step, step)
        for c in range(chunks):
            xf[r, c, pl.ds(at + 8, step), :] = x_ref[r, pl.ds(at, step), lanes_of(c)].astype(F32)
        return 0

    lax.fori_loop(0, rows * (length // step), widen, 0)
    copy_len.wait()

    def one_row(r, _):
        ends = ends_of(len_ref, r)

        def blocks(at, masked):
            for b in range(step // 16):

                def put(ref):
                    def store(c, value):
                        ref[r, c, pl.ds(at + PAD + 16 * b, 16), :] = value

                    return store

                convolve_block(
                    base,
                    ends,
                    par_ref,
                    lambda c, shift: xf[r, c, pl.ds(at + 8 + 16 * b + shift, 8), :],
                    at + PAD + 16 * b,
                    put(high_ref),
                    put(low_ref),
                    masked,
                )

        def one_step(i, _):
            at = pl.multiple_of(i * step, step)
            reach = [(end > base + at - TAPS + 1) & (end < base + at + step) for end in ends]
            starts = functools.reduce(jnp.logical_or, reach)

            @pl.when(starts)
            def _():
                blocks(at, True)

            @pl.when(jnp.logical_not(starts))
            def _():
                blocks(at, False)

            return 0

        lax.fori_loop(0, length // step, one_step, 0)
        return 0

    lax.fori_loop(0, rows, one_row, 0)


def forward_kernel(
    shapes,
    base_ref,
    len_hbm,
    x_ref,
    g_ref,
    high_ref,
    low_ref,
    near_ref,
    far_ref,
    par_ref,
    out32,
    mat,
    g32,
    grad_ref,
    xb,
    xf,
    edge,
    comp,
    cs,
    es,
    fac_a,
    fac_b,
    tot,
    rows_e_ref,
    carry_o,
    acc,
    len_ref,
    sem,
):
    rows, length, half, features, tiles = shapes
    pairs = rows * tiles // 2
    chunks = features // 128
    base = base_ref[0]
    copy_len = pltpu.make_async_copy(len_hbm, len_ref, sem.at[0])
    copy_len.start()

    sub8 = iota((8, 128), 0)
    lane8 = iota((8, 128), 1)
    slot8 = lane8 % SLOTS
    left = lane8 < SLOTS
    delta = sub8 - 3
    first = [2 * slot8 - 3 - (2 * p + lane8 // SLOTS) for p in range(2)]
    group_of = [(f + ((sub8 - f) & 7)) >> 3 for f in first]
    turn = [f & 7 for f in first]
    first_e = 2 * slot8 - 3
    group_of_e = (first_e + ((sub8 - first_e) & 7)) >> 3
    turn_e = first_e & 7

    def place(pair, side):
        r, m = 2 * (pair // tiles) + side, pair % tiles
        return r, m, r * tiles + m

    def tile_start(m):
        return base + 2 * OWN * m - PAD

    acc[...] = jnp.zeros_like(acc)
    carry_o[...] = jnp.zeros_like(carry_o)

    for r in range(rows):
        for c in range(chunks):
            g32[r, c, PAD : PAD + half, :] = g_ref[r, :, lanes_of(c)].astype(F32)

    scorer_high = [par_ref[5:6, lanes_of(c)].astype(BF16).astype(F32) for c in range(chunks)]
    scorer_low = [par_ref[5:6, lanes_of(c)] - scorer_high[c] for c in range(chunks)]

    def held_rows(r, m, c):
        parts = []
        at = 2 * OWN * m
        for ref, own in ((high_ref, 0), (low_ref, 48)):
            begin = 0
            if m == 0:
                parts.append(edge[r, c, own : own + 32, :])
                begin = 32
            if m == tiles - 1:
                end = PAD + length - at
                parts.append(ref[r, c, at + begin : at + end, :])
                parts.append(edge[r, c, own + 32 : own + 48, :])
                begin = end + 16
            if begin < WINDOW:
                parts.append(ref[r, c, at + begin : at + WINDOW, :])
        return jnp.concatenate(parts, axis=0)

    def multiply(pair):
        dots, scores = [], []
        for side in range(2):
            r, m, _ = place(pair, side)
            start = OWN * m + 8
            streamed, held = [], []
            for c in range(chunks):
                g = g32[r, c, start : start + SLOTS, :]
                top = jnp.where(sub8 == 0, scorer_high[c], jnp.where(sub8 == 1, scorer_low[c], g[0:8]))
                streamed.append(jnp.concatenate([top, g[8:]], axis=0).astype(BF16))
                held.append(held_rows(r, m, c))
            product = lax.dot_general(
                jnp.concatenate(streamed, axis=1),
                jnp.concatenate(held, axis=1),
                (((1,), (1,)), ((), ())),
                preferred_element_type=F32,
            )
            product = product[:, :WINDOW] + product[:, WINDOW:]
            dots.append(product)
            scores.append(jnp.broadcast_to(product[0:1] + product[1:2], (SLOTS, WINDOW)))
        dots = jnp.concatenate(dots, axis=0).T
        scores = jnp.concatenate(scores, axis=0).T
        banded = jnp.zeros((8, 128), F32)
        scored = jnp.zeros((8, 128), F32)
        for v in range(WINDOW // 8):
            here = group_of_e == v
            banded = jnp.where(here, dots[8 * v : 8 * v + 8], banded)
            scored = jnp.where(here, scores[8 * v : 8 * v + 8], scored)
        comp[0, pair] = banded
        comp[1, pair] = scored

    inner = [pair for pair in range(pairs) if 0 < pair % tiles < tiles - 1]
    for pair in inner:
        multiply(pair)

    copy_len.wait()
    subd = iota((8, features), 0)
    even = (base // length) % 2 == 0
    for r in range(rows):
        near = near_ref[r].astype(F32)
        far = far_ref[r].astype(F32)
        up = jnp.where(even, far, near)
        down = jnp.where(even, near, far)
        xb[r, 0:PAD, :] = up.astype(BF16)
        xb[r, PAD + length : 2 * PAD + length, :] = down.astype(BF16)
        rest = xb.shape[1] - 2 * PAD - length
        if rest > 0:
            xb[r, 2 * PAD + length :, :] = jnp.zeros((rest, features), BF16)
        xb[r, PAD : PAD + length, :] = x_ref[r]
        before = jnp.where(subd >= 6, pltpu.roll(up[0:8], 6, 0), 0.0)
        after = jnp.where(subd < 3, pltpu.roll(down[8:16], 3, 0), 0.0)
        rest = g32.shape[2] - PAD - half - 8
        for c in range(chunks):
            g32[r, c, 8:16, :] = before[:, lanes_of(c)]
            g32[r, c, PAD + half : PAD + half + 8, :] = after[:, lanes_of(c)]
            g32[r, c, PAD + half + 8 :, :] = jnp.zeros((rest, 128), F32)
        for c in range(chunks):
            lanes = lanes_of(c)
            xf[c, 0:8, :] = jnp.zeros((8, 128), F32)
            xf[c, 8:24, :] = up[:, lanes]
            xf[c, 24:40, :] = x_ref[r, 0:16, lanes].astype(F32)
            xf[c, 40:56, :] = x_ref[r, length - 16 : length, lanes].astype(F32)
            xf[c, 56:72, :] = down[:, lanes]
        ends = ends_of(len_ref, r)
        for at, where, slot in ((0, 8, 0), (PAD, 24, 16), (PAD + length, 56, 32)):

            def put(first):
                def store(c, value):
                    edge[r, c, first : first + 16, :] = value

                return store

            convolve_block(
                base,
                ends,
                par_ref,
                lambda c, shift: xf[c, where + shift : where + shift + 8, :],
                at,
                put(slot),
                put(48 + slot),
            )

    for pair in range(pairs):
        if pair not in inner:
            multiply(pair)

    ends = [ends_of(len_ref, r) for r in range(rows)]
    for pair in range(pairs):
        both = [place(pair, side) for side in range(2)]
        dots = rotate_rows(comp[0, pair], turn_e)
        scores = rotate_rows(comp[1, pair], turn_e)
        coef = jnp.zeros((8, 128), F32)
        coef_e = jnp.zeros((8, 128), F32)
        for p in range(2):
            at = tile_start(both[0][1]) + 2 * slot8 + p
            begin = [begin_of(at, ends[r]) for r, _, _ in both]
            end = [end_of(at, ends[r]) for r, _, _ in both]
            offset = jnp.maximum(at - jnp.where(left, begin[0], begin[1]), 0)
            remain = jnp.where(left, end[0], end[1]) - at
            masks, inverses, logits, grads = [], [], [], []
            for b in range(1, TAPS + 1):
                if b == 3:
                    thirds = ((offset.astype(F32) + 0.5) * (1.0 / 3.0)).astype(jnp.int32)
                    within = offset - 3 * thirds
                else:
                    within = offset & (b - 1)
                upper = jnp.minimum(b - within, remain)
                mask = (delta >= p - within) & (delta < p + upper)
                inverse = 1.0 / jnp.maximum(within + upper, 1).astype(F32)
                masks.append(mask)
                inverses.append(inverse)
                logits.append(jnp.sum(jnp.where(mask, scores, 0.0), axis=0, keepdims=True) * inverse)
                grads.append(
                    jnp.sum(jnp.where(mask, dots, 0.0), axis=0, keepdims=True) * (0.5 * inverse)
                )
            largest = functools.reduce(jnp.maximum, logits)
            powers = [jnp.exp(logit - largest) for logit in logits]
            scale = 1.0 / sum(powers)
            shares = [power * scale for power in powers]
            mean = sum(share * grad for share, grad in zip(shares, grads))
            for mask, inverse, share, grad in zip(masks, inverses, shares, grads):
                coef = coef + jnp.where(mask, (0.5 * share) * inverse, 0.0)
                coef_e = coef_e + jnp.where(mask, share * (grad - mean) * inverse, 0.0)
        owned = (slot8 >= LEAD) & (slot8 < LEAD + OWN)
        coef = jnp.where(owned, coef, 0.0)
        coef_e = jnp.where(owned, coef_e, 0.0)
        es[pair] = rotate_rows(coef_e, (8 - turn_e) & 7)
        swapped = pltpu.roll(coef, SLOTS, 1)
        for side, (r, m, tile) in enumerate(both):
            at = tile_start(m) + 2 * slot8 + delta
            offset = at - begin_of(at, ends[r])
            alone = jnp.where(left, coef, swapped) if side == 0 else jnp.where(left, swapped, coef)
            for p in range(2):
                kept = jnp.where((offset >= 2 * p + lane8 // SLOTS) & (at >= 0), alone, 0.0)
                cs[p, tile] = rotate_rows(kept, (8 - turn[p]) & 7)

    slots_down = iota((SLOTS, 128), 0)
    wide = 2 if chunks % 2 == 0 else 1
    factors = (fac_a, fac_b)

    def spread_pair(pair):
        spread = jnp.concatenate(
            [jnp.where(group_of_e == v, es[pair], 0.0) for v in range(WINDOW // 8)], axis=0
        ).T
        for side in range(2):
            _, m, _ = place(pair, side)
            from_row = OWN * m - 8
            part = spread[SLOTS * side : SLOTS * side + SLOTS]
            here = (from_row + slots_down >= 0) & (from_row + slots_down < half)
            own_e = jnp.sum(jnp.where(here, part, 0.0), axis=0, keepdims=True)
            all_e = jnp.sum(part, axis=0, keepdims=True)
            rows_e_ref[side, 0] = jnp.broadcast_to(own_e, (8, 128))
            rows_e_ref[side, 1] = jnp.broadcast_to(all_e, (8, 128))

    def build(pair, side):
        r, m, tile = place(pair, side)
        own_e = rows_e_ref[side, 0]
        all_e = rows_e_ref[side, 1]
        from_row = OWN * m - 8
        mine = [
            (from_row + 8 * i + sub8 >= 0) & (from_row + 8 * i + sub8 < half) for i in range(SLOTS // 8)
        ]
        at = tile_start(m) + lane8
        offset = at - begin_of(at, ends_of(len_ref, r))
        bands = []
        for p in range(2):
            bands.append(
                jnp.concatenate(
                    [jnp.where(group_of[p] == v, cs[p, tile], 0.0) for v in range(WINDOW // 8)], axis=0
                ).T
            )
        for k in range(TAPS):
            row_k = jnp.where((offset >= k) & (at >= 0), own_e, 0.0)
            if k > 0:
                row_k = pltpu.roll(row_k, 128 - k, 1)
            matrix = bands[k // 2][SLOTS * (k % 2) : SLOTS * (k % 2) + SLOTS]
            if k == 0:
                back = jnp.concatenate([jnp.where(sub8 < 2, all_e, matrix[0:8]), matrix[8:]], axis=0)
                high, low = split(back)
                mat[tile, :, 0:WINDOW] = high
                mat[tile, :, WINDOW:] = low
            parts = [jnp.where(mine[i], matrix[8 * i : 8 * i + 8], 0.0) for i in range(SLOTS // 8)]
            parts[0] = jnp.where(sub8 == 0, row_k, parts[0])
            matrix = jnp.concatenate(parts, axis=0)
            if k == 0:
                total = jnp.sum(matrix, axis=1, keepdims=True)
                tot[side] = jnp.broadcast_to(total, (SLOTS, 128))
            high, low = split(matrix)
            factors[side][SLOTS * k : SLOTS * (k + 1), 0:WINDOW] = high
            factors[side][SLOTS * k : SLOTS * (k + 1), WINDOW:] = low

    def apply(pair, side):
        r, m, _ = place(pair, side)
        start = pl.multiple_of(OWN * m + 8, 8)
        window = pl.multiple_of(2 * OWN * m, 16)
        factor = factors[side][...]
        total = tot[side]
        for w in range(chunks // wide):
            x = xb[r, pl.ds(window, WINDOW), 128 * wide * w : 128 * wide * (w + 1)]
            mixed = lax.dot_general(
                factor,
                jnp.concatenate([x, x], axis=0),
                (((1,), (0,)), ((), ())),
                preferred_element_type=F32,
            )
            for i in range(wide):
                c = wide * w + i
                lanes = lanes_of(c)
                g = g32[r, c, pl.ds(start, SLOTS), :]
                g = jnp.concatenate([jnp.where(sub8 == 0, par_ref[5:6, lanes], g[0:8]), g[8:]], axis=0)
                value = total * par_ref[4:5, lanes]
                for k in range(TAPS):
                    taken = mixed[SLOTS * k : SLOTS * (k + 1), lanes_of(i)]
                    value = value + taken * par_ref[k : k + 1, lanes]
                    acc[k, :, lanes] += jnp.sum((taken * g).reshape(SLOTS // 8, 8, 128), axis=0)
                acc[4, :, lanes] += jnp.sum((total * g).reshape(SLOTS // 8, 8, 128), axis=0)
                acc[5, :, lanes] += jnp.where(sub8 == 0, value[0:8], 0.0)
                top = carry_o[side, :, lanes] + jnp.where(sub8 < LEAD, 0.0, value[0:8])
                out32[r, c, pl.ds(start, 8), :] = top
                out32[r, c, pl.ds(start + 8, OWN - 8), :] = value[8:OWN]
                carry_o[side, :, lanes] = jnp.where(m < tiles - 1, value[OWN:], 0.0)

    spread_pair(0)
    build(0, 0)
    build(0, 1)

    def one_pair(pair):
        spread_pair(pair + 1)
        for side in range(2):
            apply(pair, side)
            build(pair + 1, side)

    together = 2

    def second_loop(i, _):
        for j in range(together):
            one_pair(together * i + j)
        return 0

    lax.fori_loop(0, (pairs - 1) // together, second_loop, 0)
    for pair in range((pairs - 1) // together * together, pairs - 1):
        one_pair(pair)
    apply(pairs - 1, 0)
    apply(pairs - 1, 1)
    for k in range(TAPS + 2):
        grad_ref[k : k + 1, :] = jnp.sum(acc[k], axis=0, keepdims=True)


def backward_kernel(shapes, r, base_ref, len_ref, mat, g32, out32, par_ref, *refs):
    out_hbm, gin_hbm, outb, dc, ginb, sems = refs[-6:]
    rows, length, half, features, tiles = shapes
    chunks = features // 128
    wide = 2 if chunks % 2 == 0 else 1
    base = base_ref[0]
    sub8 = iota((8, 128), 0)
    ends = ends_of(len_ref, r)
    for c in range(chunks):
        outb[:, lanes_of(c)] = out32[r, c, PAD : PAD + half, :].astype(BF16)
    copies = [pltpu.make_async_copy(outb, out_hbm.at[r], sems.at[2])]
    copies[0].start()

    for m in range(tiles):
        tile = r * tiles + m
        streamed = jnp.concatenate([mat[tile, :, 0:WINDOW].T, mat[tile, :, WINDOW:].T], axis=1)
        at = 2 * OWN * m
        for w in range(chunks // wide):
            held = []
            for i in range(wide):
                lanes = lanes_of(wide * w + i)
                scorer = par_ref[5:6, lanes]
                scorer_high = scorer.astype(BF16).astype(F32)
                g = g32[r, wide * w + i, OWN * m + 8 : OWN * m + 8 + SLOTS, :]
                top = jnp.where(
                    sub8 == 0, scorer_high, jnp.where(sub8 == 1, scorer - scorer_high, g[0:8])
                )
                held.append(jnp.concatenate([top, g[8:]], axis=0).astype(BF16))
            held = jnp.concatenate(held, axis=1)
            part = lax.dot_general(
                streamed,
                jnp.concatenate([held, held], axis=0),
                (((1,), (0,)), ((), ())),
                preferred_element_type=F32,
            )
            for i in range(wide):
                c = wide * w + i
                before = dc[c, at : at + PAD, :] if m > 0 else 0.0
                dc[c, at : at + PAD, :] = before + part[0:PAD, lanes_of(i)]
                dc[c, at + PAD : at + WINDOW, :] = part[PAD:, lanes_of(i)]

    def taps_at(at, masked):
        keeps = []
        if masked:
            for j in range(4):
                position = base + at + 8 * j + sub8
                remain = end_of(position, ends) - position
                keeps.append([remain > k for k in range(TAPS)])
        for c in range(chunks):
            parts = []
            for j in range(4):
                value = par_ref[0:1, lanes_of(c)] * dc[c, pl.ds(at + PAD + 8 * j, 8), :]
                for k in range(1, TAPS):
                    shifted = dc[c, pl.ds(at + PAD + 8 * j + k, 8), :]
                    if masked:
                        shifted = jnp.where(keeps[j][k], shifted, 0.0)
                    value = value + par_ref[k : k + 1, lanes_of(c)] * shifted
                parts.append(value)
            ginb[pl.ds(at, 32), lanes_of(c)] = jnp.concatenate(parts, axis=0).astype(BF16)

    def taps(i, _):
        at = pl.multiple_of(i * 32, 32)
        reach = [(end > base + at) & (end <= base + at + 32 + TAPS - 2) for end in ends]
        crosses = functools.reduce(jnp.logical_or, reach)

        @pl.when(crosses)
        def _():
            taps_at(at, True)

        @pl.when(jnp.logical_not(crosses))
        def _():
            taps_at(at, False)

        return 0

    pieces = 2
    for piece in range(pieces):
        size = length // pieces
        lax.fori_loop(piece * size // 32, (piece + 1) * size // 32, taps, 0)
        copies.append(
            pltpu.make_async_copy(
                ginb.at[pl.ds(piece * size, size), :],
                gin_hbm.at[r, pl.ds(piece * size, size), :],
                sems.at[piece],
            )
        )
        copies[-1].start()
    for copy in copies:
        copy.wait()


SMEM = pl.BlockSpec(memory_space=pltpu.SMEM)
VMEM = pl.BlockSpec(memory_space=pltpu.VMEM)
HBM = pl.BlockSpec(memory_space=pltpu.HBM)


def sizes_of(length, half):
    tiles = -(-(half + 3 + LEAD) // OWN)
    x_rows = 2 * OWN * (tiles - 1) + WINDOW
    g_rows = -(-(OWN * (tiles - 1) + 8 + SLOTS) // 16) * 16
    return tiles, x_rows, g_rows


def packed(base, inputs, cotangent):
    rows, _, features = inputs.shape
    part = jax.ShapeDtypeStruct((rows, PAD, features), BF16)
    return pl.pallas_call(
        pack_kernel,
        out_shape=(part, part),
        in_specs=[SMEM, HBM, HBM],
        out_specs=(VMEM, VMEM),
        scratch_shapes=[pltpu.VMEM((rows, PAD, features), BF16)] * 4 + [pltpu.SemaphoreType.DMA((4,))],
        compiler_params=pltpu.CompilerParams(vmem_limit_bytes=PACK_LIMIT),
    )(base, inputs, cotangent)


def convolved(base, lengths, inputs, params):
    rows, length, features = inputs.shape
    half = length // 2
    chunks = features // 128
    tiles, x_rows, _ = sizes_of(length, half)
    shapes = (rows, length, half, features, tiles)
    part = jax.ShapeDtypeStruct((rows, chunks, x_rows, 128), BF16)
    return pl.pallas_call(
        functools.partial(conv_kernel, shapes),
        out_shape=(part, part),
        in_specs=[SMEM, HBM, VMEM, VMEM],
        out_specs=(VMEM, VMEM),
        scratch_shapes=[
            pltpu.VMEM((rows, chunks, 8 + length, 128), F32),
            pltpu.SMEM(lengths.shape, jnp.int32),
            pltpu.SemaphoreType.DMA((1,)),
        ],
        compiler_params=pltpu.CompilerParams(vmem_limit_bytes=24 * 1024 * 1024),
        cost_estimate=pl.CostEstimate(
            flops=24 * inputs.size, bytes_accessed=8 * inputs.size, transcendentals=0
        ),
    )(base, lengths, inputs, params)


def forward(base, lengths, inputs, cotangent, high, low, near, far, params):
    rows, half, features = cotangent.shape
    length = 2 * half
    chunks = features // 128
    tiles, x_rows, g_rows = sizes_of(length, half)
    count = rows * tiles
    shapes = (rows, length, half, features, tiles)
    return pl.pallas_call(
        functools.partial(forward_kernel, shapes),
        out_shape=(
            jax.ShapeDtypeStruct((rows, chunks, g_rows, 128), F32),
            jax.ShapeDtypeStruct((count, SLOTS, 2 * WINDOW), BF16),
            jax.ShapeDtypeStruct((rows, chunks, g_rows, 128), F32),
            jax.ShapeDtypeStruct((TAPS + 2, features), F32),
        ),
        in_specs=[SMEM, HBM, VMEM, VMEM, VMEM, VMEM, VMEM, VMEM, VMEM],
        out_specs=(VMEM, VMEM, VMEM, VMEM),
        scratch_shapes=[
            pltpu.VMEM((rows, x_rows, features), BF16),
            pltpu.VMEM((chunks, 72, 128), F32),
            pltpu.VMEM((rows, chunks, 96, 128), BF16),
            pltpu.VMEM((2, count // 2, 8, 128), F32),
            pltpu.VMEM((2, count, 8, 128), F32),
            pltpu.VMEM((count // 2, 8, 128), F32),
            pltpu.VMEM((TAPS * SLOTS, 2 * WINDOW), BF16),
            pltpu.VMEM((TAPS * SLOTS, 2 * WINDOW), BF16),
            pltpu.VMEM((2, SLOTS, 128), F32),
            pltpu.VMEM((2, 2, 8, 128), F32),
            pltpu.VMEM((2, 8, features), F32),
            pltpu.VMEM((TAPS + 2, 8, features), F32),
            pltpu.SMEM(lengths.shape, jnp.int32),
            pltpu.SemaphoreType.DMA((1,)),
        ],
        compiler_params=pltpu.CompilerParams(vmem_limit_bytes=28 * 1024 * 1024),
        cost_estimate=pl.CostEstimate(
            flops=2 * count * SLOTS * WINDOW * features * 12,
            bytes_accessed=8 * inputs.size,
            transcendentals=0,
        ),
    )(base, lengths, inputs, cotangent, high, low, near, far, params)


def backward(r, base, lengths, shape, matrices, padded, outputs, params, grown):
    rows, length, features = shape
    half = length // 2
    chunks = features // 128
    tiles, x_rows, g_rows = sizes_of(length, half)
    shapes = (rows, length, half, features, tiles)
    operands = [base, lengths, matrices, padded, outputs, params]
    in_specs = [SMEM, SMEM, VMEM, VMEM, VMEM, VMEM]
    if grown is not None:
        operands.extend(grown)
        in_specs.extend([HBM, HBM])
    return pl.pallas_call(
        functools.partial(backward_kernel, shapes, r),
        out_shape=(
            jax.ShapeDtypeStruct((rows, half, features), BF16),
            jax.ShapeDtypeStruct(shape, BF16),
        ),
        in_specs=in_specs,
        out_specs=(HBM, HBM),
        scratch_shapes=[
            pltpu.VMEM((half, features), BF16),
            pltpu.VMEM((chunks, x_rows, 128), F32),
            pltpu.VMEM((length, features), BF16),
            pltpu.SemaphoreType.DMA((3,)),
        ],
        input_output_aliases={} if grown is None else {6: 0, 7: 1},
        compiler_params=pltpu.CompilerParams(vmem_limit_bytes=12 * 1024 * 1024),
        cost_estimate=pl.CostEstimate(
            flops=2 * tiles * SLOTS * WINDOW * features * 4,
            bytes_accessed=4 * length * features,
            transcendentals=0,
        ),
    )(*operands)


def update_kernel(
    grad_ref, other_ref, par_ref, first_ref, second_ref, norm_ref, new_ref, new_first_ref, new_second_ref
):
    grads = grad_ref[...] + other_ref[...]
    norm = jnp.sqrt(jnp.sum(grads * grads, keepdims=True))
    norm_ref[...] = norm
    grads = grads * jnp.minimum(1.0, clip_limit / (norm + 1e-06))
    weights = par_ref[...]
    first_new = beta_one * first_ref[...] + (1.0 - beta_one) * grads
    second_new = beta_two * second_ref[...] + (1.0 - beta_two) * grads * grads
    first_hat = first_new / (1.0 - beta_one**STEP)
    second_hat = second_new / (1.0 - beta_two**STEP)
    new_ref[...] = weights - learn_rate * (
        first_hat / (jnp.sqrt(second_hat) + adam_eps) + decay_rate * weights
    )
    new_first_ref[...] = first_new
    new_second_ref[...] = second_new


def update(grads, other, weights, first_old, second_old):
    like = jax.ShapeDtypeStruct(weights.shape, F32)
    return pl.pallas_call(
        update_kernel,
        out_shape=(jax.ShapeDtypeStruct((1, 1), F32), like, like, like),
        in_specs=[VMEM] * 5,
        out_specs=(VMEM,) * 4,
        compiler_params=pltpu.CompilerParams(vmem_limit_bytes=4 * 1024 * 1024),
    )(grads, other, weights, first_old, second_old)


def rounds_of(axes):
    rounds = []
    for axis in axes:
        count = lax.axis_size(axis)
        step = 1
        while step < count:
            rounds.append((axis, [(i, i ^ step) for i in range(count)]))
            step *= 2
    return rounds


def per_device(inputs, lengths, params, first_moment, second_moment, cotangent):
    rows_here, length_here, _ = inputs.shape
    base = (lax.axis_index("group") * length_here).astype(jnp.int32).reshape(1)
    near, far = packed(base, inputs, cotangent)
    far = lax.ppermute(far, "group", pairs_of("group", 1))
    near = lax.ppermute(near, "group", pairs_of("group", 0))
    high, low = convolved(base, lengths, inputs, params)
    outputs, matrices, padded, grad_params = forward(
        base, lengths, inputs, cotangent, high, low, near, far, params
    )

    def backward_row(row, matrices, grown):
        return backward(row, base, lengths, inputs.shape, matrices, padded, outputs, params, grown)

    grown = None
    row = 0
    received = None
    for axis, exchange in rounds_of(("group", "rows")):
        if received is not None:
            grad_params = grad_params + received
            if row < rows_here:
                matrices, grad_params = lax.optimization_barrier((matrices, grad_params))
                grown = backward_row(row, matrices, grown)
                received = lax.ppermute(grad_params, axis, exchange)
                received, grown = lax.optimization_barrier((received, grown))
                row += 1
                continue
        received = lax.ppermute(grad_params, axis, exchange)
    while row < rows_here:
        grown = backward_row(row, matrices, grown)
        row += 1
    output, grad_inputs = grown
    grad_norm, new_params, new_first, new_second = update(
        grad_params, received, params, first_moment, second_moment
    )
    grad_norm = grad_norm.reshape(())
    return (output, grad_inputs, grad_norm, new_params, new_first, new_second)


def solution(mesh):
    in_specs = (P("rows", "group", None), P("rows", None), P(), P(), P(), P("rows", "group", None))
    out_specs = (P("rows", "group", None), P("rows", "group", None), P(), P(), P(), P())
    return jax.shard_map(
        per_device, mesh=mesh, in_specs=in_specs, out_specs=out_specs, check_vma=False
    )
```

```python
import functools

import jax
import jax.numpy as jnp
from jax import lax
from jax.experimental import pallas as pl
from jax.experimental.pallas import tpu as pltpu
from jax.sharding import PartitionSpec as P

STEP = 10


beta_one = 0.9
beta_two = 0.999
learn_rate = 0.2
decay_rate = 0.01
adam_eps = 1e-08
clip_limit = 1.0

TAPS = 4
SLOTS = 64
PACK_LIMIT = 53 * 1024 * 1024
OWN = 56
LEAD = 4
WINDOW = 128
PAD = 16
F32 = jnp.float32
BF16 = jnp.bfloat16


def pairs_of(axis, first):
    count = lax.axis_size(axis)
    pairs = [(i, i + 1) for i in range(first, count - 1, 2)]
    return pairs + [(j, i) for i, j in pairs]


def rotate_rows(x, amount):
    for bit in (1, 2, 4):
        x = jnp.where((amount & bit) != 0, pltpu.roll(x, 8 - bit, x.ndim - 2), x)
    return x


def split(x):
    high = x.astype(BF16)
    return high, (x - high.astype(F32)).astype(BF16)


def iota(shape, dim):
    return lax.broadcasted_iota(jnp.int32, shape, dim)


def ends_of(len_ref, r):
    one = len_ref[r, 0]
    two = one + len_ref[r, 1]
    three = two + len_ref[r, 2]
    return one, two, three, three + len_ref[r, 3]


def begin_of(at, ends):
    begin = jnp.where(at >= ends[0], ends[0], 0)
    begin = jnp.where(at >= ends[1], ends[1], begin)
    return jnp.where(at >= ends[2], ends[2], begin)


def end_of(at, ends):
    end = jnp.where(at >= ends[0], ends[1], ends[0])
    end = jnp.where(at >= ends[1], ends[2], end)
    return jnp.where(at >= ends[2], ends[3], end)


def lanes_of(c):
    return slice(128 * c, 128 * c + 128)


def pack_kernel(base_ref, x_hbm, g_hbm, near_ref, far_ref, x_first, x_last, g_first, g_last, sems):
    rows, length, features = x_hbm.shape
    half = g_hbm.shape[1]
    copies = [
        pltpu.make_async_copy(x_hbm.at[:, pl.ds(length - PAD, PAD), :], x_last, sems.at[0]),
        pltpu.make_async_copy(g_hbm.at[:, pl.ds(half - PAD, PAD), :], g_last, sems.at[1]),
        pltpu.make_async_copy(x_hbm.at[:, pl.ds(0, PAD), :], x_first, sems.at[2]),
        pltpu.make_async_copy(g_hbm.at[:, pl.ds(0, PAD), :], g_first, sems.at[3]),
    ]
    for copy in copies:
        copy.start()
    even = (base_ref[0] // length) % 2 == 0
    sub = iota((PAD, features), 0)
    for copy in copies:
        copy.wait()
    for r in range(rows):
        moved = pltpu.roll(g_last[r].astype(F32), 2, 0)
        last = jnp.where(sub < 2, moved, x_last[r].astype(F32))
        moved = pltpu.roll(g_first[r].astype(F32), PAD - 3, 0)
        first = jnp.where(sub < PAD - 3, x_first[r].astype(F32), moved)
        near_ref[r] = jnp.where(even, last, first).astype(BF16)
        far_ref[r] = jnp.where(even, first, last).astype(BF16)


def convolve_block(base, ends, par_ref, load, at, place_high, place_low, masked=True):
    chunks = par_ref.shape[1] // 128
    sub8 = iota((8, 128), 0)
    keeps = []
    for j in range(2 if masked else 0):
        position = base - PAD + at + 8 * j + sub8
        offset = position - begin_of(position, ends)
        keeps.append([offset >= k for k in range(TAPS)])
    for c in range(chunks):
        lanes = lanes_of(c)
        parts = []
        for j in range(2):
            value = par_ref[0:1, lanes] * load(c, 8 * j)
            for k in range(1, TAPS):
                shifted = load(c, 8 * j - k)
                if masked:
                    shifted = jnp.where(keeps[j][k], shifted, 0.0)
                value = value + par_ref[k : k + 1, lanes] * shifted
            parts.append(value)
        high, low = split(jnp.concatenate(parts, axis=0))
        place_high(c, high)
        place_low(c, low)


def conv_kernel(shapes, base_ref, len_hbm, x_ref, par_ref, high_ref, low_ref, xf, len_ref, sem):
    rows, length, half, features, tiles = shapes
    chunks = features // 128
    base = base_ref[0]
    step = 64
    copy_len = pltpu.make_async_copy(len_hbm, len_ref, sem.at[0])
    copy_len.start()
    begin = 2 * PAD + length
    rest = high_ref.shape[2] - begin
    for r in range(rows):
        for c in range(chunks):
            xf[r, c, 0:8, :] = jnp.zeros((8, 128), F32)
            if rest > 0:
                for ref in (high_ref, low_ref):
                    ref[r, c, begin:, :] = jnp.zeros((rest, 128), BF16)

    def widen(i, _):
        r = i // (length // step)
        at = pl.multiple_of((i % (length // step)) * step, step)
        for c in range(chunks):
            xf[r, c, pl.ds(at + 8, step), :] = x_ref[r, pl.ds(at, step), lanes_of(c)].astype(F32)
        return 0

    lax.fori_loop(0, rows * (length // step), widen, 0)
    copy_len.wait()

    def one_row(r, _):
        ends = ends_of(len_ref, r)

        def blocks(at, masked):
            for b in range(step // 16):

                def put(ref):
                    def store(c, value):
                        ref[r, c, pl.ds(at + PAD + 16 * b, 16), :] = value

                    return store

                convolve_block(
                    base,
                    ends,
                    par_ref,
                    lambda c, shift: xf[r, c, pl.ds(at + 8 + 16 * b + shift, 8), :],
                    at + PAD + 16 * b,
                    put(high_ref),
                    put(low_ref),
                    masked,
                )

        def one_step(i, _):
            at = pl.multiple_of(i * step, step)
            reach = [(end > base + at - TAPS + 1) & (end < base + at + step) for end in ends]
            starts = functools.reduce(jnp.logical_or, reach)

            @pl.when(starts)
            def _():
                blocks(at, True)

            @pl.when(jnp.logical_not(starts))
            def _():
                blocks(at, False)

            return 0

        lax.fori_loop(0, length // step, one_step, 0)
        return 0

    lax.fori_loop(0, rows, one_row, 0)


def forward_kernel(
    shapes,
    base_ref,
    len_hbm,
    x_ref,
    g_ref,
    high_ref,
    low_ref,
    near_ref,
    far_ref,
    par_ref,
    out32,
    mat,
    g32,
    grad_ref,
    xb,
    xf,
    edge,
    comp,
    biases,
    cs,
    es,
    fac_a,
    fac_b,
    tot,
    rows_e_ref,
    carry_o,
    acc,
    len_ref,
    sem,
):
    rows, length, half, features, tiles = shapes
    pairs = rows * tiles // 2
    chunks = features // 128
    base = base_ref[0]
    copy_len = pltpu.make_async_copy(len_hbm, len_ref, sem.at[0])
    copy_len.start()

    sub8 = iota((8, 128), 0)
    lane8 = iota((8, 128), 1)
    slot8 = lane8 % SLOTS
    left = lane8 < SLOTS
    delta = sub8 - 3
    first = [2 * slot8 - 3 - (2 * p + lane8 // SLOTS) for p in range(2)]
    group_of = [(f + ((sub8 - f) & 7)) >> 3 for f in first]
    turn = [f & 7 for f in first]
    first_e = 2 * slot8 - 3
    group_of_e = (first_e + ((sub8 - first_e) & 7)) >> 3
    turn_e = first_e & 7

    def place(pair, side):
        r, m = 2 * (pair // tiles) + side, pair % tiles
        return r, m, r * tiles + m

    def tile_start(m):
        return base + 2 * OWN * m - PAD

    acc[...] = jnp.zeros_like(acc)
    carry_o[...] = jnp.zeros_like(carry_o)

    for r in range(rows):
        for c in range(chunks):
            g32[r, c, PAD : PAD + half, :] = g_ref[r, :, lanes_of(c)].astype(F32)

    scorer_high = [par_ref[5:6, lanes_of(c)].astype(BF16).astype(F32) for c in range(chunks)]
    scorer_low = [par_ref[5:6, lanes_of(c)] - scorer_high[c] for c in range(chunks)]

    def held_rows(r, m, c):
        parts = []
        at = 2 * OWN * m
        for ref, own in ((high_ref, 0), (low_ref, 48)):
            begin = 0
            if m == 0:
                parts.append(edge[r, c, own : own + 32, :])
                begin = 32
            if m == tiles - 1:
                end = PAD + length - at
                parts.append(ref[r, c, at + begin : at + end, :])
                parts.append(edge[r, c, own + 32 : own + 48, :])
                begin = end + 16
            if begin < WINDOW:
                parts.append(ref[r, c, at + begin : at + WINDOW, :])
        return jnp.concatenate(parts, axis=0)

    def multiply(pair):
        dots, scores, added = [], [], []
        for side in range(2):
            r, m, _ = place(pair, side)
            start = OWN * m + 8
            streamed, held = [], []
            biased = jnp.zeros((SLOTS, 128), F32)
            for c in range(chunks):
                g = g32[r, c, start : start + SLOTS, :]
                biased = biased + g * par_ref[4:5, lanes_of(c)]
                top = jnp.where(sub8 == 0, scorer_high[c], jnp.where(sub8 == 1, scorer_low[c], g[0:8]))
                streamed.append(jnp.concatenate([top, g[8:]], axis=0).astype(BF16))
                held.append(held_rows(r, m, c))
            product = lax.dot_general(
                jnp.concatenate(streamed, axis=1),
                jnp.concatenate(held, axis=1),
                (((1,), (1,)), ((), ())),
                preferred_element_type=F32,
            )
            product = product[:, :WINDOW] + product[:, WINDOW:]
            added.append(jnp.broadcast_to(jnp.sum(biased, axis=1, keepdims=True), (SLOTS, 128)))
            dots.append(product)
            scores.append(jnp.broadcast_to(product[0:1] + product[1:2], (SLOTS, WINDOW)))
        dots = jnp.concatenate(dots, axis=0).T
        scores = jnp.concatenate(scores, axis=0).T
        banded = jnp.zeros((8, 128), F32)
        scored = jnp.zeros((8, 128), F32)
        for v in range(WINDOW // 8):
            here = group_of_e == v
            banded = jnp.where(here, dots[8 * v : 8 * v + 8], banded)
            scored = jnp.where(here, scores[8 * v : 8 * v + 8], scored)
        comp[0, pair] = banded
        comp[1, pair] = scored
        biases[pair] = jnp.concatenate(added, axis=0).T[0:8]

    inner = [pair for pair in range(pairs) if 0 < pair % tiles < tiles - 1]
    for pair in inner:
        multiply(pair)

    copy_len.wait()
    subd = iota((8, features), 0)
    even = (base // length) % 2 == 0
    for r in range(rows):
        near = near_ref[r].astype(F32)
        far = far_ref[r].astype(F32)
        up = jnp.where(even, far, near)
        down = jnp.where(even, near, far)
        xb[r, 0:PAD, :] = up.astype(BF16)
        xb[r, PAD + length : 2 * PAD + length, :] = down.astype(BF16)
        rest = xb.shape[1] - 2 * PAD - length
        if rest > 0:
            xb[r, 2 * PAD + length :, :] = jnp.zeros((rest, features), BF16)
        xb[r, PAD : PAD + length, :] = x_ref[r]
        before = jnp.where(subd >= 6, pltpu.roll(up[0:8], 6, 0), 0.0)
        after = jnp.where(subd < 3, pltpu.roll(down[8:16], 3, 0), 0.0)
        rest = g32.shape[2] - PAD - half - 8
        for c in range(chunks):
            g32[r, c, 8:16, :] = before[:, lanes_of(c)]
            g32[r, c, PAD + half : PAD + half + 8, :] = after[:, lanes_of(c)]
            g32[r, c, PAD + half + 8 :, :] = jnp.zeros((rest, 128), F32)
        for c in range(chunks):
            lanes = lanes_of(c)
            xf[c, 0:8, :] = jnp.zeros((8, 128), F32)
            xf[c, 8:24, :] = up[:, lanes]
            xf[c, 24:40, :] = x_ref[r, 0:16, lanes].astype(F32)
            xf[c, 40:56, :] = x_ref[r, length - 16 : length, lanes].astype(F32)
            xf[c, 56:72, :] = down[:, lanes]
        ends = ends_of(len_ref, r)
        for at, where, slot in ((0, 8, 0), (PAD, 24, 16), (PAD + length, 56, 32)):

            def put(first):
                def store(c, value):
                    edge[r, c, first : first + 16, :] = value

                return store

            convolve_block(
                base,
                ends,
                par_ref,
                lambda c, shift: xf[c, where + shift : where + shift + 8, :],
                at,
                put(slot),
                put(48 + slot),
            )

    for pair in range(pairs):
        if pair not in inner:
            multiply(pair)

    bias_score = jnp.sum(par_ref[4:5, :] * par_ref[5:6, :])

    ends = [ends_of(len_ref, r) for r in range(rows)]
    for pair in range(pairs):
        both = [place(pair, side) for side in range(2)]
        dots = rotate_rows(comp[0, pair], turn_e) + biases[pair]
        scores = rotate_rows(comp[1, pair], turn_e) + bias_score
        coef = jnp.zeros((8, 128), F32)
        coef_e = jnp.zeros((8, 128), F32)
        for p in range(2):
            at = tile_start(both[0][1]) + 2 * slot8 + p
            begin = [begin_of(at, ends[r]) for r, _, _ in both]
            end = [end_of(at, ends[r]) for r, _, _ in both]
            offset = jnp.maximum(at - jnp.where(left, begin[0], begin[1]), 0)
            remain = jnp.where(left, end[0], end[1]) - at
            masks, inverses, logits, grads = [], [], [], []
            for b in range(1, TAPS + 1):
                if b == 3:
                    thirds = ((offset.astype(F32) + 0.5) * (1.0 / 3.0)).astype(jnp.int32)
                    within = offset - 3 * thirds
                else:
                    within = offset & (b - 1)
                upper = jnp.minimum(b - within, remain)
                mask = (delta >= p - within) & (delta < p + upper)
                inverse = 1.0 / jnp.maximum(within + upper, 1).astype(F32)
                masks.append(mask)
                inverses.append(inverse)
                logits.append(jnp.sum(jnp.where(mask, scores, 0.0), axis=0, keepdims=True) * inverse)
                grads.append(
                    jnp.sum(jnp.where(mask, dots, 0.0), axis=0, keepdims=True) * (0.5 * inverse)
                )
            largest = functools.reduce(jnp.maximum, logits)
            powers = [jnp.exp(logit - largest) for logit in logits]
            scale = 1.0 / sum(powers)
            shares = [power * scale for power in powers]
            mean = sum(share * grad for share, grad in zip(shares, grads))
            for mask, inverse, share, grad in zip(masks, inverses, shares, grads):
                coef = coef + jnp.where(mask, (0.5 * share) * inverse, 0.0)
                coef_e = coef_e + jnp.where(mask, share * (grad - mean) * inverse, 0.0)
        owned = (slot8 >= LEAD) & (slot8 < LEAD + OWN)
        coef = jnp.where(owned, coef, 0.0)
        coef_e = jnp.where(owned, coef_e, 0.0)
        es[pair] = rotate_rows(coef_e, (8 - turn_e) & 7)
        swapped = pltpu.roll(coef, SLOTS, 1)
        for side, (r, m, tile) in enumerate(both):
            at = tile_start(m) + 2 * slot8 + delta
            offset = at - begin_of(at, ends[r])
            alone = jnp.where(left, coef, swapped) if side == 0 else jnp.where(left, swapped, coef)
            for p in range(2):
                kept = jnp.where((offset >= 2 * p + lane8 // SLOTS) & (at >= 0), alone, 0.0)
                cs[p, tile] = rotate_rows(kept, (8 - turn[p]) & 7)

    slots_down = iota((SLOTS, 128), 0)
    wide = 2 if chunks % 2 == 0 else 1
    factors = (fac_a, fac_b)

    def spread_pair(pair):
        spread = jnp.concatenate(
            [jnp.where(group_of_e == v, es[pair], 0.0) for v in range(WINDOW // 8)], axis=0
        ).T
        for side in range(2):
            _, m, _ = place(pair, side)
            from_row = OWN * m - 8
            part = spread[SLOTS * side : SLOTS * side + SLOTS]
            here = (from_row + slots_down >= 0) & (from_row + slots_down < half)
            own_e = jnp.sum(jnp.where(here, part, 0.0), axis=0, keepdims=True)
            all_e = jnp.sum(part, axis=0, keepdims=True)
            rows_e_ref[side, 0] = jnp.broadcast_to(own_e, (8, 128))
            rows_e_ref[side, 1] = jnp.broadcast_to(all_e, (8, 128))

    def build(pair, side):
        r, m, tile = place(pair, side)
        own_e = rows_e_ref[side, 0]
        all_e = rows_e_ref[side, 1]
        from_row = OWN * m - 8
        mine = [
            (from_row + 8 * i + sub8 >= 0) & (from_row + 8 * i + sub8 < half) for i in range(SLOTS // 8)
        ]
        at = tile_start(m) + lane8
        offset = at - begin_of(at, ends_of(len_ref, r))
        bands = []
        for p in range(2):
            bands.append(
                jnp.concatenate(
                    [jnp.where(group_of[p] == v, cs[p, tile], 0.0) for v in range(WINDOW // 8)], axis=0
                ).T
            )
        for k in range(TAPS):
            row_k = jnp.where((offset >= k) & (at >= 0), own_e, 0.0)
            if k > 0:
                row_k = pltpu.roll(row_k, 128 - k, 1)
            matrix = bands[k // 2][SLOTS * (k % 2) : SLOTS * (k % 2) + SLOTS]
            if k == 0:
                back = jnp.concatenate([jnp.where(sub8 < 2, all_e, matrix[0:8]), matrix[8:]], axis=0)
                high, low = split(back)
                mat[tile, :, 0:WINDOW] = high
                mat[tile, :, WINDOW:] = low
            parts = [jnp.where(mine[i], matrix[8 * i : 8 * i + 8], 0.0) for i in range(SLOTS // 8)]
            parts[0] = jnp.where(sub8 == 0, row_k, parts[0])
            matrix = jnp.concatenate(parts, axis=0)
            if k == 0:
                total = jnp.sum(matrix, axis=1, keepdims=True)
                tot[side] = jnp.broadcast_to(total, (SLOTS, 128))
            high, low = split(matrix)
            factors[side][SLOTS * k : SLOTS * (k + 1), 0:WINDOW] = high
            factors[side][SLOTS * k : SLOTS * (k + 1), WINDOW:] = low

    def apply(pair, side):
        r, m, _ = place(pair, side)
        start = pl.multiple_of(OWN * m + 8, 8)
        window = pl.multiple_of(2 * OWN * m, 16)
        factor = factors[side][...]
        total = tot[side]
        for w in range(chunks // wide):
            x = xb[r, pl.ds(window, WINDOW), 128 * wide * w : 128 * wide * (w + 1)]
            mixed = lax.dot_general(
                factor,
                jnp.concatenate([x, x], axis=0),
                (((1,), (0,)), ((), ())),
                preferred_element_type=F32,
            )
            for i in range(wide):
                c = wide * w + i
                lanes = lanes_of(c)
                g = g32[r, c, pl.ds(start, SLOTS), :]
                g = jnp.concatenate([jnp.where(sub8 == 0, par_ref[5:6, lanes], g[0:8]), g[8:]], axis=0)
                value = total * par_ref[4:5, lanes]
                for k in range(TAPS):
                    taken = mixed[SLOTS * k : SLOTS * (k + 1), lanes_of(i)]
                    value = value + taken * par_ref[k : k + 1, lanes]
                    acc[k, :, lanes] += jnp.sum((taken * g).reshape(SLOTS // 8, 8, 128), axis=0)
                acc[4, :, lanes] += jnp.sum((total * g).reshape(SLOTS // 8, 8, 128), axis=0)
                acc[5, :, lanes] += jnp.where(sub8 == 0, value[0:8], 0.0)
                top = carry_o[side, :, lanes] + jnp.where(sub8 < LEAD, 0.0, value[0:8])
                out32[r, c, pl.ds(start, 8), :] = top
                out32[r, c, pl.ds(start + 8, OWN - 8), :] = value[8:OWN]
                carry_o[side, :, lanes] = jnp.where(m < tiles - 1, value[OWN:], 0.0)

    spread_pair(0)
    build(0, 0)
    build(0, 1)

    def one_pair(pair):
        spread_pair(pair + 1)
        for side in range(2):
            apply(pair, side)
            build(pair + 1, side)

    together = 2

    def second_loop(i, _):
        for j in range(together):
            one_pair(together * i + j)
        return 0

    lax.fori_loop(0, (pairs - 1) // together, second_loop, 0)
    for pair in range((pairs - 1) // together * together, pairs - 1):
        one_pair(pair)
    apply(pairs - 1, 0)
    apply(pairs - 1, 1)
    for k in range(TAPS + 2):
        grad_ref[k : k + 1, :] = jnp.sum(acc[k], axis=0, keepdims=True)


def backward_kernel(shapes, r, base_ref, len_ref, mat, g32, out32, par_ref, *refs):
    out_hbm, gin_hbm, outb, dc, ginb, sems = refs[-6:]
    rows, length, half, features, tiles = shapes
    chunks = features // 128
    wide = 2 if chunks % 2 == 0 else 1
    base = base_ref[0]
    sub8 = iota((8, 128), 0)
    ends = ends_of(len_ref, r)
    for c in range(chunks):
        outb[:, lanes_of(c)] = out32[r, c, PAD : PAD + half, :].astype(BF16)
    copies = [pltpu.make_async_copy(outb, out_hbm.at[r], sems.at[2])]
    copies[0].start()

    for m in range(tiles):
        tile = r * tiles + m
        streamed = jnp.concatenate([mat[tile, :, 0:WINDOW].T, mat[tile, :, WINDOW:].T], axis=1)
        at = 2 * OWN * m
        for w in range(chunks // wide):
            held = []
            for i in range(wide):
                lanes = lanes_of(wide * w + i)
                scorer = par_ref[5:6, lanes]
                scorer_high = scorer.astype(BF16).astype(F32)
                g = g32[r, wide * w + i, OWN * m + 8 : OWN * m + 8 + SLOTS, :]
                top = jnp.where(
                    sub8 == 0, scorer_high, jnp.where(sub8 == 1, scorer - scorer_high, g[0:8])
                )
                held.append(jnp.concatenate([top, g[8:]], axis=0).astype(BF16))
            held = jnp.concatenate(held, axis=1)
            part = lax.dot_general(
                streamed,
                jnp.concatenate([held, held], axis=0),
                (((1,), (0,)), ((), ())),
                preferred_element_type=F32,
            )
            for i in range(wide):
                c = wide * w + i
                before = dc[c, at : at + PAD, :] if m > 0 else 0.0
                dc[c, at : at + PAD, :] = before + part[0:PAD, lanes_of(i)]
                dc[c, at + PAD : at + WINDOW, :] = part[PAD:, lanes_of(i)]

    def taps_at(at, masked):
        keeps = []
        if masked:
            for j in range(4):
                position = base + at + 8 * j + sub8
                remain = end_of(position, ends) - position
                keeps.append([remain > k for k in range(TAPS)])
        for c in range(chunks):
            parts = []
            for j in range(4):
                value = par_ref[0:1, lanes_of(c)] * dc[c, pl.ds(at + PAD + 8 * j, 8), :]
                for k in range(1, TAPS):
                    shifted = dc[c, pl.ds(at + PAD + 8 * j + k, 8), :]
                    if masked:
                        shifted = jnp.where(keeps[j][k], shifted, 0.0)
                    value = value + par_ref[k : k + 1, lanes_of(c)] * shifted
                parts.append(value)
            ginb[pl.ds(at, 32), lanes_of(c)] = jnp.concatenate(parts, axis=0).astype(BF16)

    def taps(i, _):
        at = pl.multiple_of(i * 32, 32)
        reach = [(end > base + at) & (end <= base + at + 32 + TAPS - 2) for end in ends]
        crosses = functools.reduce(jnp.logical_or, reach)

        @pl.when(crosses)
        def _():
            taps_at(at, True)

        @pl.when(jnp.logical_not(crosses))
        def _():
            taps_at(at, False)

        return 0

    pieces = 2
    for piece in range(pieces):
        size = length // pieces
        lax.fori_loop(piece * size // 32, (piece + 1) * size // 32, taps, 0)
        copies.append(
            pltpu.make_async_copy(
                ginb.at[pl.ds(piece * size, size), :],
                gin_hbm.at[r, pl.ds(piece * size, size), :],
                sems.at[piece],
            )
        )
        copies[-1].start()
    for copy in copies:
        copy.wait()


SMEM = pl.BlockSpec(memory_space=pltpu.SMEM)
VMEM = pl.BlockSpec(memory_space=pltpu.VMEM)
HBM = pl.BlockSpec(memory_space=pltpu.HBM)


def sizes_of(length, half):
    tiles = -(-(half + 3 + LEAD) // OWN)
    x_rows = 2 * OWN * (tiles - 1) + WINDOW
    g_rows = -(-(OWN * (tiles - 1) + 8 + SLOTS) // 16) * 16
    return tiles, x_rows, g_rows


def packed(base, inputs, cotangent):
    rows, _, features = inputs.shape
    part = jax.ShapeDtypeStruct((rows, PAD, features), BF16)
    return pl.pallas_call(
        pack_kernel,
        out_shape=(part, part),
        in_specs=[SMEM, HBM, HBM],
        out_specs=(VMEM, VMEM),
        scratch_shapes=[pltpu.VMEM((rows, PAD, features), BF16)] * 4 + [pltpu.SemaphoreType.DMA((4,))],
        compiler_params=pltpu.CompilerParams(vmem_limit_bytes=PACK_LIMIT),
    )(base, inputs, cotangent)


def convolved(base, lengths, inputs, params):
    rows, length, features = inputs.shape
    half = length // 2
    chunks = features // 128
    tiles, x_rows, _ = sizes_of(length, half)
    shapes = (rows, length, half, features, tiles)
    part = jax.ShapeDtypeStruct((rows, chunks, x_rows, 128), BF16)
    return pl.pallas_call(
        functools.partial(conv_kernel, shapes),
        out_shape=(part, part),
        in_specs=[SMEM, HBM, VMEM, VMEM],
        out_specs=(VMEM, VMEM),
        scratch_shapes=[
            pltpu.VMEM((rows, chunks, 8 + length, 128), F32),
            pltpu.SMEM(lengths.shape, jnp.int32),
            pltpu.SemaphoreType.DMA((1,)),
        ],
        compiler_params=pltpu.CompilerParams(vmem_limit_bytes=24 * 1024 * 1024),
        cost_estimate=pl.CostEstimate(
            flops=24 * inputs.size, bytes_accessed=8 * inputs.size, transcendentals=0
        ),
    )(base, lengths, inputs, params)


def forward(base, lengths, inputs, cotangent, high, low, near, far, params):
    rows, half, features = cotangent.shape
    length = 2 * half
    chunks = features // 128
    tiles, x_rows, g_rows = sizes_of(length, half)
    count = rows * tiles
    shapes = (rows, length, half, features, tiles)
    return pl.pallas_call(
        functools.partial(forward_kernel, shapes),
        out_shape=(
            jax.ShapeDtypeStruct((rows, chunks, g_rows, 128), F32),
            jax.ShapeDtypeStruct((count, SLOTS, 2 * WINDOW), BF16),
            jax.ShapeDtypeStruct((rows, chunks, g_rows, 128), F32),
            jax.ShapeDtypeStruct((TAPS + 2, features), F32),
        ),
        in_specs=[SMEM, HBM, VMEM, VMEM, VMEM, VMEM, VMEM, VMEM, VMEM],
        out_specs=(VMEM, VMEM, VMEM, VMEM),
        scratch_shapes=[
            pltpu.VMEM((rows, x_rows, features), BF16),
            pltpu.VMEM((chunks, 72, 128), F32),
            pltpu.VMEM((rows, chunks, 96, 128), BF16),
            pltpu.VMEM((2, count // 2, 8, 128), F32),
            pltpu.VMEM((count // 2, 8, 128), F32),
            pltpu.VMEM((2, count, 8, 128), F32),
            pltpu.VMEM((count // 2, 8, 128), F32),
            pltpu.VMEM((TAPS * SLOTS, 2 * WINDOW), BF16),
            pltpu.VMEM((TAPS * SLOTS, 2 * WINDOW), BF16),
            pltpu.VMEM((2, SLOTS, 128), F32),
            pltpu.VMEM((2, 2, 8, 128), F32),
            pltpu.VMEM((2, 8, features), F32),
            pltpu.VMEM((TAPS + 2, 8, features), F32),
            pltpu.SMEM(lengths.shape, jnp.int32),
            pltpu.SemaphoreType.DMA((1,)),
        ],
        compiler_params=pltpu.CompilerParams(vmem_limit_bytes=28 * 1024 * 1024),
        cost_estimate=pl.CostEstimate(
            flops=2 * count * SLOTS * WINDOW * features * 12,
            bytes_accessed=8 * inputs.size,
            transcendentals=0,
        ),
    )(base, lengths, inputs, cotangent, high, low, near, far, params)


def backward(r, base, lengths, shape, matrices, padded, outputs, params, grown):
    rows, length, features = shape
    half = length // 2
    chunks = features // 128
    tiles, x_rows, g_rows = sizes_of(length, half)
    shapes = (rows, length, half, features, tiles)
    operands = [base, lengths, matrices, padded, outputs, params]
    in_specs = [SMEM, SMEM, VMEM, VMEM, VMEM, VMEM]
    if grown is not None:
        operands.extend(grown)
        in_specs.extend([HBM, HBM])
    return pl.pallas_call(
        functools.partial(backward_kernel, shapes, r),
        out_shape=(
            jax.ShapeDtypeStruct((rows, half, features), BF16),
            jax.ShapeDtypeStruct(shape, BF16),
        ),
        in_specs=in_specs,
        out_specs=(HBM, HBM),
        scratch_shapes=[
            pltpu.VMEM((half, features), BF16),
            pltpu.VMEM((chunks, x_rows, 128), F32),
            pltpu.VMEM((length, features), BF16),
            pltpu.SemaphoreType.DMA((3,)),
        ],
        input_output_aliases={} if grown is None else {6: 0, 7: 1},
        compiler_params=pltpu.CompilerParams(vmem_limit_bytes=12 * 1024 * 1024),
        cost_estimate=pl.CostEstimate(
            flops=2 * tiles * SLOTS * WINDOW * features * 4,
            bytes_accessed=4 * length * features,
            transcendentals=0,
        ),
    )(*operands)


def update_kernel(
    grad_ref, other_ref, par_ref, first_ref, second_ref, norm_ref, new_ref, new_first_ref, new_second_ref
):
    grads = grad_ref[...] + other_ref[...]
    norm = jnp.sqrt(jnp.sum(grads * grads, keepdims=True))
    norm_ref[...] = norm
    grads = grads * jnp.minimum(1.0, clip_limit / (norm + 1e-06))
    weights = par_ref[...]
    first_new = beta_one * first_ref[...] + (1.0 - beta_one) * grads
    second_new = beta_two * second_ref[...] + (1.0 - beta_two) * grads * grads
    first_hat = first_new / (1.0 - beta_one**STEP)
    second_hat = second_new / (1.0 - beta_two**STEP)
    new_ref[...] = weights - learn_rate * (
        first_hat / (jnp.sqrt(second_hat) + adam_eps) + decay_rate * weights
    )
    new_first_ref[...] = first_new
    new_second_ref[...] = second_new


def update(grads, other, weights, first_old, second_old):
    like = jax.ShapeDtypeStruct(weights.shape, F32)
    return pl.pallas_call(
        update_kernel,
        out_shape=(jax.ShapeDtypeStruct((1, 1), F32), like, like, like),
        in_specs=[VMEM] * 5,
        out_specs=(VMEM,) * 4,
        compiler_params=pltpu.CompilerParams(vmem_limit_bytes=4 * 1024 * 1024),
    )(grads, other, weights, first_old, second_old)


def rounds_of(axes):
    rounds = []
    for axis in axes:
        count = lax.axis_size(axis)
        step = 1
        while step < count:
            rounds.append((axis, [(i, i ^ step) for i in range(count)]))
            step *= 2
    return rounds


def per_device(inputs, lengths, params, first_moment, second_moment, cotangent):
    rows_here, length_here, _ = inputs.shape
    base = (lax.axis_index("group") * length_here).astype(jnp.int32).reshape(1)
    near, far = packed(base, inputs, cotangent)
    far = lax.ppermute(far, "group", pairs_of("group", 1))
    near = lax.ppermute(near, "group", pairs_of("group", 0))
    high, low = convolved(base, lengths, inputs, params)
    outputs, matrices, padded, grad_params = forward(
        base, lengths, inputs, cotangent, high, low, near, far, params
    )

    def backward_row(row, matrices, grown):
        return backward(row, base, lengths, inputs.shape, matrices, padded, outputs, params, grown)

    grown = None
    row = 0
    received = None
    for axis, exchange in rounds_of(("group", "rows")):
        if received is not None:
            grad_params = grad_params + received
            if row < rows_here:
                matrices, grad_params = lax.optimization_barrier((matrices, grad_params))
                grown = backward_row(row, matrices, grown)
                received = lax.ppermute(grad_params, axis, exchange)
                received, grown = lax.optimization_barrier((received, grown))
                row += 1
                continue
        received = lax.ppermute(grad_params, axis, exchange)
    while row < rows_here:
        grown = backward_row(row, matrices, grown)
        row += 1
    output, grad_inputs = grown
    grad_norm, new_params, new_first, new_second = update(
        grad_params, received, params, first_moment, second_moment
    )
    grad_norm = grad_norm.reshape(())
    return (output, grad_inputs, grad_norm, new_params, new_first, new_second)


def solution(mesh):
    in_specs = (P("rows", "group", None), P("rows", None), P(), P(), P(), P("rows", "group", None))
    out_specs = (P("rows", "group", None), P("rows", "group", None), P(), P(), P(), P())
    return jax.shard_map(
        per_device, mesh=mesh, in_specs=in_specs, out_specs=out_specs, check_vma=False
    )
```

```python
import functools

import jax
import jax.numpy as jnp
from jax import lax
from jax.experimental import pallas as pl
from jax.experimental.pallas import tpu as pltpu
from jax.sharding import PartitionSpec as P

STEP = 10


beta_one = 0.9
beta_two = 0.999
learn_rate = 0.2
decay_rate = 0.01
adam_eps = 1e-08
clip_limit = 1.0

TAPS = 4
SLOTS = 64
PACK_LIMIT = 53 * 1024 * 1024
OWN = 56
LEAD = 4
WINDOW = 128
PAD = 16
F32 = jnp.float32
BF16 = jnp.bfloat16


def pairs_of(axis, first):
    count = lax.axis_size(axis)
    pairs = [(i, i + 1) for i in range(first, count - 1, 2)]
    return pairs + [(j, i) for i, j in pairs]


def rotate_rows(x, amount):
    for bit in (1, 2, 4):
        x = jnp.where((amount & bit) != 0, pltpu.roll(x, 8 - bit, x.ndim - 2), x)
    return x


def split(x):
    high = x.astype(BF16)
    return high, (x - high.astype(F32)).astype(BF16)


def iota(shape, dim):
    return lax.broadcasted_iota(jnp.int32, shape, dim)


def ends_of(len_ref, r):
    one = len_ref[r, 0]
    two = one + len_ref[r, 1]
    three = two + len_ref[r, 2]
    return one, two, three, three + len_ref[r, 3]


def begin_of(at, ends):
    begin = jnp.where(at >= ends[0], ends[0], 0)
    begin = jnp.where(at >= ends[1], ends[1], begin)
    return jnp.where(at >= ends[2], ends[2], begin)


def end_of(at, ends):
    end = jnp.where(at >= ends[0], ends[1], ends[0])
    end = jnp.where(at >= ends[1], ends[2], end)
    return jnp.where(at >= ends[2], ends[3], end)


def lanes_of(c):
    return slice(128 * c, 128 * c + 128)


def pack_kernel(base_ref, x_hbm, g_hbm, near_ref, far_ref, x_first, x_last, g_first, g_last, sems):
    rows, length, features = x_hbm.shape
    half = g_hbm.shape[1]
    copies = [
        pltpu.make_async_copy(x_hbm.at[:, pl.ds(length - PAD, PAD), :], x_last, sems.at[0]),
        pltpu.make_async_copy(g_hbm.at[:, pl.ds(half - PAD, PAD), :], g_last, sems.at[1]),
        pltpu.make_async_copy(x_hbm.at[:, pl.ds(0, PAD), :], x_first, sems.at[2]),
        pltpu.make_async_copy(g_hbm.at[:, pl.ds(0, PAD), :], g_first, sems.at[3]),
    ]
    for copy in copies:
        copy.start()
    even = (base_ref[0] // length) % 2 == 0
    sub = iota((PAD, features), 0)
    for copy in copies:
        copy.wait()
    for r in range(rows):
        moved = pltpu.roll(g_last[r].astype(F32), 2, 0)
        last = jnp.where(sub < 2, moved, x_last[r].astype(F32))
        moved = pltpu.roll(g_first[r].astype(F32), PAD - 3, 0)
        first = jnp.where(sub < PAD - 3, x_first[r].astype(F32), moved)
        near_ref[r] = jnp.where(even, last, first).astype(BF16)
        far_ref[r] = jnp.where(even, first, last).astype(BF16)


def convolve_block(base, ends, par_ref, load, at, place_high, place_low, masked=True):
    chunks = par_ref.shape[1] // 128
    sub8 = iota((8, 128), 0)
    keeps = []
    for j in range(2 if masked else 0):
        position = base - PAD + at + 8 * j + sub8
        offset = position - begin_of(position, ends)
        keeps.append([offset >= k for k in range(TAPS)])
    for c in range(chunks):
        lanes = lanes_of(c)
        parts = []
        for j in range(2):
            value = par_ref[0:1, lanes] * load(c, 8 * j)
            for k in range(1, TAPS):
                shifted = load(c, 8 * j - k)
                if masked:
                    shifted = jnp.where(keeps[j][k], shifted, 0.0)
                value = value + par_ref[k : k + 1, lanes] * shifted
            parts.append(value)
        high, low = split(jnp.concatenate(parts, axis=0))
        place_high(c, high)
        place_low(c, low)


def conv_kernel(shapes, base_ref, len_hbm, x_ref, par_ref, high_ref, low_ref, xf, len_ref, sem):
    rows, length, half, features, tiles = shapes
    chunks = features // 128
    base = base_ref[0]
    step = 64
    copy_len = pltpu.make_async_copy(len_hbm, len_ref, sem.at[0])
    copy_len.start()
    begin = 2 * PAD + length
    rest = high_ref.shape[2] - begin
    for r in range(rows):
        for c in range(chunks):
            xf[r, c, 0:8, :] = jnp.zeros((8, 128), F32)
            if rest > 0:
                for ref in (high_ref, low_ref):
                    ref[r, c, begin:, :] = jnp.zeros((rest, 128), BF16)

    widened = 2 * step

    def widen(i, _):
        r = i // (length // widened)
        at = pl.multiple_of((i % (length // widened)) * widened, widened)
        for c in range(chunks):
            xf[r, c, pl.ds(at + 8, widened), :] = x_ref[r, pl.ds(at, widened), lanes_of(c)].astype(F32)
        return 0

    lax.fori_loop(0, rows * (length // widened), widen, 0)
    copy_len.wait()

    def one_row(r, _):
        ends = ends_of(len_ref, r)

        def blocks(at, masked):
            for b in range(step // 16):

                def put(ref):
                    def store(c, value):
                        ref[r, c, pl.ds(at + PAD + 16 * b, 16), :] = value

                    return store

                convolve_block(
                    base,
                    ends,
                    par_ref,
                    lambda c, shift: xf[r, c, pl.ds(at + 8 + 16 * b + shift, 8), :],
                    at + PAD + 16 * b,
                    put(high_ref),
                    put(low_ref),
                    masked,
                )

        def one_step(i, _):
            at = pl.multiple_of(i * step, step)
            reach = [(end > base + at - TAPS + 1) & (end < base + at + step) for end in ends]
            starts = functools.reduce(jnp.logical_or, reach)

            @pl.when(starts)
            def _():
                blocks(at, True)

            @pl.when(jnp.logical_not(starts))
            def _():
                blocks(at, False)

            return 0

        lax.fori_loop(0, length // step, one_step, 0)
        return 0

    lax.fori_loop(0, rows, one_row, 0)


def forward_kernel(
    shapes,
    base_ref,
    len_hbm,
    x_ref,
    g_ref,
    high_ref,
    low_ref,
    near_ref,
    far_ref,
    par_ref,
    out32,
    mat,
    g32,
    grad_ref,
    xb,
    xf,
    edge,
    comp,
    biases,
    cs,
    es,
    fac_a,
    fac_b,
    tot,
    rows_e_ref,
    carry_o,
    acc,
    len_ref,
    sem,
):
    rows, length, half, features, tiles = shapes
    pairs = rows * tiles // 2
    chunks = features // 128
    base = base_ref[0]
    copy_len = pltpu.make_async_copy(len_hbm, len_ref, sem.at[0])
    copy_len.start()

    sub8 = iota((8, 128), 0)
    lane8 = iota((8, 128), 1)
    slot8 = lane8 % SLOTS
    left = lane8 < SLOTS
    delta = sub8 - 3
    first = [2 * slot8 - 3 - (2 * p + lane8 // SLOTS) for p in range(2)]
    group_of = [(f + ((sub8 - f) & 7)) >> 3 for f in first]
    turn = [f & 7 for f in first]
    first_e = 2 * slot8 - 3
    group_of_e = (first_e + ((sub8 - first_e) & 7)) >> 3
    turn_e = first_e & 7

    def place(pair, side):
        r, m = 2 * (pair // tiles) + side, pair % tiles
        return r, m, r * tiles + m

    def tile_start(m):
        return base + 2 * OWN * m - PAD

    acc[...] = jnp.zeros_like(acc)
    carry_o[...] = jnp.zeros_like(carry_o)

    for r in range(rows):
        for c in range(chunks):
            g32[r, c, PAD : PAD + half, :] = g_ref[r, :, lanes_of(c)].astype(F32)

    scorer_high = [par_ref[5:6, lanes_of(c)].astype(BF16).astype(F32) for c in range(chunks)]
    scorer_low = [par_ref[5:6, lanes_of(c)] - scorer_high[c] for c in range(chunks)]

    def held_rows(r, m, c):
        parts = []
        at = 2 * OWN * m
        for ref, own in ((high_ref, 0), (low_ref, 48)):
            begin = 0
            if m == 0:
                parts.append(edge[r, c, own : own + 32, :])
                begin = 32
            if m == tiles - 1:
                end = PAD + length - at
                parts.append(ref[r, c, at + begin : at + end, :])
                parts.append(edge[r, c, own + 32 : own + 48, :])
                begin = end + 16
            if begin < WINDOW:
                parts.append(ref[r, c, at + begin : at + WINDOW, :])
        return jnp.concatenate(parts, axis=0)

    def multiply(pair):
        dots, scores, added = [], [], []
        for side in range(2):
            r, m, _ = place(pair, side)
            start = OWN * m + 8
            streamed, held = [], []
            biased = jnp.zeros((SLOTS, 128), F32)
            for c in range(chunks):
                g = g32[r, c, start : start + SLOTS, :]
                biased = biased + g * par_ref[4:5, lanes_of(c)]
                top = jnp.where(sub8 == 0, scorer_high[c], jnp.where(sub8 == 1, scorer_low[c], g[0:8]))
                streamed.append(jnp.concatenate([top, g[8:]], axis=0).astype(BF16))
                held.append(held_rows(r, m, c))
            product = lax.dot_general(
                jnp.concatenate(streamed, axis=1),
                jnp.concatenate(held, axis=1),
                (((1,), (1,)), ((), ())),
                preferred_element_type=F32,
            )
            product = product[:, :WINDOW] + product[:, WINDOW:]
            added.append(jnp.broadcast_to(jnp.sum(biased, axis=1, keepdims=True), (SLOTS, 128)))
            dots.append(product)
            scores.append(jnp.broadcast_to(product[0:1] + product[1:2], (SLOTS, WINDOW)))
        dots = jnp.concatenate(dots, axis=0).T
        scores = jnp.concatenate(scores, axis=0).T
        banded = jnp.zeros((8, 128), F32)
        scored = jnp.zeros((8, 128), F32)
        for v in range(WINDOW // 8):
            here = group_of_e == v
            banded = jnp.where(here, dots[8 * v : 8 * v + 8], banded)
            scored = jnp.where(here, scores[8 * v : 8 * v + 8], scored)
        comp[0, pair] = banded
        comp[1, pair] = scored
        biases[pair] = jnp.concatenate(added, axis=0).T[0:8]

    inner = [pair for pair in range(pairs) if 0 < pair % tiles < tiles - 1]
    for pair in inner:
        multiply(pair)

    copy_len.wait()
    subd = iota((8, features), 0)
    even = (base // length) % 2 == 0
    for r in range(rows):
        near = near_ref[r].astype(F32)
        far = far_ref[r].astype(F32)
        up = jnp.where(even, far, near)
        down = jnp.where(even, near, far)
        xb[r, 0:PAD, :] = up.astype(BF16)
        xb[r, PAD + length : 2 * PAD + length, :] = down.astype(BF16)
        rest = xb.shape[1] - 2 * PAD - length
        if rest > 0:
            xb[r, 2 * PAD + length :, :] = jnp.zeros((rest, features), BF16)
        xb[r, PAD : PAD + length, :] = x_ref[r]
        before = jnp.where(subd >= 6, pltpu.roll(up[0:8], 6, 0), 0.0)
        after = jnp.where(subd < 3, pltpu.roll(down[8:16], 3, 0), 0.0)
        rest = g32.shape[2] - PAD - half - 8
        for c in range(chunks):
            g32[r, c, 8:16, :] = before[:, lanes_of(c)]
            g32[r, c, PAD + half : PAD + half + 8, :] = after[:, lanes_of(c)]
            g32[r, c, PAD + half + 8 :, :] = jnp.zeros((rest, 128), F32)
        for c in range(chunks):
            lanes = lanes_of(c)
            xf[c, 0:8, :] = jnp.zeros((8, 128), F32)
            xf[c, 8:24, :] = up[:, lanes]
            xf[c, 24:40, :] = x_ref[r, 0:16, lanes].astype(F32)
            xf[c, 40:56, :] = x_ref[r, length - 16 : length, lanes].astype(F32)
            xf[c, 56:72, :] = down[:, lanes]
        ends = ends_of(len_ref, r)
        for at, where, slot in ((0, 8, 0), (PAD, 24, 16), (PAD + length, 56, 32)):

            def put(first):
                def store(c, value):
                    edge[r, c, first : first + 16, :] = value

                return store

            convolve_block(
                base,
                ends,
                par_ref,
                lambda c, shift: xf[c, where + shift : where + shift + 8, :],
                at,
                put(slot),
                put(48 + slot),
            )

    for pair in range(pairs):
        if pair not in inner:
            multiply(pair)

    bias_score = jnp.sum(par_ref[4:5, :] * par_ref[5:6, :])

    ends = [ends_of(len_ref, r) for r in range(rows)]
    for pair in range(pairs):
        both = [place(pair, side) for side in range(2)]
        dots = rotate_rows(comp[0, pair], turn_e) + biases[pair]
        scores = rotate_rows(comp[1, pair], turn_e) + bias_score
        coef = jnp.zeros((8, 128), F32)
        coef_e = jnp.zeros((8, 128), F32)
        for p in range(2):
            at = tile_start(both[0][1]) + 2 * slot8 + p
            begin = [begin_of(at, ends[r]) for r, _, _ in both]
            end = [end_of(at, ends[r]) for r, _, _ in both]
            offset = jnp.maximum(at - jnp.where(left, begin[0], begin[1]), 0)
            remain = jnp.where(left, end[0], end[1]) - at
            masks, inverses, logits, grads = [], [], [], []
            for b in range(1, TAPS + 1):
                if b == 3:
                    thirds = ((offset.astype(F32) + 0.5) * (1.0 / 3.0)).astype(jnp.int32)
                    within = offset - 3 * thirds
                else:
                    within = offset & (b - 1)
                upper = jnp.minimum(b - within, remain)
                mask = (delta >= p - within) & (delta < p + upper)
                inverse = 1.0 / jnp.maximum(within + upper, 1).astype(F32)
                masks.append(mask)
                inverses.append(inverse)
                logits.append(jnp.sum(jnp.where(mask, scores, 0.0), axis=0, keepdims=True) * inverse)
                grads.append(
                    jnp.sum(jnp.where(mask, dots, 0.0), axis=0, keepdims=True) * (0.5 * inverse)
                )
            largest = functools.reduce(jnp.maximum, logits)
            powers = [jnp.exp(logit - largest) for logit in logits]
            scale = 1.0 / sum(powers)
            shares = [power * scale for power in powers]
            mean = sum(share * grad for share, grad in zip(shares, grads))
            for mask, inverse, share, grad in zip(masks, inverses, shares, grads):
                coef = coef + jnp.where(mask, (0.5 * share) * inverse, 0.0)
                coef_e = coef_e + jnp.where(mask, share * (grad - mean) * inverse, 0.0)
        owned = (slot8 >= LEAD) & (slot8 < LEAD + OWN)
        coef = jnp.where(owned, coef, 0.0)
        coef_e = jnp.where(owned, coef_e, 0.0)
        es[pair] = rotate_rows(coef_e, (8 - turn_e) & 7)
        swapped = pltpu.roll(coef, SLOTS, 1)
        for side, (r, m, tile) in enumerate(both):
            at = tile_start(m) + 2 * slot8 + delta
            offset = at - begin_of(at, ends[r])
            alone = jnp.where(left, coef, swapped) if side == 0 else jnp.where(left, swapped, coef)
            for p in range(2):
                kept = jnp.where((offset >= 2 * p + lane8 // SLOTS) & (at >= 0), alone, 0.0)
                cs[p, tile] = rotate_rows(kept, (8 - turn[p]) & 7)

    slots_down = iota((SLOTS, 128), 0)
    wide = 2 if chunks % 2 == 0 else 1
    factors = (fac_a, fac_b)

    def spread_pair(pair):
        spread = jnp.concatenate(
            [jnp.where(group_of_e == v, es[pair], 0.0) for v in range(WINDOW // 8)], axis=0
        ).T
        for side in range(2):
            _, m, _ = place(pair, side)
            from_row = OWN * m - 8
            part = spread[SLOTS * side : SLOTS * side + SLOTS]
            here = (from_row + slots_down >= 0) & (from_row + slots_down < half)
            own_e = jnp.sum(jnp.where(here, part, 0.0), axis=0, keepdims=True)
            all_e = jnp.sum(part, axis=0, keepdims=True)
            rows_e_ref[side, 0] = jnp.broadcast_to(own_e, (8, 128))
            rows_e_ref[side, 1] = jnp.broadcast_to(all_e, (8, 128))

    def build(pair, side):
        r, m, tile = place(pair, side)
        own_e = rows_e_ref[side, 0]
        all_e = rows_e_ref[side, 1]
        from_row = OWN * m - 8
        mine = [
            (from_row + 8 * i + sub8 >= 0) & (from_row + 8 * i + sub8 < half) for i in range(SLOTS // 8)
        ]
        at = tile_start(m) + lane8
        offset = at - begin_of(at, ends_of(len_ref, r))
        bands = []
        for p in range(2):
            bands.append(
                jnp.concatenate(
                    [jnp.where(group_of[p] == v, cs[p, tile], 0.0) for v in range(WINDOW // 8)], axis=0
                ).T
            )
        for k in range(TAPS):
            row_k = jnp.where((offset >= k) & (at >= 0), own_e, 0.0)
            if k > 0:
                row_k = pltpu.roll(row_k, 128 - k, 1)
            matrix = bands[k // 2][SLOTS * (k % 2) : SLOTS * (k % 2) + SLOTS]
            if k == 0:
                back = jnp.concatenate([jnp.where(sub8 < 2, all_e, matrix[0:8]), matrix[8:]], axis=0)
                high, low = split(back)
                mat[tile, :, 0:WINDOW] = high
                mat[tile, :, WINDOW:] = low
            parts = [jnp.where(mine[i], matrix[8 * i : 8 * i + 8], 0.0) for i in range(SLOTS // 8)]
            parts[0] = jnp.where(sub8 == 0, row_k, parts[0])
            matrix = jnp.concatenate(parts, axis=0)
            if k == 0:
                total = jnp.sum(matrix, axis=1, keepdims=True)
                tot[side] = jnp.broadcast_to(total, (SLOTS, 128))
            high, low = split(matrix)
            factors[side][SLOTS * k : SLOTS * (k + 1), 0:WINDOW] = high
            factors[side][SLOTS * k : SLOTS * (k + 1), WINDOW:] = low

    def apply(pair, side):
        r, m, _ = place(pair, side)
        start = pl.multiple_of(OWN * m + 8, 8)
        window = pl.multiple_of(2 * OWN * m, 16)
        factor = factors[side][...]
        total = tot[side]
        for w in range(chunks // wide):
            x = xb[r, pl.ds(window, WINDOW), 128 * wide * w : 128 * wide * (w + 1)]
            mixed = lax.dot_general(
                factor,
                jnp.concatenate([x, x], axis=0),
                (((1,), (0,)), ((), ())),
                preferred_element_type=F32,
            )
            for i in range(wide):
                c = wide * w + i
                lanes = lanes_of(c)
                g = g32[r, c, pl.ds(start, SLOTS), :]
                g = jnp.concatenate([jnp.where(sub8 == 0, par_ref[5:6, lanes], g[0:8]), g[8:]], axis=0)
                value = total * par_ref[4:5, lanes]
                for k in range(TAPS):
                    taken = mixed[SLOTS * k : SLOTS * (k + 1), lanes_of(i)]
                    value = value + taken * par_ref[k : k + 1, lanes]
                    acc[k, :, lanes] += jnp.sum((taken * g).reshape(SLOTS // 8, 8, 128), axis=0)
                acc[4, :, lanes] += jnp.sum((total * g).reshape(SLOTS // 8, 8, 128), axis=0)
                acc[5, :, lanes] += jnp.where(sub8 == 0, value[0:8], 0.0)
                top = carry_o[side, :, lanes] + jnp.where(sub8 < LEAD, 0.0, value[0:8])
                out32[r, c, pl.ds(start, 8), :] = top
                out32[r, c, pl.ds(start + 8, OWN - 8), :] = value[8:OWN]
                carry_o[side, :, lanes] = jnp.where(m < tiles - 1, value[OWN:], 0.0)

    spread_pair(0)
    build(0, 0)
    build(0, 1)

    def one_pair(pair):
        spread_pair(pair + 1)
        for side in range(2):
            apply(pair, side)
            build(pair + 1, side)

    together = 2

    def second_loop(i, _):
        for j in range(together):
            one_pair(together * i + j)
        return 0

    lax.fori_loop(0, (pairs - 1) // together, second_loop, 0)
    for pair in range((pairs - 1) // together * together, pairs - 1):
        one_pair(pair)
    apply(pairs - 1, 0)
    apply(pairs - 1, 1)
    for k in range(TAPS + 2):
        grad_ref[k : k + 1, :] = jnp.sum(acc[k], axis=0, keepdims=True)


def backward_kernel(shapes, r, base_ref, len_ref, mat, g32, out32, par_ref, *refs):
    out_hbm, gin_hbm, outb, dc, ginb, sems = refs[-6:]
    rows, length, half, features, tiles = shapes
    chunks = features // 128
    wide = 2 if chunks % 2 == 0 else 1
    base = base_ref[0]
    sub8 = iota((8, 128), 0)
    ends = ends_of(len_ref, r)
    for c in range(chunks):
        outb[:, lanes_of(c)] = out32[r, c, PAD : PAD + half, :].astype(BF16)
    copies = [pltpu.make_async_copy(outb, out_hbm.at[r], sems.at[2])]
    copies[0].start()

    for m in range(tiles):
        tile = r * tiles + m
        streamed = jnp.concatenate([mat[tile, :, 0:WINDOW].T, mat[tile, :, WINDOW:].T], axis=1)
        at = 2 * OWN * m
        for w in range(chunks // wide):
            held = []
            for i in range(wide):
                lanes = lanes_of(wide * w + i)
                scorer = par_ref[5:6, lanes]
                scorer_high = scorer.astype(BF16).astype(F32)
                g = g32[r, wide * w + i, OWN * m + 8 : OWN * m + 8 + SLOTS, :]
                top = jnp.where(
                    sub8 == 0, scorer_high, jnp.where(sub8 == 1, scorer - scorer_high, g[0:8])
                )
                held.append(jnp.concatenate([top, g[8:]], axis=0).astype(BF16))
            held = jnp.concatenate(held, axis=1)
            part = lax.dot_general(
                streamed,
                jnp.concatenate([held, held], axis=0),
                (((1,), (0,)), ((), ())),
                preferred_element_type=F32,
            )
            for i in range(wide):
                c = wide * w + i
                before = dc[c, at : at + PAD, :] if m > 0 else 0.0
                dc[c, at : at + PAD, :] = before + part[0:PAD, lanes_of(i)]
                dc[c, at + PAD : at + WINDOW, :] = part[PAD:, lanes_of(i)]

    def taps_at(at, masked):
        keeps = []
        if masked:
            for j in range(4):
                position = base + at + 8 * j + sub8
                remain = end_of(position, ends) - position
                keeps.append([remain > k for k in range(TAPS)])
        for c in range(chunks):
            parts = []
            for j in range(4):
                value = par_ref[0:1, lanes_of(c)] * dc[c, pl.ds(at + PAD + 8 * j, 8), :]
                for k in range(1, TAPS):
                    shifted = dc[c, pl.ds(at + PAD + 8 * j + k, 8), :]
                    if masked:
                        shifted = jnp.where(keeps[j][k], shifted, 0.0)
                    value = value + par_ref[k : k + 1, lanes_of(c)] * shifted
                parts.append(value)
            ginb[pl.ds(at, 32), lanes_of(c)] = jnp.concatenate(parts, axis=0).astype(BF16)

    def taps(i, _):
        at = pl.multiple_of(i * 32, 32)
        reach = [(end > base + at) & (end <= base + at + 32 + TAPS - 2) for end in ends]
        crosses = functools.reduce(jnp.logical_or, reach)

        @pl.when(crosses)
        def _():
            taps_at(at, True)

        @pl.when(jnp.logical_not(crosses))
        def _():
            taps_at(at, False)

        return 0

    pieces = 2
    for piece in range(pieces):
        size = length // pieces
        lax.fori_loop(piece * size // 32, (piece + 1) * size // 32, taps, 0)
        copies.append(
            pltpu.make_async_copy(
                ginb.at[pl.ds(piece * size, size), :],
                gin_hbm.at[r, pl.ds(piece * size, size), :],
                sems.at[piece],
            )
        )
        copies[-1].start()
    for copy in copies:
        copy.wait()


SMEM = pl.BlockSpec(memory_space=pltpu.SMEM)
VMEM = pl.BlockSpec(memory_space=pltpu.VMEM)
HBM = pl.BlockSpec(memory_space=pltpu.HBM)


def sizes_of(length, half):
    tiles = -(-(half + 3 + LEAD) // OWN)
    x_rows = 2 * OWN * (tiles - 1) + WINDOW
    g_rows = -(-(OWN * (tiles - 1) + 8 + SLOTS) // 16) * 16
    return tiles, x_rows, g_rows


def packed(base, inputs, cotangent):
    rows, _, features = inputs.shape
    part = jax.ShapeDtypeStruct((rows, PAD, features), BF16)
    return pl.pallas_call(
        pack_kernel,
        out_shape=(part, part),
        in_specs=[SMEM, HBM, HBM],
        out_specs=(VMEM, VMEM),
        scratch_shapes=[pltpu.VMEM((rows, PAD, features), BF16)] * 4 + [pltpu.SemaphoreType.DMA((4,))],
        compiler_params=pltpu.CompilerParams(vmem_limit_bytes=PACK_LIMIT),
    )(base, inputs, cotangent)


def convolved(base, lengths, inputs, params):
    rows, length, features = inputs.shape
    half = length // 2
    chunks = features // 128
    tiles, x_rows, _ = sizes_of(length, half)
    shapes = (rows, length, half, features, tiles)
    part = jax.ShapeDtypeStruct((rows, chunks, x_rows, 128), BF16)
    return pl.pallas_call(
        functools.partial(conv_kernel, shapes),
        out_shape=(part, part),
        in_specs=[SMEM, HBM, VMEM, VMEM],
        out_specs=(VMEM, VMEM),
        scratch_shapes=[
            pltpu.VMEM((rows, chunks, 8 + length, 128), F32),
            pltpu.SMEM(lengths.shape, jnp.int32),
            pltpu.SemaphoreType.DMA((1,)),
        ],
        compiler_params=pltpu.CompilerParams(vmem_limit_bytes=24 * 1024 * 1024),
        cost_estimate=pl.CostEstimate(
            flops=24 * inputs.size, bytes_accessed=8 * inputs.size, transcendentals=0
        ),
    )(base, lengths, inputs, params)


def forward(base, lengths, inputs, cotangent, high, low, near, far, params):
    rows, half, features = cotangent.shape
    length = 2 * half
    chunks = features // 128
    tiles, x_rows, g_rows = sizes_of(length, half)
    count = rows * tiles
    shapes = (rows, length, half, features, tiles)
    return pl.pallas_call(
        functools.partial(forward_kernel, shapes),
        out_shape=(
            jax.ShapeDtypeStruct((rows, chunks, g_rows, 128), F32),
            jax.ShapeDtypeStruct((count, SLOTS, 2 * WINDOW), BF16),
            jax.ShapeDtypeStruct((rows, chunks, g_rows, 128), F32),
            jax.ShapeDtypeStruct((TAPS + 2, features), F32),
        ),
        in_specs=[SMEM, HBM, VMEM, VMEM, VMEM, VMEM, VMEM, VMEM, VMEM],
        out_specs=(VMEM, VMEM, VMEM, VMEM),
        scratch_shapes=[
            pltpu.VMEM((rows, x_rows, features), BF16),
            pltpu.VMEM((chunks, 72, 128), F32),
            pltpu.VMEM((rows, chunks, 96, 128), BF16),
            pltpu.VMEM((2, count // 2, 8, 128), F32),
            pltpu.VMEM((count // 2, 8, 128), F32),
            pltpu.VMEM((2, count, 8, 128), F32),
            pltpu.VMEM((count // 2, 8, 128), F32),
            pltpu.VMEM((TAPS * SLOTS, 2 * WINDOW), BF16),
            pltpu.VMEM((TAPS * SLOTS, 2 * WINDOW), BF16),
            pltpu.VMEM((2, SLOTS, 128), F32),
            pltpu.VMEM((2, 2, 8, 128), F32),
            pltpu.VMEM((2, 8, features), F32),
            pltpu.VMEM((TAPS + 2, 8, features), F32),
            pltpu.SMEM(lengths.shape, jnp.int32),
            pltpu.SemaphoreType.DMA((1,)),
        ],
        compiler_params=pltpu.CompilerParams(vmem_limit_bytes=28 * 1024 * 1024),
        cost_estimate=pl.CostEstimate(
            flops=2 * count * SLOTS * WINDOW * features * 12,
            bytes_accessed=8 * inputs.size,
            transcendentals=0,
        ),
    )(base, lengths, inputs, cotangent, high, low, near, far, params)


def backward(r, base, lengths, shape, matrices, padded, outputs, params, grown):
    rows, length, features = shape
    half = length // 2
    chunks = features // 128
    tiles, x_rows, g_rows = sizes_of(length, half)
    shapes = (rows, length, half, features, tiles)
    operands = [base, lengths, matrices, padded, outputs, params]
    in_specs = [SMEM, SMEM, VMEM, VMEM, VMEM, VMEM]
    if grown is not None:
        operands.extend(grown)
        in_specs.extend([HBM, HBM])
    return pl.pallas_call(
        functools.partial(backward_kernel, shapes, r),
        out_shape=(
            jax.ShapeDtypeStruct((rows, half, features), BF16),
            jax.ShapeDtypeStruct(shape, BF16),
        ),
        in_specs=in_specs,
        out_specs=(HBM, HBM),
        scratch_shapes=[
            pltpu.VMEM((half, features), BF16),
            pltpu.VMEM((chunks, x_rows, 128), F32),
            pltpu.VMEM((length, features), BF16),
            pltpu.SemaphoreType.DMA((3,)),
        ],
        input_output_aliases={} if grown is None else {6: 0, 7: 1},
        compiler_params=pltpu.CompilerParams(vmem_limit_bytes=12 * 1024 * 1024),
        cost_estimate=pl.CostEstimate(
            flops=2 * tiles * SLOTS * WINDOW * features * 4,
            bytes_accessed=4 * length * features,
            transcendentals=0,
        ),
    )(*operands)


def update_kernel(
    grad_ref, other_ref, par_ref, first_ref, second_ref, norm_ref, new_ref, new_first_ref, new_second_ref
):
    grads = grad_ref[...] + other_ref[...]
    norm = jnp.sqrt(jnp.sum(grads * grads, keepdims=True))
    norm_ref[...] = norm
    grads = grads * jnp.minimum(1.0, clip_limit / (norm + 1e-06))
    weights = par_ref[...]
    first_new = beta_one * first_ref[...] + (1.0 - beta_one) * grads
    second_new = beta_two * second_ref[...] + (1.0 - beta_two) * grads * grads
    first_hat = first_new / (1.0 - beta_one**STEP)
    second_hat = second_new / (1.0 - beta_two**STEP)
    new_ref[...] = weights - learn_rate * (
        first_hat / (jnp.sqrt(second_hat) + adam_eps) + decay_rate * weights
    )
    new_first_ref[...] = first_new
    new_second_ref[...] = second_new


def update(grads, other, weights, first_old, second_old):
    like = jax.ShapeDtypeStruct(weights.shape, F32)
    return pl.pallas_call(
        update_kernel,
        out_shape=(jax.ShapeDtypeStruct((1, 1), F32), like, like, like),
        in_specs=[VMEM] * 5,
        out_specs=(VMEM,) * 4,
        compiler_params=pltpu.CompilerParams(vmem_limit_bytes=4 * 1024 * 1024),
    )(grads, other, weights, first_old, second_old)


def rounds_of(axes):
    rounds = []
    for axis in axes:
        count = lax.axis_size(axis)
        step = 1
        while step < count:
            rounds.append((axis, [(i, i ^ step) for i in range(count)]))
            step *= 2
    return rounds


def per_device(inputs, lengths, params, first_moment, second_moment, cotangent):
    rows_here, length_here, _ = inputs.shape
    base = (lax.axis_index("group") * length_here).astype(jnp.int32).reshape(1)
    near, far = packed(base, inputs, cotangent)
    far = lax.ppermute(far, "group", pairs_of("group", 1))
    near = lax.ppermute(near, "group", pairs_of("group", 0))
    high, low = convolved(base, lengths, inputs, params)
    outputs, matrices, padded, grad_params = forward(
        base, lengths, inputs, cotangent, high, low, near, far, params
    )

    def backward_row(row, matrices, grown):
        return backward(row, base, lengths, inputs.shape, matrices, padded, outputs, params, grown)

    grown = None
    row = 0
    received = None
    for axis, exchange in rounds_of(("group", "rows")):
        if received is not None:
            grad_params = grad_params + received
            if row < rows_here:
                matrices, grad_params = lax.optimization_barrier((matrices, grad_params))
                grown = backward_row(row, matrices, grown)
                received = lax.ppermute(grad_params, axis, exchange)
                received, grown = lax.optimization_barrier((received, grown))
                row += 1
                continue
        received = lax.ppermute(grad_params, axis, exchange)
    while row < rows_here:
        grown = backward_row(row, matrices, grown)
        row += 1
    output, grad_inputs = grown
    grad_norm, new_params, new_first, new_second = update(
        grad_params, received, params, first_moment, second_moment
    )
    grad_norm = grad_norm.reshape(())
    return (output, grad_inputs, grad_norm, new_params, new_first, new_second)


def solution(mesh):
    in_specs = (P("rows", "group", None), P("rows", None), P(), P(), P(), P("rows", "group", None))
    out_specs = (P("rows", "group", None), P("rows", "group", None), P(), P(), P(), P())
    return jax.shard_map(
        per_device, mesh=mesh, in_specs=in_specs, out_specs=out_specs, check_vma=False
    )
```
